128 devices in a mesh: blk: 8 (over x_lo, y), grid: 16 (over x_hi, z, core).
Axes of the slice: x: 4 (x_hi: 2, x_lo: 2; x = x_hi * 2 + x_lo), y: 4, z: 4, core: 2. Of those that a mesh axis runs over, the one named last changes fastest.
Arguments:
- conn: int32 [2048, 9], P(('blk', 'grid')), may hold values from 0 to 2047, as said below
- extract: float32 [9, 9, 2048], P(None, None, ('blk', 'grid')), may hold values from 0.1 to 1
- points: float32 [3, 9, 2048], P(None, None, ('blk', 'grid')), as said below
Outputs:
- factor: float32 [1, 2048, 2, 1024], P(None, 'grid', None, 'blk')
The draws below stay inside these ranges and needn't reach their ends.
Inputs may be any that keep to these rules, and one draw needn't show every extreme that they name: `conn`: element e = ix 32 + iy of the periodic 64 x 32 grid of elements names the functions ((ix + s) mod 64) * 32 + (iy + t) mod 32 for s, t in 0, 1, 2, each once, in an order that differs from element to element. The 9 points of element e = ix 32 + iy are the 3 x 3 Gauss points of the cell [ix / 64, (ix + 1) / 64] x [iy / 64, (iy + 1) / 64], each coordinate then moved by at most 3.5 / 64; points[2] is positive.
All inputs are finite; a program needn't handle non-finite values.
Results may differ from the reference program's by a relative error of at most 0.0003.
Values sent between devices are 32-bit elements; how exact they have to be, the bound alone decides.
A program may use at most 128 MiB of HBM per device.

```python
import math
import jax
import jax.numpy as jnp
from jax import lax

M = 2048
EX = 64
EY = 32
E = 2048
QP = 9
TB = 128
RCY = 1
CCY = 2
N_BLK = 8
N_GRID = 16


def draw_points(key, part):
    phase_key, amp_key, weight_key, jitter_key = jax.random.split(key, 4)
    phases = jax.random.uniform(phase_key, (3,), jnp.float32, 0.0, 2.0 * math.pi)
    amplitude = jax.random.uniform(amp_key, (2,), jnp.float32, 0.25, 1.0) / EX
    jitter = jax.random.uniform(jitter_key, (2, QP, E), jnp.float32, -2.5, 2.5) / EX
    height = EY / EX
    spread_root = 0.5 * math.sqrt(0.6)
    gauss_nodes = jnp.array([0.5 - spread_root, 0.5, 0.5 + spread_root], jnp.float32)
    element = jnp.arange(E, dtype=jnp.int32)
    cell_x = (element // EY).astype(jnp.float32)
    cell_y = (element % EY).astype(jnp.float32)
    local_x = jnp.repeat(gauss_nodes, 3)
    local_y = jnp.tile(gauss_nodes, 3)
    base_x = (cell_x[None, :] + local_x[:, None]) / EX
    base_y = (cell_y[None, :] + local_y[:, None]) / EX
    place_x = base_x + amplitude[0] * jnp.sin(2.0 * math.pi * base_y / height + phases[0]) + jitter[0]
    place_y = base_y + amplitude[1] * jnp.sin(2.0 * math.pi * base_x + phases[1]) + jitter[1]
    weight = jnp.exp(jax.random.uniform(weight_key, (QP, E), jnp.float32, math.log(0.05), math.log(0.5)))
    return jnp.stack([place_x, place_y, weight], axis=0)


def draw_conn(key, part):
    turn = jax.random.randint(key, (E,), 0, 8)
    element = jnp.arange(E, dtype=jnp.int32)
    cell_x = element // EY
    cell_y = element % EY
    local = jnp.arange(QP, dtype=jnp.int32)
    first_step = local // 3
    second_step = local % 3
    swapped = (turn // 4)[:, None] == 1
    step_x = jnp.where(swapped, second_step[None, :], first_step[None, :])
    step_y = jnp.where(swapped, first_step[None, :], second_step[None, :])
    step_x = jnp.where((turn % 2)[:, None] == 1, 2 - step_x, step_x)
    step_y = jnp.where((turn // 2 % 2)[:, None] == 1, 2 - step_y, step_y)
    return (cell_x[:, None] + step_x) % EX * EY + (cell_y[:, None] + step_y) % EY


def block_levels(own_key, dims, pieces, smallest, high):
    loudness, own = 1.0, jax.random.fold_in(own_key, 6)
    for axis_at, blocks in pieces:
        draws = jnp.exp(jax.random.uniform(jax.random.fold_in(own, axis_at), (blocks,), jnp.float32, smallest / len(pieces), high / len(pieces)))
        loudness = loudness * jnp.repeat(draws, dims[axis_at] // blocks).reshape([-1 if axis == axis_at else 1 for axis in range(len(dims))])
    return loudness


def setup_inputs(seed: int = 0) -> dict:
    key_of = jax.random.split(jax.random.key(seed), 4)
    return {
        "conn": draw_conn(jax.random.fold_in(key_of[3], 71), 0),
        "extract": jnp.clip(0.1 + 0.9 * jax.random.uniform(key_of[1], (QP, QP, E), jnp.float32) ** block_levels(key_of[1], (QP, QP, E), ((2, 128),), -0.2, 0.2), 0.1, 1.0),
        "points": draw_points(jax.random.fold_in(key_of[3], 71), 0),
    }


kernel_gain = 0.02
mass_shift = 0.05

def bernstein_table():
    spread_root = 0.5 * math.sqrt(0.6)
    gauss_nodes = [0.5 - spread_root, 0.5, 0.5 + spread_root]

    def bern_poly(which, where):
        return [(1.0 - where) ** 2, 2.0 * where * (1.0 - where), where * where][which]
    table_rows = []
    for i in range(3):
        for j in range(3):
            table_row = []
            for a in range(3):
                for b in range(3):
                    table_row.append(bern_poly(a, gauss_nodes[i]) * bern_poly(b, gauss_nodes[j]))
            table_rows.append(table_row)
    return jnp.asarray(table_rows, jnp.float32)

def torus_square(first_x, first_y, second_x, second_y):
    height = EY / EX
    gap_x = jnp.abs(first_x - second_x)
    gap_x = jnp.minimum(gap_x, jnp.abs(1.0 - gap_x))
    gap_y = jnp.abs(first_y - second_y)
    gap_y = jnp.minimum(gap_y, jnp.abs(height - gap_y))
    return gap_x * gap_x + gap_y * gap_y

def kernel_rows(test_x, test_y, trial_x, trial_y, trial_w):
    distance = torus_square(test_x[:, None], test_y[:, None], trial_x[None, :], trial_y[None, :])
    return kernel_gain * trial_w[None, :] * (1.0 + distance * (EX * EX / 4.0)) ** (-1.75)

def reference(conn, extract, points):
    values = jnp.einsum('kb,abe->eka', bernstein_table(), extract, precision=lax.Precision.HIGHEST)
    place_x = points[0].T.reshape(-1)
    place_y = points[1].T.reshape(-1)
    weight = points[2].T.reshape(-1)
    flat_conn = conn.reshape(-1)
    span = math.gcd(E, 128)
    rows = span * QP
    slot = jnp.arange(rows, dtype=jnp.int32).reshape(span, QP)
    row_index = jnp.broadcast_to(slot[:, :, None], (span, QP, QP))

    def one_block(stiff, index):
        start = (index * span).astype(jnp.int32)
        block_x = lax.dynamic_slice_in_dim(place_x, start * QP, rows)
        block_y = lax.dynamic_slice_in_dim(place_y, start * QP, rows)
        block_w = lax.dynamic_slice_in_dim(weight, start * QP, rows)
        block_vals = lax.dynamic_slice_in_dim(values, start, span, 0)
        block_conn = lax.dynamic_slice_in_dim(conn, start, span, 0)
        kernel_block = kernel_rows(block_x, block_y, place_x, place_y, weight)
        total = lax.optimization_barrier(jnp.sum(kernel_block, axis=1))
        summed = jnp.einsum('pek,eka->pea', kernel_block.reshape(rows, E, QP), values, precision=lax.Precision.HIGHEST)
        potential = jnp.zeros((rows, M), jnp.float32).at[:, flat_conn].add(summed.reshape(rows, E * QP))
        col_index = jnp.broadcast_to(block_conn[:, None, :], (span, QP, QP))
        phi_rows = jnp.zeros((rows, M), jnp.float32).at[row_index, col_index].add(block_vals)
        share = block_w[:, None] * ((mass_shift + total)[:, None] * phi_rows - potential)
        contrib = jnp.einsum('eka,ekm->eam', block_vals, share.reshape(span, QP, M), precision=lax.Precision.HIGHEST)
        stiff = stiff.at[block_conn.reshape(-1)].add(contrib.reshape(span * QP, M))
        return (stiff, None)
    stiff, unused = lax.scan(one_block, jnp.zeros((M, M), jnp.float32), jnp.arange(E // span, dtype=jnp.int32))
    head = stiff[:TB, :TB]
    lower = jnp.linalg.cholesky(0.5 * (head + head.T))
    rest = lax.linalg.triangular_solve(lower, stiff[TB:, :TB], left_side=False, lower=True, transpose_a=True)
    trail = stiff[TB:, TB:] - jnp.dot(rest.astype(jnp.float32), rest.T.astype(jnp.float32), precision=lax.Precision.HIGHEST, preferred_element_type=jnp.float32)
    top_rows = jnp.concatenate([lower, jnp.zeros((TB, M - TB), jnp.float32)], axis=1)
    bottom_rows = jnp.concatenate([rest, trail], axis=1)
    whole = jnp.tril(jnp.concatenate([top_rows, bottom_rows], axis=0))
    return whole.reshape(RCY, N_GRID * TB, CCY, N_BLK * TB)
```

```python
import functools
import math

import jax
import jax.numpy as jnp
import numpy as np
from jax import lax
from jax.experimental import pallas as pl
from jax.experimental.pallas import tpu as pltpu
from jax.sharding import PartitionSpec as P

M = 2048
EX = 64
EY = 32
QP = 9
TB = 128
BLK = 8
GRID = 16
PTS = QP * TB
WIN = 256
AUG = 192

KERNEL_GAIN = 0.02
MASS_SHIFT = 0.05

FX, FY, FW, FV, FC = 0, 9, 18, 27, 108

MESH = pl.DeviceIdType.MESH
VMEM_LIMIT = 48 * 1024 * 1024
EXACT = lax.Precision.HIGHEST


def bernstein_table():
    spread_root = 0.5 * math.sqrt(0.6)
    nodes = [0.5 - spread_root, 0.5, 0.5 + spread_root]
    poly = [[(1.0 - t) ** 2, 2.0 * t * (1.0 - t), t * t] for t in nodes]
    return np.array(
        [
            [poly[i][a] * poly[j][b] for a in range(3) for b in range(3)]
            for i in range(3)
            for j in range(3)
        ],
        np.float32,
    )


def field_map():
    table = np.zeros((TB, TB), np.float32)
    bern = bernstein_table()
    for i in range(FV):
        table[i, i] = 1.0
    for i in range(FC, FC + QP):
        table[i, i] = 1.0
    for k in range(QP):
        for a in range(QP):
            for b in range(QP):
                table[FV + k * QP + a, FV + a * QP + b] = bern[k, b]
    return table


def pair_device(first, second):
    hi, lo = jnp.maximum(first, second), jnp.minimum(first, second)
    same = hi == lo
    low = lo < BLK
    b = jnp.where(same, hi % BLK, jnp.where(low, lo, hi - BLK))
    g = jnp.where(same, hi % BLK, jnp.where(low, hi, lo - BLK))
    return b, g


def here():
    return lax.axis_index("blk"), lax.axis_index("grid")


def own_pair(b, g):
    diag = b == g
    hi = jnp.where(g >= b, g, b + BLK)
    lo = jnp.where(g > b, b, g + BLK)
    return hi, lo, diag


def greet(barrier, b, g):
    pl.semaphore_signal(barrier, inc=1, device_id=(b, g), device_id_type=MESH)


def gather_greetings(barrier, number):
    @pl.when(number > 0)
    def _():
        pl.semaphore_wait(barrier, number)


def differs(b, g, mb, mg):
    return jnp.logical_or(b != mb, g != mg)


def gather_kernel(map_ref, conn_ref, extract_ref, points_ref, out_ref, raw, record, send_sem, recv_sem):
    mb, mg = here()
    hi, lo, diag = own_pair(mb, mg)
    block = 2 * mb + mg // 8
    place = mg % 8
    barrier = pltpu.get_barrier_semaphore()

    def source(n):
        wanted = jnp.where(n // 8 == 0, hi, lo)
        return wanted // 2, (wanted % 2) * 8 + n % 8

    def say(n, carry):
        b, g = source(n)

        @pl.when(differs(b, g, mb, mg))
        def _():
            greet(barrier, b, g)

        return carry

    lax.fori_loop(0, 16, say, 0)

    raw[...] = jnp.zeros_like(raw)
    for c in range(3):
        raw[9 * c : 9 * c + 9, 0:16] = points_ref[c]
    for a in range(QP):
        raw[FV + 9 * a : FV + 9 * a + 9, 0:16] = extract_ref[a]
    raw[FC : FC + 9, 0:16] = conn_ref[...].astype(jnp.float32).T
    made = jnp.dot(map_ref[...], raw[...], precision=EXACT, preferred_element_type=jnp.float32)
    record[...] = made.T[0:16, :]

    own_dest = lambda j: pair_device(block, j)

    def count(j, total):
        b, g = own_dest(j)
        return total + jnp.where(differs(b, g, mb, mg), 1, 0)

    gather_greetings(barrier, lax.fori_loop(0, 16, count, 0))

    def slot_of(j):
        diag_pair = j == block
        return jnp.where(diag_pair, block // BLK, jnp.where(block > j, 0, 1))

    def copy(j):
        b, g = own_dest(j)
        slot = slot_of(j)
        return pltpu.make_async_remote_copy(
            src_ref=record,
            dst_ref=out_ref.at[slot, pl.ds(16 * place, 16), :],
            send_sem=send_sem.at[j],
            recv_sem=recv_sem.at[slot * 8 + place],
            device_id=(b, g),
            device_id_type=MESH,
        )

    def send(j, carry):
        b, g = own_dest(j)
        away = differs(b, g, mb, mg)

        @pl.when(away)
        def _():
            copy(j).start()

        @pl.when(jnp.logical_not(away))
        def _():
            out_ref[slot_of(j), pl.ds(pl.multiple_of(16 * place, 16), 16), :] = record[...]

        return carry

    lax.fori_loop(0, 16, send, 0)

    def finish(n, carry):
        b, g = source(n)

        @pl.when(differs(b, g, mb, mg))
        def _():
            pltpu.make_async_remote_copy(
                src_ref=record,
                dst_ref=out_ref.at[n // 8, pl.ds(16 * (n % 8), 16), :],
                send_sem=send_sem.at[n],
                recv_sem=recv_sem.at[n],
                device_id=(b, g),
                device_id_type=MESH,
            ).wait_recv()

        db, dg = own_dest(n)

        @pl.when(differs(db, dg, mb, mg))
        def _():
            copy(n).wait_send()

        return carry

    lax.fori_loop(0, 16, finish, 0)


def gather(conn, extract, points):
    vmem = pl.BlockSpec(memory_space=pltpu.VMEM)
    return pl.pallas_call(
        gather_kernel,
        out_shape=jax.ShapeDtypeStruct((2, TB, TB), jnp.float32),
        in_specs=[vmem] * 4,
        out_specs=vmem,
        scratch_shapes=[
            pltpu.VMEM((TB, TB), jnp.float32),
            pltpu.VMEM((16, TB), jnp.float32),
            pltpu.SemaphoreType.DMA((16,)),
            pltpu.SemaphoreType.DMA((16,)),
        ],
        compiler_params=pltpu.CompilerParams(
            collective_id=0, has_side_effects=True, vmem_limit_bytes=VMEM_LIMIT
        ),
        name="gather_elements",
    )(jnp.asarray(field_map()), conn, extract, points)


def split(value):
    high = value.astype(jnp.bfloat16)
    return high, (value - high.astype(jnp.float32)).astype(jnp.bfloat16)


def build_phi(fields, start, weigh, high_ref, low_ref):
    rows = 32
    for jx in range(6):
        iota = lax.broadcasted_iota(jnp.int32, (rows, TB), 0).astype(jnp.float32) + float(rows * jx)
        sums = [jnp.zeros((rows, TB), jnp.float32) for _ in range(QP)]
        for a in range(QP):
            target = fields[FC + a : FC + a + 1, :] - start
            target = jnp.where(target < 0.0, target + float(M), target)
            hit = jnp.broadcast_to(target, (rows, TB)) == iota
            for k in range(QP):
                value = fields[FV + k * QP + a : FV + k * QP + a + 1, :]
                sums[k] = jnp.where(hit, jnp.broadcast_to(value, (rows, TB)), sums[k])
        for k in range(QP):
            value = weigh(sums[k], k)
            high, low = split(value)
            high_ref[rows * jx : rows * (jx + 1), TB * k : TB * (k + 1)] = high
            low_ref[rows * jx : rows * (jx + 1), TB * k : TB * (k + 1)] = low


def nt(a, b):
    return lax.dot_general(a, b, (((1,), (1,)), ((), ())), preferred_element_type=jnp.float32)


def nn(a, b):
    return lax.dot_general(a, b, (((1,), (0,)), ((), ())), preferred_element_type=jnp.float32)


def pair_kernel(
    rec_ref, x_ref, total_ref, fields, phi_hi, phi_lo, splat, kern, pot_hi, pot_lo, col_sum, row_sum
):
    mb, mg = here()
    hi, lo, diag = own_pair(mb, mg)
    for slot in range(2):
        fields[slot] = rec_ref[slot].T
    for slot, block in ((0, hi), (1, lo)):
        start = (block * TB).astype(jnp.float32)
        view = fields.at[slot]
        build_phi(
            view,
            start,
            lambda v, k: v * jnp.broadcast_to(view[FW + k : FW + k + 1, :], v.shape),
            phi_hi.at[slot],
            phi_lo.at[slot],
        )
        phi_hi[slot, AUG:WIN, :] = jnp.zeros((WIN - AUG, PTS), jnp.bfloat16)
        phi_lo[slot, AUG:WIN, :] = jnp.zeros((WIN - AUG, PTS), jnp.bfloat16)
        for k in range(QP):
            first = lax.broadcasted_iota(jnp.int32, (16, TB), 0) == 0
            weight = jnp.broadcast_to(view[FW + k : FW + k + 1, :], (16, TB))
            high, low = split(jnp.where(first, weight, 0.0))
            phi_hi[slot, AUG : AUG + 16, TB * k : TB * (k + 1)] = high
            phi_lo[slot, AUG : AUG + 16, TB * k : TB * (k + 1)] = low
    total_ref[...] = jnp.zeros_like(total_ref)
    x_ref[1] = jnp.zeros((WIN, WIN), jnp.float32)

    def run(r, carry):
        p_slot = jnp.where(diag, r, 0)
        q_slot = jnp.where(diag, r, 1)
        col_sum[...] = jnp.zeros_like(col_sum)

        def row_chunk(i, carry):
            record = rec_ref[p_slot]

            lane = lax.broadcasted_iota(jnp.int32, (TB, TB), 1)
            for n, base in ((0, FX), (1, FY), (2, FW)):
                picked = jnp.sum(jnp.where(lane == base + i, record, 0.0), axis=1, keepdims=True)
                scaled = picked * (float(EX) / 2.0) if n < 2 else picked * KERNEL_GAIN
                splat[n] = jnp.broadcast_to(scaled, (TB, TB))

            def col_chunk(j, carry):
                wanted = jnp.logical_or(jnp.logical_not(diag), j >= i)

                @pl.when(jnp.logical_not(wanted))
                def _():
                    kern[:, pl.ds(pl.multiple_of(j * TB, TB), TB)] = jnp.zeros((TB, TB), jnp.bfloat16)

                @pl.when(wanted)
                def _():
                    factor = jnp.where(jnp.logical_and(diag, j == i), 0.5, 1.0)
                    qx = fields[q_slot, pl.ds(FX + j, 1), :] * (float(EX) / 2.0)
                    qy = fields[q_slot, pl.ds(FY + j, 1), :] * (float(EX) / 2.0)
                    gap_x = jnp.abs(splat[0] - qx)
                    gap_x = jnp.minimum(gap_x, jnp.abs(float(EX) / 2.0 - gap_x))
                    gap_y = jnp.abs(splat[1] - qy)
                    gap_y = jnp.minimum(gap_y, jnp.abs(float(EY) / 2.0 - gap_y))
                    base = 1.0 + (gap_x * gap_x + gap_y * gap_y)
                    root = lax.rsqrt(base)
                    square = root * root
                    value = factor * (square * square * lax.rsqrt(root))
                    kern[:, pl.ds(pl.multiple_of(j * TB, TB), TB)] = value.astype(jnp.bfloat16)
                    weighed = jnp.sum(value * splat[2], axis=0, keepdims=True)
                    col_sum[pl.ds(j, 1), :] += weighed

                return carry

            lax.fori_loop(0, QP, col_chunk, 0)
            block = kern[...]
            pot = nt(block, phi_hi[q_slot]) + nt(block, phi_lo[q_slot])
            row_sum[pl.ds(i, 1), :] = pot[:, TB:WIN].T[AUG - TB : AUG - TB + 1, :] * KERNEL_GAIN
            high, low = split(pot)
            pot_hi[pl.ds(pl.multiple_of(i * TB, TB), TB), :] = high
            pot_lo[pl.ds(pl.multiple_of(i * TB, TB), TB), :] = low
            return carry

        lax.fori_loop(0, QP, row_chunk, 0)
        inside = jnp.logical_and(
            lax.broadcasted_iota(jnp.int32, (WIN, WIN), 0) < AUG,
            lax.broadcasted_iota(jnp.int32, (WIN, WIN), 1) < AUG,
        )
        x_ref[r] = jnp.where(
            inside,
            KERNEL_GAIN
            * (
                nn(phi_hi[p_slot], pot_hi[...])
                + nn(phi_lo[p_slot], pot_hi[...])
                + nn(phi_hi[p_slot], pot_lo[...])
            ),
            0.0,
        )
        total_ref[p_slot, 0:QP, :] += row_sum[0:QP, :]
        total_ref[q_slot, 0:QP, :] += col_sum[0:QP, :]
        return carry

    lax.fori_loop(0, jnp.where(diag, 2, 1), run, 0)


def pair_work(records):
    vmem = pl.BlockSpec(memory_space=pltpu.VMEM)
    return pl.pallas_call(
        pair_kernel,
        out_shape=(
            jax.ShapeDtypeStruct((2, WIN, WIN), jnp.float32),
            jax.ShapeDtypeStruct((2, 16, TB), jnp.float32),
        ),
        in_specs=[vmem],
        out_specs=(vmem, vmem),
        scratch_shapes=[
            pltpu.VMEM((2, TB, TB), jnp.float32),
            pltpu.VMEM((2, WIN, PTS), jnp.bfloat16),
            pltpu.VMEM((2, WIN, PTS), jnp.bfloat16),
            pltpu.VMEM((3, TB, TB), jnp.float32),
            pltpu.VMEM((TB, PTS), jnp.bfloat16),
            pltpu.VMEM((PTS, WIN), jnp.bfloat16),
            pltpu.VMEM((PTS, WIN), jnp.bfloat16),
            pltpu.VMEM((16, TB), jnp.float32),
            pltpu.VMEM((16, TB), jnp.float32),
        ],
        compiler_params=pltpu.CompilerParams(vmem_limit_bytes=VMEM_LIMIT),
        name="pair_blocks",
    )(records)


def totals_kernel(total_ref, out_ref, send_sem, recv_sem):
    mb, mg = here()
    hi, lo, diag = own_pair(mb, mg)
    barrier = pltpu.get_barrier_semaphore()

    def copy(slot):
        mine, other = (hi, lo) if slot == 0 else (lo, hi)
        return pltpu.make_async_remote_copy(
            src_ref=total_ref.at[slot],
            dst_ref=out_ref.at[mine // BLK, other],
            send_sem=send_sem.at[slot],
            recv_sem=recv_sem.at[mine // BLK, other],
            device_id=(mine % BLK, mine % BLK),
            device_id_type=MESH,
        )

    @pl.when(diag)
    def _():
        def say(n, carry):
            block, other = mg + (n // 16) * BLK, n % 16

            @pl.when(block != other)
            def _():
                b, g = pair_device(block, other)
                greet(barrier, b, g)

            return carry

        lax.fori_loop(0, 32, say, 0)
        for slot in range(2):
            out_ref[slot, mg + slot * BLK] = total_ref[slot]

        def take(n, carry):
            half, other = n // 16, n % 16

            @pl.when(mg + half * BLK != other)
            def _():
                pltpu.make_async_remote_copy(
                    src_ref=total_ref.at[0],
                    dst_ref=out_ref.at[half, other],
                    send_sem=send_sem.at[0],
                    recv_sem=recv_sem.at[half, other],
                    device_id=(mb, mg),
                    device_id_type=MESH,
                ).wait_recv()

            return carry

        lax.fori_loop(0, 32, take, 0)

    @pl.when(jnp.logical_not(diag))
    def _():
        pl.semaphore_wait(barrier, 2)
        for slot in range(2):
            copy(slot).start()
        for slot in range(2):
            copy(slot).wait_send()


def totals_exchange(total):
    vmem = pl.BlockSpec(memory_space=pltpu.VMEM)
    return pl.pallas_call(
        totals_kernel,
        out_shape=jax.ShapeDtypeStruct((2, 16, 16, TB), jnp.float32),
        in_specs=[vmem],
        out_specs=vmem,
        scratch_shapes=[pltpu.SemaphoreType.DMA((2,)), pltpu.SemaphoreType.DMA((2, 16))],
        compiler_params=pltpu.CompilerParams(
            collective_id=1, has_side_effects=True, vmem_limit_bytes=VMEM_LIMIT
        ),
        name="send_totals",
    )(total)


def pieces_kernel(rec_ref, x_ref, parts_ref, out_ref, fields, phi_hi, phi_lo):
    mb, mg = here()
    hi, lo, diag = own_pair(mb, mg)

    @pl.when(jnp.logical_not(diag))
    def _():
        for n in range(4):
            u, v = n // 2, n % 2
            piece = -x_ref[0, TB * u : TB * (u + 1), TB * v : TB * (v + 1)]
            row, col = (hi + u) % 16, (lo + v) % 16
            if u == 0 and v == 0:
                out_ref[n] = piece
            else:
                other = piece.T
                out_ref[n] = jnp.where(row < col, 0.0, piece) + jnp.where(row > col, 0.0, other)

    @pl.when(diag)
    def _():
        for r in range(2):
            block = mg + BLK * r
            fields[...] = rec_ref[r].T
            build_phi(fields, (block * TB).astype(jnp.float32), lambda v, k: v, phi_hi, phi_lo)
            for ref in (phi_hi, phi_lo):
                ref[AUG:WIN, :] = jnp.zeros((WIN - AUG, PTS), jnp.bfloat16)
            gain = jnp.sum(parts_ref[r], axis=0)
            mass = jnp.zeros((WIN, WIN), jnp.float32)
            for k in range(QP):
                lanes = slice(TB * k, TB * (k + 1))
                left = phi_hi[:, lanes].astype(jnp.float32) + phi_lo[:, lanes].astype(jnp.float32)
                factor = fields[FW + k : FW + k + 1, :] * (MASS_SHIFT + gain[k : k + 1, :])
                high, low = split(left * factor)
                mass += (
                    nt(high, phi_hi[:, lanes]) + nt(low, phi_hi[:, lanes]) + nt(high, phi_lo[:, lanes])
                )
            x = x_ref[r]
            for n, (u, v) in enumerate(((0, 0), (1, 0), (1, 1))):
                one = x[TB * u : TB * (u + 1), TB * v : TB * (v + 1)]
                two = x[TB * v : TB * (v + 1), TB * u : TB * (u + 1)]
                whole = mass[TB * u : TB * (u + 1), TB * v : TB * (v + 1)] - one - two.T
                if u != v and r == 1:
                    flip = block == 15
                    whole = jnp.where(flip, 0.0, whole) + jnp.where(flip, whole.T, 0.0)
                out_ref[3 * r + n] = whole


def make_pieces(records, x, parts):
    vmem = pl.BlockSpec(memory_space=pltpu.VMEM)
    return pl.pallas_call(
        pieces_kernel,
        out_shape=jax.ShapeDtypeStruct((6, TB, TB), jnp.float32),
        in_specs=[vmem] * 3,
        out_specs=vmem,
        scratch_shapes=[
            pltpu.VMEM((TB, TB), jnp.float32),
            pltpu.VMEM((WIN, PTS), jnp.bfloat16),
            pltpu.VMEM((WIN, PTS), jnp.bfloat16),
        ],
        compiler_params=pltpu.CompilerParams(vmem_limit_bytes=VMEM_LIMIT),
        name="make_pieces",
    )(records, x, parts)


def piece_target(n, hi, lo, diag, g):
    u, v = n // 2, n % 2
    row, col = (hi + u) % 16, (lo + v) % 16
    slot = jnp.where(row == col, 1, jnp.where(row > col, 2 * u + v, 2 * v + u))
    r, m = n // 3, n % 3
    block = g + BLK * r
    after = (block + 1) % 16
    drow = jnp.where(m == 0, block, jnp.where(m == 1, jnp.maximum(block, after), after))
    dcol = jnp.where(m == 0, block, jnp.where(m == 1, jnp.minimum(block, after), after))
    dslot = jnp.where(m == 0, 0, jnp.where(m == 1, jnp.where(block == 15, 1, 2), 3))
    big = jnp.where(diag, drow, jnp.maximum(row, col))
    small = jnp.where(diag, dcol, jnp.minimum(row, col))
    there = jnp.where(diag, 6, 4) > n
    return small % BLK, big, small // BLK, jnp.where(diag, dslot, slot), there


def piece_source(t, s, b, g):
    row, col = g, b + BLK * t
    there = jnp.logical_and(row >= col, jnp.logical_not(jnp.logical_and(row == col, s == 2)))
    sb, sg = pair_device((row - s // 2 + 16) % 16, (col - s % 2 + 16) % 16)
    return sb, sg, there


def reduce_kernel(piece_ref, out_ref, landed, send_sem, recv_sem):
    mb, mg = here()
    hi, lo, diag = own_pair(mb, mg)
    barrier = pltpu.get_barrier_semaphore()

    def say(n, carry):
        sb, sg, there = piece_source(n // 4, n % 4, mb, mg)

        @pl.when(jnp.logical_and(there, differs(sb, sg, mb, mg)))
        def _():
            greet(barrier, sb, sg)

        return carry

    lax.fori_loop(0, 8, say, 0)

    def count(n, total):
        b, g, t, s, there = piece_target(n, hi, lo, diag, mg)
        return total + jnp.where(jnp.logical_and(there, differs(b, g, mb, mg)), 1, 0)

    gather_greetings(barrier, lax.fori_loop(0, 6, count, 0))

    def copy(n):
        b, g, t, s, there = piece_target(n, hi, lo, diag, mg)
        return pltpu.make_async_remote_copy(
            src_ref=piece_ref.at[n],
            dst_ref=landed.at[t, s],
            send_sem=send_sem.at[n],
            recv_sem=recv_sem.at[t, s],
            device_id=(b, g),
            device_id_type=MESH,
        )

    def send(n, carry):
        b, g, t, s, there = piece_target(n, hi, lo, diag, mg)
        away = differs(b, g, mb, mg)

        @pl.when(jnp.logical_and(there, away))
        def _():
            copy(n).start()

        @pl.when(jnp.logical_and(there, jnp.logical_not(away)))
        def _():
            landed[t, s] = piece_ref[n]

        return carry

    lax.fori_loop(0, 6, send, 0)
    out_ref[...] = jnp.zeros_like(out_ref)

    def take(n, carry):
        t, s = n // 4, n % 4
        sb, sg, there = piece_source(t, s, mb, mg)

        @pl.when(there)
        def _():
            @pl.when(differs(sb, sg, mb, mg))
            def _():
                pltpu.make_async_remote_copy(
                    src_ref=piece_ref.at[0],
                    dst_ref=landed.at[t, s],
                    send_sem=send_sem.at[0],
                    recv_sem=recv_sem.at[t, s],
                    device_id=(sb, sg),
                    device_id_type=MESH,
                ).wait_recv()

            out_ref[t] += landed[t, s]

        return carry

    lax.fori_loop(0, 8, take, 0)

    def drain(n, carry):
        b, g, t, s, there = piece_target(n, hi, lo, diag, mg)

        @pl.when(jnp.logical_and(there, differs(b, g, mb, mg)))
        def _():
            copy(n).wait_send()

        return carry

    lax.fori_loop(0, 6, drain, 0)


def reduce_pieces(pieces):
    vmem = pl.BlockSpec(memory_space=pltpu.VMEM)
    return pl.pallas_call(
        reduce_kernel,
        out_shape=jax.ShapeDtypeStruct((2, TB, TB), jnp.float32),
        in_specs=[vmem],
        out_specs=vmem,
        scratch_shapes=[
            pltpu.VMEM((2, 4, TB, TB), jnp.float32),
            pltpu.SemaphoreType.DMA((6,)),
            pltpu.SemaphoreType.DMA((2, 4)),
        ],
        compiler_params=pltpu.CompilerParams(
            collective_id=2, has_side_effects=True, vmem_limit_bytes=VMEM_LIMIT
        ),
        name="sum_pieces",
    )(pieces)


def panel_kernel(tile_ref, out_ref, send_sem, recv_sem):
    mb, mg = here()
    barrier = pltpu.get_barrier_semaphore()
    first = mb == 0
    root = jnp.logical_and(first, mg == 0)
    relay = jnp.logical_and(mg >= 1, mb == mg % BLK)

    def wants(t):
        col = mb + BLK * t
        return jnp.logical_and(col >= 1, mg > col)

    @pl.when(jnp.logical_not(first))
    def _():
        greet(barrier, 0, mg)

    @pl.when(jnp.logical_and(first, mg > 0))
    def _():
        greet(barrier, 0, 0)

    for t in range(2):
        @pl.when(wants(t))
        def _(t=t):
            greet(barrier, mb, mb + BLK * t)

    expected = (
        jnp.where(first, BLK - 1, 0)
        + jnp.where(root, GRID - 1, 0)
        + jnp.where(relay, GRID - 1 - mg, 0)
    )
    gather_greetings(barrier, expected)

    def copy(source, n, sem, b, g):
        return pltpu.make_async_remote_copy(
            src_ref=source,
            dst_ref=out_ref.at[n],
            send_sem=send_sem.at[sem],
            recv_sem=recv_sem.at[n],
            device_id=(b, g),
            device_id_type=MESH,
        )

    @pl.when(root)
    def _():
        out_ref[0] = tile_ref[0]

    def root_send(g, carry):
        copy(tile_ref.at[0], 0, g, 0, g).start()
        return carry

    @pl.when(root)
    def _():
        lax.fori_loop(1, GRID, root_send, 0)

    @pl.when(first)
    def _():
        out_ref[1] = tile_ref[0]

        def row_send(b, carry):
            copy(tile_ref.at[0], 1, 16 + b, b, mg).start()
            return carry

        lax.fori_loop(1, BLK, row_send, 0)

    @pl.when(jnp.logical_not(first))
    def _():
        copy(tile_ref.at[0], 1, 0, mb, mg).wait_recv()

    def relay_copy(g):
        return copy(out_ref.at[1], 2 + mg // BLK, 40 + g, mb, g)

    @pl.when(relay)
    def _():
        def relay_send(g, carry):
            relay_copy(g).start()
            return carry

        lax.fori_loop(mg + 1, GRID, relay_send, 0)

    @pl.when(jnp.logical_not(root))
    def _():
        copy(tile_ref.at[0], 0, 0, mb, mg).wait_recv()

    @pl.when(first)
    def _():
        def head_send(b, carry):
            copy(out_ref.at[0], 0, 24 + b, b, mg).start()
            return carry

        lax.fori_loop(1, BLK, head_send, 0)

    for t in range(2):
        col = mb + BLK * t

        @pl.when(mg == col)
        def _(t=t):
            out_ref[2 + t] = out_ref[1]

        @pl.when(wants(t))
        def _(t=t):
            copy(tile_ref.at[0], 2 + t, 0, mb, mg).wait_recv()

        @pl.when(jnp.logical_not(jnp.logical_or(mg == col, wants(t))))
        def _(t=t):
            out_ref[2 + t] = jnp.zeros((TB, TB), jnp.float32)

    @pl.when(root)
    def _():
        def root_wait(g, carry):
            copy(tile_ref.at[0], 0, g, 0, g).wait_send()
            return carry

        lax.fori_loop(1, GRID, root_wait, 0)

    @pl.when(first)
    def _():
        def row_wait(b, carry):
            copy(tile_ref.at[0], 1, 16 + b, b, mg).wait_send()
            copy(out_ref.at[0], 0, 24 + b, b, mg).wait_send()
            return carry

        lax.fori_loop(1, BLK, row_wait, 0)

    @pl.when(relay)
    def _():
        def relay_wait(g, carry):
            relay_copy(g).wait_send()
            return carry

        lax.fori_loop(mg + 1, GRID, relay_wait, 0)


def share_panel(tiles):
    vmem = pl.BlockSpec(memory_space=pltpu.VMEM)
    return pl.pallas_call(
        panel_kernel,
        out_shape=jax.ShapeDtypeStruct((4, TB, TB), jnp.float32),
        in_specs=[vmem],
        out_specs=vmem,
        scratch_shapes=[pltpu.SemaphoreType.DMA((56,)), pltpu.SemaphoreType.DMA((4,))],
        compiler_params=pltpu.CompilerParams(
            collective_id=3, has_side_effects=True, vmem_limit_bytes=VMEM_LIMIT
        ),
        name="share_panel",
    )(tiles)


def eliminate(work):
    for kb in range(TB // 8):
        lo = 8 * kb
        panel = work[lo : lo + 8, :]
        row_at = lax.broadcasted_iota(jnp.int32, (8, 1), 0)
        for j in range(8):
            col = panel[:, lo + j : lo + j + 1]
            pivot = panel[j : j + 1, :]
            scale = lax.rsqrt(pivot[:, lo + j : lo + j + 1])
            done = pivot * scale
            panel = jnp.where(
                row_at == j, done, panel - jnp.where(row_at > j, col * scale, 0.0) * done
            )
        work[lo : lo + 8, :] = panel
        if lo + 8 < TB:
            work[lo + 8 : TB, :] -= lax.dot_general(
                panel[:, lo + 8 : TB],
                panel,
                (((0,), (0,)), ((), ())),
                precision=EXACT,
                preferred_element_type=jnp.float32,
            )


def factor_kernel(panel_ref, tile_ref, out_ref, work):
    mb, mg = here()
    head = panel_ref[0]
    row = lax.broadcasted_iota(jnp.int32, (TB, TB), 0)
    col = lax.broadcasted_iota(jnp.int32, (TB, TB), 1)
    work[:, 0:TB] = 0.5 * (head + head.T)
    work[:, TB:WIN] = jnp.where(row == col, 1.0, 0.0)
    eliminate(work)
    lower = jnp.where(row >= col, work[:, 0:TB].T, 0.0)
    inverse = jnp.where(row >= col, work[:, TB:WIN], 0.0)

    def solve(n):
        return lax.dot_general(
            panel_ref[n],
            inverse,
            (((1,), (1,)), ((), ())),
            precision=EXACT,
            preferred_element_type=jnp.float32,
        )

    left = jnp.where(mg == 0, lower, solve(1))
    for t in range(2):
        tile_col = mb + BLK * t
        update = lax.dot_general(
            left,
            solve(2 + t),
            (((1,), (1,)), ((), ())),
            precision=EXACT,
            preferred_element_type=jnp.float32,
        )
        value = jnp.where(tile_col == 0, left, tile_ref[t] - update)
        keep = mg * TB + row >= tile_col * TB + col
        out_ref[0, :, t, :] = jnp.where(keep, value, 0.0)


def factor(panel, tiles):
    vmem = pl.BlockSpec(memory_space=pltpu.VMEM)
    return pl.pallas_call(
        factor_kernel,
        out_shape=jax.ShapeDtypeStruct((1, TB, 2, TB), jnp.float32),
        in_specs=[vmem] * 2,
        out_specs=vmem,
        scratch_shapes=[pltpu.VMEM((TB, WIN), jnp.float32)],
        compiler_params=pltpu.CompilerParams(vmem_limit_bytes=VMEM_LIMIT),
        name="factor_tiles",
    )(panel, tiles)


def shards(conn, extract, points):
    records = gather(conn, extract, points)
    x, total = pair_work(records)
    parts = totals_exchange(total)
    pieces = make_pieces(records, x, parts)
    tiles = reduce_pieces(pieces)
    panel = share_panel(tiles)
    return factor(panel, tiles)


def solution(mesh):
    in_specs = (
        P(("blk", "grid"), None),
        P(None, None, ("blk", "grid")),
        P(None, None, ("blk", "grid")),
    )
    out_specs = P(None, "grid", None, "blk")
    return jax.shard_map(shards, mesh=mesh, in_specs=in_specs, out_specs=out_specs, check_vma=False)
```

```python
import functools
import math

import jax
import jax.numpy as jnp
import numpy as np
from jax import lax
from jax.experimental import pallas as pl
from jax.experimental.pallas import tpu as pltpu
from jax.sharding import PartitionSpec as P

M = 2048
EX = 64
EY = 32
QP = 9
TB = 128
BLK = 8
GRID = 16
PTS = QP * TB
WIN = 256
AUG = 192

KERNEL_GAIN = 0.02
MASS_SHIFT = 0.05

FX, FY, FW, FV, FC = 0, 9, 18, 27, 108

MESH = pl.DeviceIdType.MESH
VMEM_LIMIT = 48 * 1024 * 1024
EXACT = lax.Precision.HIGHEST


def bernstein_table():
    spread_root = 0.5 * math.sqrt(0.6)
    nodes = [0.5 - spread_root, 0.5, 0.5 + spread_root]
    poly = [[(1.0 - t) ** 2, 2.0 * t * (1.0 - t), t * t] for t in nodes]
    return np.array(
        [
            [poly[i][a] * poly[j][b] for a in range(3) for b in range(3)]
            for i in range(3)
            for j in range(3)
        ],
        np.float32,
    )


def field_map():
    table = np.zeros((TB, TB), np.float32)
    bern = bernstein_table()
    for i in range(FV):
        table[i, i] = 1.0
    for i in range(FC, FC + QP):
        table[i, i] = 1.0
    for k in range(QP):
        for a in range(QP):
            for b in range(QP):
                table[FV + a * QP + k, FV + a * QP + b] = bern[k, b]
    return table


def pair_device(first, second):
    hi, lo = jnp.maximum(first, second), jnp.minimum(first, second)
    same = hi == lo
    low = lo < BLK
    b = jnp.where(same, hi % BLK, jnp.where(low, lo, hi - BLK))
    g = jnp.where(same, hi % BLK, jnp.where(low, hi, lo - BLK))
    return b, g


def here():
    return lax.axis_index("blk"), lax.axis_index("grid")


def own_pair(b, g):
    diag = b == g
    hi = jnp.where(g >= b, g, b + BLK)
    lo = jnp.where(g > b, b, g + BLK)
    return hi, lo, diag


def greet(barrier, b, g):
    pl.semaphore_signal(barrier, inc=1, device_id=(b, g), device_id_type=MESH)


def gather_greetings(barrier, number):
    @pl.when(number > 0)
    def _():
        pl.semaphore_wait(barrier, number)


def differs(b, g, mb, mg):
    return jnp.logical_or(b != mb, g != mg)


def gather_kernel(map_ref, conn_ref, extract_ref, points_ref, out_ref, raw, record, send_sem, recv_sem):
    mb, mg = here()
    hi, lo, diag = own_pair(mb, mg)
    block = 2 * mb + mg // 8
    place = mg % 8
    barrier = pltpu.get_barrier_semaphore()

    def source(n):
        wanted = jnp.where(n // 8 == 0, hi, lo)
        return wanted // 2, (wanted % 2) * 8 + n % 8

    def say(n, carry):
        b, g = source(n)

        @pl.when(differs(b, g, mb, mg))
        def _():
            greet(barrier, b, g)

        return carry

    lax.fori_loop(0, 16, say, 0)

    raw[...] = jnp.zeros_like(raw)
    for c in range(3):
        raw[9 * c : 9 * c + 9, 0:16] = points_ref[c]
    for a in range(QP):
        raw[FV + 9 * a : FV + 9 * a + 9, 0:16] = extract_ref[a]
    raw[FC : FC + 9, 0:16] = conn_ref[...].astype(jnp.float32).T
    made = jnp.dot(map_ref[...], raw[...], precision=EXACT, preferred_element_type=jnp.float32)
    record[...] = made.T[0:16, :]

    own_dest = lambda j: pair_device(block, j)

    def count(j, total):
        b, g = own_dest(j)
        return total + jnp.where(differs(b, g, mb, mg), 1, 0)

    gather_greetings(barrier, lax.fori_loop(0, 16, count, 0))

    def slot_of(j):
        diag_pair = j == block
        return jnp.where(diag_pair, block // BLK, jnp.where(block > j, 0, 1))

    def copy(j):
        b, g = own_dest(j)
        slot = slot_of(j)
        return pltpu.make_async_remote_copy(
            src_ref=record,
            dst_ref=out_ref.at[slot, pl.ds(16 * place, 16), :],
            send_sem=send_sem.at[j],
            recv_sem=recv_sem.at[slot * 8 + place],
            device_id=(b, g),
            device_id_type=MESH,
        )

    def send(j, carry):
        b, g = own_dest(j)
        away = differs(b, g, mb, mg)

        @pl.when(away)
        def _():
            copy(j).start()

        @pl.when(jnp.logical_not(away))
        def _():
            out_ref[slot_of(j), pl.ds(pl.multiple_of(16 * place, 16), 16), :] = record[...]

        return carry

    lax.fori_loop(0, 16, send, 0)

    def finish(n, carry):
        b, g = source(n)

        @pl.when(differs(b, g, mb, mg))
        def _():
            pltpu.make_async_remote_copy(
                src_ref=record,
                dst_ref=out_ref.at[n // 8, pl.ds(16 * (n % 8), 16), :],
                send_sem=send_sem.at[n],
                recv_sem=recv_sem.at[n],
                device_id=(b, g),
                device_id_type=MESH,
            ).wait_recv()

        db, dg = own_dest(n)

        @pl.when(differs(db, dg, mb, mg))
        def _():
            copy(n).wait_send()

        return carry

    lax.fori_loop(0, 16, finish, 0)


def gather(conn, extract, points):
    vmem = pl.BlockSpec(memory_space=pltpu.VMEM)
    return pl.pallas_call(
        gather_kernel,
        out_shape=jax.ShapeDtypeStruct((2, TB, TB), jnp.float32),
        in_specs=[vmem] * 4,
        out_specs=vmem,
        scratch_shapes=[
            pltpu.VMEM((TB, TB), jnp.float32),
            pltpu.VMEM((16, TB), jnp.float32),
            pltpu.SemaphoreType.DMA((16,)),
            pltpu.SemaphoreType.DMA((16,)),
        ],
        compiler_params=pltpu.CompilerParams(
            collective_id=0, has_side_effects=True, vmem_limit_bytes=VMEM_LIMIT
        ),
        name="gather_elements",
    )(jnp.asarray(field_map()), conn, extract, points)


def split(value):
    high = value.astype(jnp.bfloat16)
    return high, (value - high.astype(jnp.float32)).astype(jnp.bfloat16)


def build_phi(fields, start, weigh, spread, high_ref, low_ref):
    lane = lax.broadcasted_iota(jnp.int32, (QP, TB), 1)
    cell_y = lane % EY
    cell_x = lane // EY
    target = fields[FC : FC + QP, :].astype(jnp.int32) - start
    target = jnp.where(target < 0, target + M, target)
    place = 3 * (target // EY - cell_x) + (target % EY - cell_y + EY) % EY
    weight = fields[FW : FW + QP, :]
    slots = [jnp.zeros((QP, TB), jnp.float32) for _ in range(QP)]
    for a in range(QP):
        value = fields[FV + QP * a : FV + QP * (a + 1), :]
        if weigh:
            value = value * weight
        here_a = jnp.broadcast_to(place[a : a + 1, :], (QP, TB))
        for n in range(QP):
            slots[n] = jnp.where(here_a == n, value, slots[n])
    for jx in range(6):
        for t in range(3):
            row = jnp.zeros((QP, TB), jnp.float32)
            for step in range(3):
                if 0 <= jx - step <= 3:
                    row = jnp.where(cell_x == jx - step, slots[3 * step + t], row)
            spread[3 * jx + t, 0:QP, :] = row
    rows = EY
    wide_y = lax.broadcasted_iota(jnp.int32, (rows, TB), 1) % EY
    down_y = lax.broadcasted_iota(jnp.int32, (rows, TB), 0)
    hits = [(wide_y + t) % EY == down_y for t in range(3)]
    for jx in range(6):
        for k in range(QP):
            value = jnp.zeros((rows, TB), jnp.float32)
            for t in range(3):
                line = jnp.broadcast_to(spread[3 * jx + t, k : k + 1, :], (rows, TB))
                value = jnp.where(hits[t], line, value)
            high, low = split(value)
            high_ref[rows * jx : rows * (jx + 1), TB * k : TB * (k + 1)] = high
            low_ref[rows * jx : rows * (jx + 1), TB * k : TB * (k + 1)] = low


def nt(a, b):
    return lax.dot_general(a, b, (((1,), (1,)), ((), ())), preferred_element_type=jnp.float32)


def nn(a, b):
    return lax.dot_general(a, b, (((1,), (0,)), ((), ())), preferred_element_type=jnp.float32)


HALF_X = float(EX) / 4.0
HALF_Y = float(EY) / 4.0


def pair_kernel(
    rec_ref, x_ref, total_ref, fields, spread, phi_hi, phi_lo, trial_x, trial_y, splat, kern, pot, col_sum
):
    mb, mg = here()
    hi, lo, diag = own_pair(mb, mg)
    cell_y = lax.broadcasted_iota(jnp.int32, (QP, TB), 1) % EY
    first = lax.broadcasted_iota(jnp.int32, (16, TB), 0) == 0
    for slot, block in ((0, hi), (1, lo)):
        view = fields.at[slot]
        view[...] = rec_ref[slot].T
        build_phi(view, block * TB, True, spread, phi_hi.at[slot], phi_lo.at[slot])
        for ref in (phi_hi, phi_lo):
            ref[slot, AUG:WIN, :] = jnp.zeros((WIN - AUG, PTS), jnp.bfloat16)
        for k in range(QP):
            weight = jnp.broadcast_to(view[FW + k : FW + k + 1, :], (16, TB))
            high, low = split(jnp.where(first, weight, 0.0))
            phi_hi[slot, AUG : AUG + 16, TB * k : TB * (k + 1)] = high
            phi_lo[slot, AUG : AUG + 16, TB * k : TB * (k + 1)] = low
        trial_x[slot, 0:QP, :] = view[FX : FX + QP, :] * (EX / 2.0) + HALF_X
        for quarter in range(4):
            turn = jnp.where(cell_y > 8 * quarter + 8, HALF_Y - 2.0 * HALF_Y, HALF_Y)
            trial_y[slot, quarter, 0:QP, :] = view[FY : FY + QP, :] * (EX / 2.0) + turn
    total_ref[...] = jnp.zeros_like(total_ref)
    x_ref[1] = jnp.zeros((WIN, WIN), jnp.float32)

    def run(r, carry):
        p_slot = jnp.where(diag, r, 0)
        q_slot = jnp.where(diag, r, 1)
        col_sum[...] = jnp.zeros_like(col_sum)

        def chunk(i, j):
            qx = jnp.broadcast_to(trial_x[q_slot, pl.ds(j, 1), :], (8, TB))
            qy = [
                jnp.broadcast_to(trial_y[q_slot, quarter, pl.ds(j, 1), :], (8, TB)) for quarter in range(4)
            ]
            sums = jnp.zeros((8, TB), jnp.float32)
            for h in range(8):
                values = []
                for n in (2 * h, 2 * h + 1):
                    rows = slice(8 * n, 8 * n + 8)
                    gap_x = HALF_X - jnp.abs(splat[0, rows, :] - qx)
                    gap_y = HALF_Y - jnp.abs(splat[1, rows, :] - qy[n % 4])
                    root = lax.rsqrt(1.0 + (gap_x * gap_x + gap_y * gap_y))
                    square = root * root
                    value = square * square * lax.rsqrt(root)
                    sums = sums + value * splat[2, rows, :]
                    values.append(value)
                kern[TB * i + 16 * h : TB * i + 16 * h + 16, pl.ds(pl.multiple_of(j * TB, TB), TB)] = (
                    jnp.concatenate(values, axis=0).astype(jnp.bfloat16)
                )
            return jnp.sum(sums, axis=0, keepdims=True)

        for i in range(QP):
            for n, base in ((0, FX), (1, FY), (2, FW)):
                picked = rec_ref[p_slot, :, base + i : base + i + 1] * (EX / 2.0 if n < 2 else KERNEL_GAIN)
                splat[n] = jnp.broadcast_to(picked, (TB, TB))

            @pl.when(jnp.logical_not(diag))
            def _(i=i):
                def full(j, carry):
                    col_sum[pl.ds(j, 1), :] += chunk(i, j)
                    return carry

                lax.fori_loop(0, QP, full, 0, unroll=3)

            @pl.when(diag)
            def _(i=i):
                if i > 0:
                    kern[TB * i : TB * (i + 1), 0 : TB * i] = jnp.zeros((TB, TB * i), jnp.bfloat16)
                col_sum[i : i + 1, :] += 0.5 * chunk(i, i)
                here_i = slice(TB * i, TB * (i + 1))
                kern[here_i, here_i] = kern[here_i, here_i] * 0.5

                def part(j, carry):
                    col_sum[pl.ds(j, 1), :] += chunk(i, j)
                    return carry

                lax.fori_loop(i + 1, QP, part, 0)

        pot[...] = nt(kern[...], phi_hi[q_slot]) + nt(kern[...], phi_lo[q_slot])
        total_ref[q_slot, 0:QP, :] += col_sum[0:QP, :]
        for i in range(QP):
            column = pot[TB * i : TB * (i + 1), TB:WIN].T
            total_ref[p_slot, i : i + 1, :] += column[AUG - TB : AUG - TB + 1, :] * KERNEL_GAIN
        high, low = split(pot[...])
        inside = jnp.logical_and(
            lax.broadcasted_iota(jnp.int32, (WIN, WIN), 0) < AUG,
            lax.broadcasted_iota(jnp.int32, (WIN, WIN), 1) < AUG,
        )
        value = nn(phi_hi[p_slot], high) + nn(phi_lo[p_slot], high) + nn(phi_hi[p_slot], low)
        x_ref[r] = jnp.where(inside, KERNEL_GAIN * value, 0.0)
        return carry

    lax.fori_loop(0, jnp.where(diag, 2, 1), run, 0)


def pair_work(records):
    vmem = pl.BlockSpec(memory_space=pltpu.VMEM)
    return pl.pallas_call(
        pair_kernel,
        out_shape=(
            jax.ShapeDtypeStruct((2, WIN, WIN), jnp.float32),
            jax.ShapeDtypeStruct((2, 16, TB), jnp.float32),
        ),
        in_specs=[vmem],
        out_specs=(vmem, vmem),
        scratch_shapes=[
            pltpu.VMEM((2, TB, TB), jnp.float32),
            pltpu.VMEM((18, 16, TB), jnp.float32),
            pltpu.VMEM((2, WIN, PTS), jnp.bfloat16),
            pltpu.VMEM((2, WIN, PTS), jnp.bfloat16),
            pltpu.VMEM((2, 16, TB), jnp.float32),
            pltpu.VMEM((2, 4, 16, TB), jnp.float32),
            pltpu.VMEM((3, TB, TB), jnp.float32),
            pltpu.VMEM((PTS, PTS), jnp.bfloat16),
            pltpu.VMEM((PTS, WIN), jnp.float32),
            pltpu.VMEM((16, TB), jnp.float32),
        ],
        compiler_params=pltpu.CompilerParams(vmem_limit_bytes=VMEM_LIMIT),
        name="pair_blocks",
    )(records)


def totals_kernel(total_ref, out_ref, send_sem, recv_sem):
    mb, mg = here()
    hi, lo, diag = own_pair(mb, mg)
    barrier = pltpu.get_barrier_semaphore()

    def copy(slot):
        mine, other = (hi, lo) if slot == 0 else (lo, hi)
        return pltpu.make_async_remote_copy(
            src_ref=total_ref.at[slot],
            dst_ref=out_ref.at[mine // BLK, other],
            send_sem=send_sem.at[slot],
            recv_sem=recv_sem.at[mine // BLK, other],
            device_id=(mine % BLK, mine % BLK),
            device_id_type=MESH,
        )

    @pl.when(diag)
    def _():
        def say(n, carry):
            block, other = mg + (n // 16) * BLK, n % 16

            @pl.when(block != other)
            def _():
                b, g = pair_device(block, other)
                greet(barrier, b, g)

            return carry

        lax.fori_loop(0, 32, say, 0)
        for slot in range(2):
            out_ref[slot, mg + slot * BLK] = total_ref[slot]

        def take(n, carry):
            half, other = n // 16, n % 16

            @pl.when(mg + half * BLK != other)
            def _():
                pltpu.make_async_remote_copy(
                    src_ref=total_ref.at[0],
                    dst_ref=out_ref.at[half, other],
                    send_sem=send_sem.at[0],
                    recv_sem=recv_sem.at[half, other],
                    device_id=(mb, mg),
                    device_id_type=MESH,
                ).wait_recv()

            return carry

        lax.fori_loop(0, 32, take, 0)

    @pl.when(jnp.logical_not(diag))
    def _():
        pl.semaphore_wait(barrier, 2)
        for slot in range(2):
            copy(slot).start()
        for slot in range(2):
            copy(slot).wait_send()


def totals_exchange(total):
    vmem = pl.BlockSpec(memory_space=pltpu.VMEM)
    return pl.pallas_call(
        totals_kernel,
        out_shape=jax.ShapeDtypeStruct((2, 16, 16, TB), jnp.float32),
        in_specs=[vmem],
        out_specs=vmem,
        scratch_shapes=[pltpu.SemaphoreType.DMA((2,)), pltpu.SemaphoreType.DMA((2, 16))],
        compiler_params=pltpu.CompilerParams(
            collective_id=1, has_side_effects=True, vmem_limit_bytes=VMEM_LIMIT
        ),
        name="send_totals",
    )(total)


def pieces_kernel(rec_ref, x_ref, parts_ref, out_ref, fields, spread, phi_hi, phi_lo):
    mb, mg = here()
    hi, lo, diag = own_pair(mb, mg)

    @pl.when(jnp.logical_not(diag))
    def _():
        for n in range(4):
            u, v = n // 2, n % 2
            piece = -x_ref[0, TB * u : TB * (u + 1), TB * v : TB * (v + 1)]
            row, col = (hi + u) % 16, (lo + v) % 16
            if u == 0 and v == 0:
                out_ref[n] = piece
            else:
                other = piece.T
                out_ref[n] = jnp.where(row < col, 0.0, piece) + jnp.where(row > col, 0.0, other)

    @pl.when(diag)
    def _():
        for r in range(2):
            block = mg + BLK * r
            fields[...] = rec_ref[r].T
            build_phi(fields, block * TB, False, spread, phi_hi, phi_lo)
            for ref in (phi_hi, phi_lo):
                ref[AUG:WIN, :] = jnp.zeros((WIN - AUG, PTS), jnp.bfloat16)
            gain = jnp.sum(parts_ref[r], axis=0)
            mass = jnp.zeros((WIN, WIN), jnp.float32)
            for k in range(QP):
                lanes = slice(TB * k, TB * (k + 1))
                left = phi_hi[:, lanes].astype(jnp.float32) + phi_lo[:, lanes].astype(jnp.float32)
                factor = fields[FW + k : FW + k + 1, :] * (MASS_SHIFT + gain[k : k + 1, :])
                high, low = split(left * factor)
                mass += (
                    nt(high, phi_hi[:, lanes]) + nt(low, phi_hi[:, lanes]) + nt(high, phi_lo[:, lanes])
                )
            x = x_ref[r]
            for n, (u, v) in enumerate(((0, 0), (1, 0), (1, 1))):
                one = x[TB * u : TB * (u + 1), TB * v : TB * (v + 1)]
                two = x[TB * v : TB * (v + 1), TB * u : TB * (u + 1)]
                whole = mass[TB * u : TB * (u + 1), TB * v : TB * (v + 1)] - one - two.T
                if u != v and r == 1:
                    flip = block == 15
                    whole = jnp.where(flip, 0.0, whole) + jnp.where(flip, whole.T, 0.0)
                out_ref[3 * r + n] = whole


def make_pieces(records, x, parts):
    vmem = pl.BlockSpec(memory_space=pltpu.VMEM)
    return pl.pallas_call(
        pieces_kernel,
        out_shape=jax.ShapeDtypeStruct((6, TB, TB), jnp.float32),
        in_specs=[vmem] * 3,
        out_specs=vmem,
        scratch_shapes=[
            pltpu.VMEM((TB, TB), jnp.float32),
            pltpu.VMEM((18, 16, TB), jnp.float32),
            pltpu.VMEM((WIN, PTS), jnp.bfloat16),
            pltpu.VMEM((WIN, PTS), jnp.bfloat16),
        ],
        compiler_params=pltpu.CompilerParams(vmem_limit_bytes=VMEM_LIMIT),
        name="make_pieces",
    )(records, x, parts)


def piece_target(n, hi, lo, diag, g):
    u, v = n // 2, n % 2
    row, col = (hi + u) % 16, (lo + v) % 16
    slot = jnp.where(row == col, 1, jnp.where(row > col, 2 * u + v, 2 * v + u))
    r, m = n // 3, n % 3
    block = g + BLK * r
    after = (block + 1) % 16
    drow = jnp.where(m == 0, block, jnp.where(m == 1, jnp.maximum(block, after), after))
    dcol = jnp.where(m == 0, block, jnp.where(m == 1, jnp.minimum(block, after), after))
    dslot = jnp.where(m == 0, 0, jnp.where(m == 1, jnp.where(block == 15, 1, 2), 3))
    big = jnp.where(diag, drow, jnp.maximum(row, col))
    small = jnp.where(diag, dcol, jnp.minimum(row, col))
    there = jnp.where(diag, 6, 4) > n
    return small % BLK, big, small // BLK, jnp.where(diag, dslot, slot), there


def piece_source(t, s, b, g):
    row, col = g, b + BLK * t
    there = jnp.logical_and(row >= col, jnp.logical_not(jnp.logical_and(row == col, s == 2)))
    sb, sg = pair_device((row - s // 2 + 16) % 16, (col - s % 2 + 16) % 16)
    return sb, sg, there


def reduce_kernel(piece_ref, out_ref, landed, send_sem, recv_sem):
    mb, mg = here()
    hi, lo, diag = own_pair(mb, mg)
    barrier = pltpu.get_barrier_semaphore()

    def say(n, carry):
        sb, sg, there = piece_source(n // 4, n % 4, mb, mg)

        @pl.when(jnp.logical_and(there, differs(sb, sg, mb, mg)))
        def _():
            greet(barrier, sb, sg)

        return carry

    lax.fori_loop(0, 8, say, 0)

    def count(n, total):
        b, g, t, s, there = piece_target(n, hi, lo, diag, mg)
        return total + jnp.where(jnp.logical_and(there, differs(b, g, mb, mg)), 1, 0)

    gather_greetings(barrier, lax.fori_loop(0, 6, count, 0))

    def copy(n):
        b, g, t, s, there = piece_target(n, hi, lo, diag, mg)
        return pltpu.make_async_remote_copy(
            src_ref=piece_ref.at[n],
            dst_ref=landed.at[t, s],
            send_sem=send_sem.at[n],
            recv_sem=recv_sem.at[t, s],
            device_id=(b, g),
            device_id_type=MESH,
        )

    def send(n, carry):
        b, g, t, s, there = piece_target(n, hi, lo, diag, mg)
        away = differs(b, g, mb, mg)

        @pl.when(jnp.logical_and(there, away))
        def _():
            copy(n).start()

        @pl.when(jnp.logical_and(there, jnp.logical_not(away)))
        def _():
            landed[t, s] = piece_ref[n]

        return carry

    lax.fori_loop(0, 6, send, 0)
    out_ref[...] = jnp.zeros_like(out_ref)

    def take(n, carry):
        t, s = n // 4, n % 4
        sb, sg, there = piece_source(t, s, mb, mg)

        @pl.when(there)
        def _():
            @pl.when(differs(sb, sg, mb, mg))
            def _():
                pltpu.make_async_remote_copy(
                    src_ref=piece_ref.at[0],
                    dst_ref=landed.at[t, s],
                    send_sem=send_sem.at[0],
                    recv_sem=recv_sem.at[t, s],
                    device_id=(sb, sg),
                    device_id_type=MESH,
                ).wait_recv()

            out_ref[t] += landed[t, s]

        return carry

    lax.fori_loop(0, 8, take, 0)

    def drain(n, carry):
        b, g, t, s, there = piece_target(n, hi, lo, diag, mg)

        @pl.when(jnp.logical_and(there, differs(b, g, mb, mg)))
        def _():
            copy(n).wait_send()

        return carry

    lax.fori_loop(0, 6, drain, 0)


def reduce_pieces(pieces):
    vmem = pl.BlockSpec(memory_space=pltpu.VMEM)
    return pl.pallas_call(
        reduce_kernel,
        out_shape=jax.ShapeDtypeStruct((2, TB, TB), jnp.float32),
        in_specs=[vmem],
        out_specs=vmem,
        scratch_shapes=[
            pltpu.VMEM((2, 4, TB, TB), jnp.float32),
            pltpu.SemaphoreType.DMA((6,)),
            pltpu.SemaphoreType.DMA((2, 4)),
        ],
        compiler_params=pltpu.CompilerParams(
            collective_id=2, has_side_effects=True, vmem_limit_bytes=VMEM_LIMIT
        ),
        name="sum_pieces",
    )(pieces)


def panel_kernel(tile_ref, out_ref, send_sem, recv_sem):
    mb, mg = here()
    barrier = pltpu.get_barrier_semaphore()
    first = mb == 0
    root = jnp.logical_and(first, mg == 0)
    relay = jnp.logical_and(mg >= 1, mb == mg % BLK)

    def wants(t):
        col = mb + BLK * t
        return jnp.logical_and(col >= 1, mg > col)

    @pl.when(jnp.logical_not(first))
    def _():
        greet(barrier, 0, mg)

    @pl.when(jnp.logical_and(first, mg > 0))
    def _():
        greet(barrier, 0, 0)

    for t in range(2):
        @pl.when(wants(t))
        def _(t=t):
            greet(barrier, mb, mb + BLK * t)

    expected = (
        jnp.where(first, BLK - 1, 0)
        + jnp.where(root, GRID - 1, 0)
        + jnp.where(relay, GRID - 1 - mg, 0)
    )
    gather_greetings(barrier, expected)

    def copy(source, n, sem, b, g):
        return pltpu.make_async_remote_copy(
            src_ref=source,
            dst_ref=out_ref.at[n],
            send_sem=send_sem.at[sem],
            recv_sem=recv_sem.at[n],
            device_id=(b, g),
            device_id_type=MESH,
        )

    @pl.when(root)
    def _():
        out_ref[0] = tile_ref[0]

    def root_send(g, carry):
        copy(tile_ref.at[0], 0, g, 0, g).start()
        return carry

    @pl.when(root)
    def _():
        lax.fori_loop(1, GRID, root_send, 0)

    @pl.when(first)
    def _():
        out_ref[1] = tile_ref[0]

        def row_send(b, carry):
            copy(tile_ref.at[0], 1, 16 + b, b, mg).start()
            return carry

        lax.fori_loop(1, BLK, row_send, 0)

    @pl.when(jnp.logical_not(first))
    def _():
        copy(tile_ref.at[0], 1, 0, mb, mg).wait_recv()

    def relay_copy(g):
        return copy(out_ref.at[1], 2 + mg // BLK, 40 + g, mb, g)

    @pl.when(relay)
    def _():
        def relay_send(g, carry):
            relay_copy(g).start()
            return carry

        lax.fori_loop(mg + 1, GRID, relay_send, 0)

    @pl.when(jnp.logical_not(root))
    def _():
        copy(tile_ref.at[0], 0, 0, mb, mg).wait_recv()

    @pl.when(first)
    def _():
        def head_send(b, carry):
            copy(out_ref.at[0], 0, 24 + b, b, mg).start()
            return carry

        lax.fori_loop(1, BLK, head_send, 0)

    for t in range(2):
        col = mb + BLK * t

        @pl.when(mg == col)
        def _(t=t):
            out_ref[2 + t] = out_ref[1]

        @pl.when(wants(t))
        def _(t=t):
            copy(tile_ref.at[0], 2 + t, 0, mb, mg).wait_recv()

        @pl.when(jnp.logical_not(jnp.logical_or(mg == col, wants(t))))
        def _(t=t):
            out_ref[2 + t] = jnp.zeros((TB, TB), jnp.float32)

    @pl.when(root)
    def _():
        def root_wait(g, carry):
            copy(tile_ref.at[0], 0, g, 0, g).wait_send()
            return carry

        lax.fori_loop(1, GRID, root_wait, 0)

    @pl.when(first)
    def _():
        def row_wait(b, carry):
            copy(tile_ref.at[0], 1, 16 + b, b, mg).wait_send()
            copy(out_ref.at[0], 0, 24 + b, b, mg).wait_send()
            return carry

        lax.fori_loop(1, BLK, row_wait, 0)

    @pl.when(relay)
    def _():
        def relay_wait(g, carry):
            relay_copy(g).wait_send()
            return carry

        lax.fori_loop(mg + 1, GRID, relay_wait, 0)


def share_panel(tiles):
    vmem = pl.BlockSpec(memory_space=pltpu.VMEM)
    return pl.pallas_call(
        panel_kernel,
        out_shape=jax.ShapeDtypeStruct((4, TB, TB), jnp.float32),
        in_specs=[vmem],
        out_specs=vmem,
        scratch_shapes=[pltpu.SemaphoreType.DMA((56,)), pltpu.SemaphoreType.DMA((4,))],
        compiler_params=pltpu.CompilerParams(
            collective_id=3, has_side_effects=True, vmem_limit_bytes=VMEM_LIMIT
        ),
        name="share_panel",
    )(tiles)


STEP = 16


def both(value):
    return jnp.concatenate([value, value], axis=1)


def eliminate(work):
    at = lax.broadcasted_iota(jnp.int32, (8, WIN), 0)
    for top in range(0, TB, STEP):
        rows = [jnp.broadcast_to(work[top + i : top + i + 1, :], (8, WIN)) for i in range(STEP)]
        entry = {
            (i, j): jnp.broadcast_to(rows[i][:, top + j : top + j + 1], (8, TB))
            for i in range(STEP)
            for j in range(i + 1)
        }
        for j in range(STEP):
            scale = lax.rsqrt(entry[j, j])
            for i in range(j + 1, STEP):
                entry[i, j] = entry[i, j] * scale
            for i in range(j + 1, STEP):
                for k in range(j + 1, i + 1):
                    entry[i, k] = entry[i, k] - entry[i, j] * entry[k, j]
            rows[j] = rows[j] * both(scale)
            for i in range(j + 1, STEP):
                rows[i] = rows[i] - both(entry[i, j]) * rows[j]
        groups = []
        for g in range(0, STEP, 8):
            group = rows[g]
            for i in range(1, 8):
                group = jnp.where(at == i, rows[g + i], group)
            groups.append(group)
        panel = jnp.concatenate(groups, axis=0)
        work[top : top + STEP, :] = panel
        after = top + STEP
        if after < TB:
            high, low = split(panel)
            left = jnp.concatenate([high, high, low], axis=0)
            right = jnp.concatenate([high, low, high], axis=0)
            for lo, up in ((after, after + STEP), (after + STEP, TB)):
                if lo < up:
                    work[lo:up, :] -= lax.dot_general(
                        left[:, lo:up],
                        right,
                        (((0,), (0,)), ((), ())),
                        preferred_element_type=jnp.float32,
                    )


def nt3(a, b):
    (a_hi, a_lo), (b_hi, b_lo) = split(a), split(b)
    return nt(a_hi, b_hi) + (nt(a_lo, b_hi) + nt(a_hi, b_lo))


def factor_kernel(panel_ref, tile_ref, out_ref, work):
    mb, mg = here()
    head = panel_ref[0]
    row = lax.broadcasted_iota(jnp.int32, (TB, TB), 0)
    col = lax.broadcasted_iota(jnp.int32, (TB, TB), 1)
    work[:, 0:TB] = 0.5 * (head + head.T)
    work[:, TB:WIN] = jnp.where(row == col, 1.0, 0.0)
    eliminate(work)
    lower = jnp.where(row >= col, work[:, 0:TB].T, 0.0)
    inverse = jnp.where(row >= col, work[:, TB:WIN], 0.0)
    solved = nt3(panel_ref[1:4].reshape(3 * TB, TB), inverse)
    left = jnp.where(mg == 0, lower, solved[0:TB])
    update = nt3(left, solved[TB : 3 * TB])
    for t in range(2):
        tile_col = mb + BLK * t
        value = jnp.where(tile_col == 0, left, tile_ref[t] - update[:, TB * t : TB * (t + 1)])
        keep = mg * TB + row >= tile_col * TB + col
        out_ref[0, :, t, :] = jnp.where(keep, value, 0.0)


def factor(panel, tiles):
    vmem = pl.BlockSpec(memory_space=pltpu.VMEM)
    return pl.pallas_call(
        factor_kernel,
        out_shape=jax.ShapeDtypeStruct((1, TB, 2, TB), jnp.float32),
        in_specs=[vmem] * 2,
        out_specs=vmem,
        scratch_shapes=[pltpu.VMEM((TB, WIN), jnp.float32)],
        compiler_params=pltpu.CompilerParams(vmem_limit_bytes=VMEM_LIMIT),
        name="factor_tiles",
    )(panel, tiles)


def shards(conn, extract, points):
    records = gather(conn, extract, points)
    x, total = pair_work(records)
    parts = totals_exchange(total)
    pieces = make_pieces(records, x, parts)
    tiles = reduce_pieces(pieces)
    panel = share_panel(tiles)
    return factor(panel, tiles)


def solution(mesh):
    in_specs = (
        P(("blk", "grid"), None),
        P(None, None, ("blk", "grid")),
        P(None, None, ("blk", "grid")),
    )
    out_specs = P(None, "grid", None, "blk")
    return jax.shard_map(shards, mesh=mesh, in_specs=in_specs, out_specs=out_specs, check_vma=False)
```

```python
import functools
import math

import jax
import jax.numpy as jnp
import numpy as np
from jax import lax
from jax.experimental import pallas as pl
from jax.experimental.pallas import tpu as pltpu
from jax.sharding import PartitionSpec as P

M = 2048
EX = 64
EY = 32
QP = 9
TB = 128
BLK = 8
GRID = 16
PTS = QP * TB
WIN = 256
AUG = 192

KERNEL_GAIN = 0.02
MASS_SHIFT = 0.05

FX, FY, FW, FV, FC = 0, 9, 18, 27, 108

MESH = pl.DeviceIdType.MESH
VMEM_LIMIT = 48 * 1024 * 1024
EXACT = lax.Precision.HIGHEST


def bernstein_table():
    spread_root = 0.5 * math.sqrt(0.6)
    nodes = [0.5 - spread_root, 0.5, 0.5 + spread_root]
    poly = [[(1.0 - t) ** 2, 2.0 * t * (1.0 - t), t * t] for t in nodes]
    return np.array(
        [
            [poly[i][a] * poly[j][b] for a in range(3) for b in range(3)]
            for i in range(3)
            for j in range(3)
        ],
        np.float32,
    )


def field_map():
    table = np.zeros((TB, TB), np.float32)
    bern = bernstein_table()
    for i in range(FV):
        table[i, i] = 1.0
    for i in range(FC, FC + QP):
        table[i, i] = 1.0
    for k in range(QP):
        for a in range(QP):
            for b in range(QP):
                table[FV + a * QP + k, FV + a * QP + b] = bern[k, b]
    return table


def pair_device(first, second):
    hi, lo = jnp.maximum(first, second), jnp.minimum(first, second)
    same = hi == lo
    low = lo < BLK
    b = jnp.where(same, hi % BLK, jnp.where(low, lo, hi - BLK))
    g = jnp.where(same, hi % BLK, jnp.where(low, hi, lo - BLK))
    return b, g


def here():
    return lax.axis_index("blk"), lax.axis_index("grid")


def own_pair(b, g):
    diag = b == g
    hi = jnp.where(g >= b, g, b + BLK)
    lo = jnp.where(g > b, b, g + BLK)
    return hi, lo, diag


def greet(barrier, b, g):
    pl.semaphore_signal(barrier, inc=1, device_id=(b, g), device_id_type=MESH)


def gather_greetings(barrier, number):
    @pl.when(number > 0)
    def _():
        pl.semaphore_wait(barrier, number)


def differs(b, g, mb, mg):
    return jnp.logical_or(b != mb, g != mg)


def gather_kernel(map_ref, conn_ref, extract_ref, points_ref, out_ref, raw, record, send_sem, recv_sem):
    mb, mg = here()
    hi, lo, diag = own_pair(mb, mg)
    block = 2 * mb + mg // 8
    place = mg % 8
    barrier = pltpu.get_barrier_semaphore()

    def source(n):
        wanted = jnp.where(n // 8 == 0, hi, lo)
        return wanted // 2, (wanted % 2) * 8 + n % 8

    def say(n, carry):
        b, g = source(n)

        @pl.when(differs(b, g, mb, mg))
        def _():
            greet(barrier, b, g)

        return carry

    lax.fori_loop(0, 16, say, 0)

    raw[...] = jnp.zeros_like(raw)
    for c in range(3):
        raw[9 * c : 9 * c + 9, 0:16] = points_ref[c]
    for a in range(QP):
        raw[FV + 9 * a : FV + 9 * a + 9, 0:16] = extract_ref[a]
    raw[FC : FC + 9, 0:16] = conn_ref[...].astype(jnp.float32).T
    made = jnp.dot(map_ref[...], raw[...], precision=EXACT, preferred_element_type=jnp.float32)
    record[...] = made.T[0:16, :]

    own_dest = lambda j: pair_device(block, j)

    def count(j, total):
        b, g = own_dest(j)
        return total + jnp.where(differs(b, g, mb, mg), 1, 0)

    gather_greetings(barrier, lax.fori_loop(0, 16, count, 0))

    def slot_of(j):
        diag_pair = j == block
        return jnp.where(diag_pair, block // BLK, jnp.where(block > j, 0, 1))

    def copy(j):
        b, g = own_dest(j)
        slot = slot_of(j)
        return pltpu.make_async_remote_copy(
            src_ref=record,
            dst_ref=out_ref.at[slot, pl.ds(16 * place, 16), :],
            send_sem=send_sem.at[j],
            recv_sem=recv_sem.at[slot * 8 + place],
            device_id=(b, g),
            device_id_type=MESH,
        )

    def send(j, carry):
        b, g = own_dest(j)
        away = differs(b, g, mb, mg)

        @pl.when(away)
        def _():
            copy(j).start()

        @pl.when(jnp.logical_not(away))
        def _():
            out_ref[slot_of(j), pl.ds(pl.multiple_of(16 * place, 16), 16), :] = record[...]

        return carry

    lax.fori_loop(0, 16, send, 0)

    def finish(n, carry):
        b, g = source(n)

        @pl.when(differs(b, g, mb, mg))
        def _():
            pltpu.make_async_remote_copy(
                src_ref=record,
                dst_ref=out_ref.at[n // 8, pl.ds(16 * (n % 8), 16), :],
                send_sem=send_sem.at[n],
                recv_sem=recv_sem.at[n],
                device_id=(b, g),
                device_id_type=MESH,
            ).wait_recv()

        db, dg = own_dest(n)

        @pl.when(differs(db, dg, mb, mg))
        def _():
            copy(n).wait_send()

        return carry

    lax.fori_loop(0, 16, finish, 0)


def split(value):
    high = value.astype(jnp.bfloat16)
    return high, (value - high.astype(jnp.float32)).astype(jnp.bfloat16)


def build_phi(fields, start, weigh, spread, high_ref, low_ref):
    lane = lax.broadcasted_iota(jnp.int32, (QP, TB), 1)
    cell_y = lane % EY
    cell_x = lane // EY
    target = fields[FC : FC + QP, :].astype(jnp.int32) - start
    target = jnp.where(target < 0, target + M, target)
    place = 3 * (target // EY - cell_x) + (target % EY - cell_y + EY) % EY
    weight = fields[FW : FW + QP, :]
    slots = [jnp.zeros((QP, TB), jnp.float32) for _ in range(QP)]
    for a in range(QP):
        value = fields[FV + QP * a : FV + QP * (a + 1), :]
        if weigh:
            value = value * weight
        here_a = jnp.broadcast_to(place[a : a + 1, :], (QP, TB))
        for n in range(QP):
            slots[n] = jnp.where(here_a == n, value, slots[n])
    for jx in range(6):
        for t in range(3):
            row = jnp.zeros((QP, TB), jnp.float32)
            for step in range(3):
                if 0 <= jx - step <= 3:
                    row = jnp.where(cell_x == jx - step, slots[3 * step + t], row)
            spread[3 * jx + t, 0:QP, :] = row
    rows = EY
    wide_y = lax.broadcasted_iota(jnp.int32, (rows, TB), 1) % EY
    down_y = lax.broadcasted_iota(jnp.int32, (rows, TB), 0)
    hits = [(wide_y + t) % EY == down_y for t in range(3)]
    for jx in range(6):
        for k in range(QP):
            value = jnp.zeros((rows, TB), jnp.float32)
            for t in range(3):
                line = jnp.broadcast_to(spread[3 * jx + t, k : k + 1, :], (rows, TB))
                value = jnp.where(hits[t], line, value)
            high, low = split(value)
            high_ref[rows * jx : rows * (jx + 1), TB * k : TB * (k + 1)] = high
            low_ref[rows * jx : rows * (jx + 1), TB * k : TB * (k + 1)] = low


def nt(a, b):
    return lax.dot_general(a, b, (((1,), (1,)), ((), ())), preferred_element_type=jnp.float32)


def nn(a, b):
    return lax.dot_general(a, b, (((1,), (0,)), ((), ())), preferred_element_type=jnp.float32)


HALF_X = float(EX) / 4.0
HALF_Y = float(EY) / 4.0


def pair_kernel(
    rec_ref, x_ref, total_ref, fields, spread, phi_hi, phi_lo, trial_x, trial_y, splat, kern, pot, col_sum
):
    mb, mg = here()
    hi, lo, diag = own_pair(mb, mg)
    cell_y = lax.broadcasted_iota(jnp.int32, (QP, TB), 1) % EY
    first = lax.broadcasted_iota(jnp.int32, (16, TB), 0) == 0
    for slot, block in ((0, hi), (1, lo)):
        view = fields.at[slot]
        view[...] = rec_ref[slot].T
        build_phi(view, block * TB, True, spread, phi_hi.at[slot], phi_lo.at[slot])
        for ref in (phi_hi, phi_lo):
            ref[slot, AUG:WIN, :] = jnp.zeros((WIN - AUG, PTS), jnp.bfloat16)
        for k in range(QP):
            weight = jnp.broadcast_to(view[FW + k : FW + k + 1, :], (16, TB))
            high, low = split(jnp.where(first, weight, 0.0))
            phi_hi[slot, AUG : AUG + 16, TB * k : TB * (k + 1)] = high
            phi_lo[slot, AUG : AUG + 16, TB * k : TB * (k + 1)] = low
        trial_x[slot, 0:QP, :] = view[FX : FX + QP, :] * (EX / 2.0) + HALF_X
        for quarter in range(4):
            turn = jnp.where(cell_y > 8 * quarter + 8, HALF_Y - 2.0 * HALF_Y, HALF_Y)
            trial_y[slot, quarter, 0:QP, :] = view[FY : FY + QP, :] * (EX / 2.0) + turn
    total_ref[...] = jnp.zeros_like(total_ref)
    x_ref[1] = jnp.zeros((WIN, WIN), jnp.float32)

    def run(r, carry):
        p_slot = jnp.where(diag, r, 0)
        q_slot = jnp.where(diag, r, 1)
        col_sum[...] = jnp.zeros_like(col_sum)

        def chunk(i, j):
            qx = jnp.broadcast_to(trial_x[q_slot, pl.ds(j, 1), :], (8, TB))
            qy = [
                jnp.broadcast_to(trial_y[q_slot, quarter, pl.ds(j, 1), :], (8, TB)) for quarter in range(4)
            ]
            sums = jnp.zeros((8, TB), jnp.float32)
            for h in range(8):
                values = []
                for n in (2 * h, 2 * h + 1):
                    rows = slice(8 * n, 8 * n + 8)
                    gap_x = HALF_X - jnp.abs(splat[0, rows, :] - qx)
                    gap_y = HALF_Y - jnp.abs(splat[1, rows, :] - qy[n % 4])
                    root = lax.rsqrt(1.0 + (gap_x * gap_x + gap_y * gap_y))
                    square = root * root
                    value = square * square * lax.rsqrt(root)
                    sums = sums + value * splat[2, rows, :]
                    values.append(value)
                kern[TB * i + 16 * h : TB * i + 16 * h + 16, pl.ds(pl.multiple_of(j * TB, TB), TB)] = (
                    jnp.concatenate(values, axis=0).astype(jnp.bfloat16)
                )
            return jnp.sum(sums, axis=0, keepdims=True)

        for i in range(QP):
            for n, base in ((0, FX), (1, FY), (2, FW)):
                picked = rec_ref[p_slot, :, base + i : base + i + 1] * (EX / 2.0 if n < 2 else KERNEL_GAIN)
                splat[n] = jnp.broadcast_to(picked, (TB, TB))

            @pl.when(jnp.logical_not(diag))
            def _(i=i):
                def full(j, carry):
                    col_sum[pl.ds(j, 1), :] += chunk(i, j)
                    return carry

                lax.fori_loop(0, QP, full, 0, unroll=3)

            @pl.when(diag)
            def _(i=i):
                if i > 0:
                    kern[TB * i : TB * (i + 1), 0 : TB * i] = jnp.zeros((TB, TB * i), jnp.bfloat16)
                col_sum[i : i + 1, :] += 0.5 * chunk(i, i)
                here_i = slice(TB * i, TB * (i + 1))
                kern[here_i, here_i] = kern[here_i, here_i] * 0.5

                def part(j, carry):
                    col_sum[pl.ds(j, 1), :] += chunk(i, j)
                    return carry

                lax.fori_loop(i + 1, QP, part, 0)

        pot[...] = nt(kern[...], phi_hi[q_slot]) + nt(kern[...], phi_lo[q_slot])
        total_ref[q_slot, 0:QP, :] += col_sum[0:QP, :]
        for i in range(QP):
            column = pot[TB * i : TB * (i + 1), TB:WIN].T
            total_ref[p_slot, i : i + 1, :] += column[AUG - TB : AUG - TB + 1, :] * KERNEL_GAIN
        high, low = split(pot[...])
        inside = jnp.logical_and(
            lax.broadcasted_iota(jnp.int32, (WIN, WIN), 0) < AUG,
            lax.broadcasted_iota(jnp.int32, (WIN, WIN), 1) < AUG,
        )
        value = nn(phi_hi[p_slot], high) + nn(phi_lo[p_slot], high) + nn(phi_hi[p_slot], low)
        x_ref[r] = jnp.where(inside, KERNEL_GAIN * value, 0.0)
        return carry

    lax.fori_loop(0, jnp.where(diag, 2, 1), run, 0)


def gather_pair_kernel(
    map_ref, conn_ref, extract_ref, points_ref, rec_ref, x_ref, total_ref, raw, record, send_sem, recv_sem, *rest
):
    gather_kernel(map_ref, conn_ref, extract_ref, points_ref, rec_ref, raw, record, send_sem, recv_sem)
    pair_kernel(rec_ref, x_ref, total_ref, *rest)


def gather_pair(conn, extract, points):
    vmem = pl.BlockSpec(memory_space=pltpu.VMEM)
    return pl.pallas_call(
        gather_pair_kernel,
        out_shape=(
            jax.ShapeDtypeStruct((2, TB, TB), jnp.float32),
            jax.ShapeDtypeStruct((2, WIN, WIN), jnp.float32),
            jax.ShapeDtypeStruct((2, 16, TB), jnp.float32),
        ),
        in_specs=[vmem] * 4,
        out_specs=(vmem, vmem, vmem),
        scratch_shapes=[
            pltpu.VMEM((TB, TB), jnp.float32),
            pltpu.VMEM((16, TB), jnp.float32),
            pltpu.SemaphoreType.DMA((16,)),
            pltpu.SemaphoreType.DMA((16,)),
            pltpu.VMEM((2, TB, TB), jnp.float32),
            pltpu.VMEM((18, 16, TB), jnp.float32),
            pltpu.VMEM((2, WIN, PTS), jnp.bfloat16),
            pltpu.VMEM((2, WIN, PTS), jnp.bfloat16),
            pltpu.VMEM((2, 16, TB), jnp.float32),
            pltpu.VMEM((2, 4, 16, TB), jnp.float32),
            pltpu.VMEM((3, TB, TB), jnp.float32),
            pltpu.VMEM((PTS, PTS), jnp.bfloat16),
            pltpu.VMEM((PTS, WIN), jnp.float32),
            pltpu.VMEM((16, TB), jnp.float32),
        ],
        compiler_params=pltpu.CompilerParams(
            collective_id=0, has_side_effects=True, vmem_limit_bytes=VMEM_LIMIT
        ),
        name="gather_and_pair",
    )(jnp.asarray(field_map()), conn, extract, points)


def totals_kernel(total_ref, out_ref, send_sem, recv_sem):
    mb, mg = here()
    hi, lo, diag = own_pair(mb, mg)
    barrier = pltpu.get_barrier_semaphore()

    def copy(slot):
        mine, other = (hi, lo) if slot == 0 else (lo, hi)
        return pltpu.make_async_remote_copy(
            src_ref=total_ref.at[slot],
            dst_ref=out_ref.at[mine // BLK, other],
            send_sem=send_sem.at[slot],
            recv_sem=recv_sem.at[mine // BLK, other],
            device_id=(mine % BLK, mine % BLK),
            device_id_type=MESH,
        )

    @pl.when(diag)
    def _():
        def say(n, carry):
            block, other = mg + (n // 16) * BLK, n % 16

            @pl.when(block != other)
            def _():
                b, g = pair_device(block, other)
                greet(barrier, b, g)

            return carry

        lax.fori_loop(0, 32, say, 0)
        for slot in range(2):
            out_ref[slot, mg + slot * BLK] = total_ref[slot]

        def take(n, carry):
            half, other = n // 16, n % 16

            @pl.when(mg + half * BLK != other)
            def _():
                pltpu.make_async_remote_copy(
                    src_ref=total_ref.at[0],
                    dst_ref=out_ref.at[half, other],
                    send_sem=send_sem.at[0],
                    recv_sem=recv_sem.at[half, other],
                    device_id=(mb, mg),
                    device_id_type=MESH,
                ).wait_recv()

            return carry

        lax.fori_loop(0, 32, take, 0)

    @pl.when(jnp.logical_not(diag))
    def _():
        pl.semaphore_wait(barrier, 2)
        for slot in range(2):
            copy(slot).start()
        for slot in range(2):
            copy(slot).wait_send()


def totals_exchange(total):
    vmem = pl.BlockSpec(memory_space=pltpu.VMEM)
    return pl.pallas_call(
        totals_kernel,
        out_shape=jax.ShapeDtypeStruct((2, 16, 16, TB), jnp.float32),
        in_specs=[vmem],
        out_specs=vmem,
        scratch_shapes=[pltpu.SemaphoreType.DMA((2,)), pltpu.SemaphoreType.DMA((2, 16))],
        compiler_params=pltpu.CompilerParams(
            collective_id=1, has_side_effects=True, vmem_limit_bytes=VMEM_LIMIT
        ),
        name="send_totals",
    )(total)


def pieces_kernel(rec_ref, x_ref, parts_ref, out_ref, fields, spread, phi_hi, phi_lo):
    mb, mg = here()
    hi, lo, diag = own_pair(mb, mg)

    @pl.when(jnp.logical_not(diag))
    def _():
        for n in range(4):
            u, v = n // 2, n % 2
            piece = -x_ref[0, TB * u : TB * (u + 1), TB * v : TB * (v + 1)]
            row, col = (hi + u) % 16, (lo + v) % 16
            if u == 0 and v == 0:
                out_ref[n] = piece
            else:
                other = piece.T
                out_ref[n] = jnp.where(row < col, 0.0, piece) + jnp.where(row > col, 0.0, other)

    @pl.when(diag)
    def _():
        for r in range(2):
            block = mg + BLK * r
            fields[...] = rec_ref[r].T
            build_phi(fields, block * TB, False, spread, phi_hi, phi_lo)
            for ref in (phi_hi, phi_lo):
                ref[AUG:WIN, :] = jnp.zeros((WIN - AUG, PTS), jnp.bfloat16)
            gain = jnp.sum(parts_ref[r], axis=0)
            mass = jnp.zeros((WIN, WIN), jnp.float32)
            for k in range(QP):
                lanes = slice(TB * k, TB * (k + 1))
                left = phi_hi[:, lanes].astype(jnp.float32) + phi_lo[:, lanes].astype(jnp.float32)
                factor = fields[FW + k : FW + k + 1, :] * (MASS_SHIFT + gain[k : k + 1, :])
                high, low = split(left * factor)
                mass += (
                    nt(high, phi_hi[:, lanes]) + nt(low, phi_hi[:, lanes]) + nt(high, phi_lo[:, lanes])
                )
            x = x_ref[r]
            for n, (u, v) in enumerate(((0, 0), (1, 0), (1, 1))):
                one = x[TB * u : TB * (u + 1), TB * v : TB * (v + 1)]
                two = x[TB * v : TB * (v + 1), TB * u : TB * (u + 1)]
                whole = mass[TB * u : TB * (u + 1), TB * v : TB * (v + 1)] - one - two.T
                if u != v and r == 1:
                    flip = block == 15
                    whole = jnp.where(flip, 0.0, whole) + jnp.where(flip, whole.T, 0.0)
                out_ref[3 * r + n] = whole


def make_pieces(records, x, parts):
    vmem = pl.BlockSpec(memory_space=pltpu.VMEM)
    return pl.pallas_call(
        pieces_kernel,
        out_shape=jax.ShapeDtypeStruct((6, TB, TB), jnp.float32),
        in_specs=[vmem] * 3,
        out_specs=vmem,
        scratch_shapes=[
            pltpu.VMEM((TB, TB), jnp.float32),
            pltpu.VMEM((18, 16, TB), jnp.float32),
            pltpu.VMEM((WIN, PTS), jnp.bfloat16),
            pltpu.VMEM((WIN, PTS), jnp.bfloat16),
        ],
        compiler_params=pltpu.CompilerParams(vmem_limit_bytes=VMEM_LIMIT),
        name="make_pieces",
    )(records, x, parts)


def piece_target(n, hi, lo, diag, g):
    u, v = n // 2, n % 2
    row, col = (hi + u) % 16, (lo + v) % 16
    slot = jnp.where(row == col, 1, jnp.where(row > col, 2 * u + v, 2 * v + u))
    r, m = n // 3, n % 3
    block = g + BLK * r
    after = (block + 1) % 16
    drow = jnp.where(m == 0, block, jnp.where(m == 1, jnp.maximum(block, after), after))
    dcol = jnp.where(m == 0, block, jnp.where(m == 1, jnp.minimum(block, after), after))
    dslot = jnp.where(m == 0, 0, jnp.where(m == 1, jnp.where(block == 15, 1, 2), 3))
    big = jnp.where(diag, drow, jnp.maximum(row, col))
    small = jnp.where(diag, dcol, jnp.minimum(row, col))
    there = jnp.where(diag, 6, 4) > n
    return small % BLK, big, small // BLK, jnp.where(diag, dslot, slot), there


def piece_source(t, s, b, g):
    row, col = g, b + BLK * t
    there = jnp.logical_and(row >= col, jnp.logical_not(jnp.logical_and(row == col, s == 2)))
    sb, sg = pair_device((row - s // 2 + 16) % 16, (col - s % 2 + 16) % 16)
    return sb, sg, there


def reduce_kernel(piece_ref, out_ref, landed, send_sem, recv_sem):
    mb, mg = here()
    hi, lo, diag = own_pair(mb, mg)
    barrier = pltpu.get_barrier_semaphore()

    def say(n, carry):
        sb, sg, there = piece_source(n // 4, n % 4, mb, mg)

        @pl.when(jnp.logical_and(there, differs(sb, sg, mb, mg)))
        def _():
            greet(barrier, sb, sg)

        return carry

    lax.fori_loop(0, 8, say, 0)

    def count(n, total):
        b, g, t, s, there = piece_target(n, hi, lo, diag, mg)
        return total + jnp.where(jnp.logical_and(there, differs(b, g, mb, mg)), 1, 0)

    gather_greetings(barrier, lax.fori_loop(0, 6, count, 0))

    def copy(n):
        b, g, t, s, there = piece_target(n, hi, lo, diag, mg)
        return pltpu.make_async_remote_copy(
            src_ref=piece_ref.at[n],
            dst_ref=landed.at[t, s],
            send_sem=send_sem.at[n],
            recv_sem=recv_sem.at[t, s],
            device_id=(b, g),
            device_id_type=MESH,
        )

    def send(n, carry):
        b, g, t, s, there = piece_target(n, hi, lo, diag, mg)
        away = differs(b, g, mb, mg)

        @pl.when(jnp.logical_and(there, away))
        def _():
            copy(n).start()

        @pl.when(jnp.logical_and(there, jnp.logical_not(away)))
        def _():
            landed[t, s] = piece_ref[n]

        return carry

    lax.fori_loop(0, 6, send, 0)
    out_ref[...] = jnp.zeros_like(out_ref)

    def take(n, carry):
        t, s = n // 4, n % 4
        sb, sg, there = piece_source(t, s, mb, mg)

        @pl.when(there)
        def _():
            @pl.when(differs(sb, sg, mb, mg))
            def _():
                pltpu.make_async_remote_copy(
                    src_ref=piece_ref.at[0],
                    dst_ref=landed.at[t, s],
                    send_sem=send_sem.at[0],
                    recv_sem=recv_sem.at[t, s],
                    device_id=(sb, sg),
                    device_id_type=MESH,
                ).wait_recv()

            out_ref[t] += landed[t, s]

        return carry

    lax.fori_loop(0, 8, take, 0)

    def drain(n, carry):
        b, g, t, s, there = piece_target(n, hi, lo, diag, mg)

        @pl.when(jnp.logical_and(there, differs(b, g, mb, mg)))
        def _():
            copy(n).wait_send()

        return carry

    lax.fori_loop(0, 6, drain, 0)


def reduce_pieces(pieces):
    vmem = pl.BlockSpec(memory_space=pltpu.VMEM)
    return pl.pallas_call(
        reduce_kernel,
        out_shape=jax.ShapeDtypeStruct((2, TB, TB), jnp.float32),
        in_specs=[vmem],
        out_specs=vmem,
        scratch_shapes=[
            pltpu.VMEM((2, 4, TB, TB), jnp.float32),
            pltpu.SemaphoreType.DMA((6,)),
            pltpu.SemaphoreType.DMA((2, 4)),
        ],
        compiler_params=pltpu.CompilerParams(
            collective_id=2, has_side_effects=True, vmem_limit_bytes=VMEM_LIMIT
        ),
        name="sum_pieces",
    )(pieces)


def panel_kernel(tile_ref, out_ref, send_sem, recv_sem):
    mb, mg = here()
    barrier = pltpu.get_barrier_semaphore()
    first = mb == 0
    root = jnp.logical_and(first, mg == 0)
    relay = jnp.logical_and(mg >= 1, mb == mg % BLK)

    def wants(t):
        col = mb + BLK * t
        return jnp.logical_and(col >= 1, mg > col)

    @pl.when(jnp.logical_not(first))
    def _():
        greet(barrier, 0, mg)

    @pl.when(jnp.logical_and(first, mg > 0))
    def _():
        greet(barrier, 0, 0)

    for t in range(2):
        @pl.when(wants(t))
        def _(t=t):
            greet(barrier, mb, mb + BLK * t)

    expected = (
        jnp.where(first, BLK - 1, 0)
        + jnp.where(root, GRID - 1, 0)
        + jnp.where(relay, GRID - 1 - mg, 0)
    )
    gather_greetings(barrier, expected)

    def copy(source, n, sem, b, g):
        return pltpu.make_async_remote_copy(
            src_ref=source,
            dst_ref=out_ref.at[n],
            send_sem=send_sem.at[sem],
            recv_sem=recv_sem.at[n],
            device_id=(b, g),
            device_id_type=MESH,
        )

    @pl.when(root)
    def _():
        out_ref[0] = tile_ref[0]

    def root_send(g, carry):
        copy(tile_ref.at[0], 0, g, 0, g).start()
        return carry

    @pl.when(root)
    def _():
        lax.fori_loop(1, GRID, root_send, 0)

    @pl.when(first)
    def _():
        out_ref[1] = tile_ref[0]

        def row_send(b, carry):
            copy(tile_ref.at[0], 1, 16 + b, b, mg).start()
            return carry

        lax.fori_loop(1, BLK, row_send, 0)

    @pl.when(jnp.logical_not(first))
    def _():
        copy(tile_ref.at[0], 1, 0, mb, mg).wait_recv()

    def relay_copy(g):
        return copy(out_ref.at[1], 2 + mg // BLK, 40 + g, mb, g)

    @pl.when(relay)
    def _():
        def relay_send(g, carry):
            relay_copy(g).start()
            return carry

        lax.fori_loop(mg + 1, GRID, relay_send, 0)

    @pl.when(jnp.logical_not(root))
    def _():
        copy(tile_ref.at[0], 0, 0, mb, mg).wait_recv()

    @pl.when(first)
    def _():
        def head_send(b, carry):
            copy(out_ref.at[0], 0, 24 + b, b, mg).start()
            return carry

        lax.fori_loop(1, BLK, head_send, 0)

    for t in range(2):
        col = mb + BLK * t

        @pl.when(mg == col)
        def _(t=t):
            out_ref[2 + t] = out_ref[1]

        @pl.when(wants(t))
        def _(t=t):
            copy(tile_ref.at[0], 2 + t, 0, mb, mg).wait_recv()

        @pl.when(jnp.logical_not(jnp.logical_or(mg == col, wants(t))))
        def _(t=t):
            out_ref[2 + t] = jnp.zeros((TB, TB), jnp.float32)

    @pl.when(root)
    def _():
        def root_wait(g, carry):
            copy(tile_ref.at[0], 0, g, 0, g).wait_send()
            return carry

        lax.fori_loop(1, GRID, root_wait, 0)

    @pl.when(first)
    def _():
        def row_wait(b, carry):
            copy(tile_ref.at[0], 1, 16 + b, b, mg).wait_send()
            copy(out_ref.at[0], 0, 24 + b, b, mg).wait_send()
            return carry

        lax.fori_loop(1, BLK, row_wait, 0)

    @pl.when(relay)
    def _():
        def relay_wait(g, carry):
            relay_copy(g).wait_send()
            return carry

        lax.fori_loop(mg + 1, GRID, relay_wait, 0)


def share_panel(tiles):
    vmem = pl.BlockSpec(memory_space=pltpu.VMEM)
    return pl.pallas_call(
        panel_kernel,
        out_shape=jax.ShapeDtypeStruct((4, TB, TB), jnp.float32),
        in_specs=[vmem],
        out_specs=vmem,
        scratch_shapes=[pltpu.SemaphoreType.DMA((56,)), pltpu.SemaphoreType.DMA((4,))],
        compiler_params=pltpu.CompilerParams(
            collective_id=3, has_side_effects=True, vmem_limit_bytes=VMEM_LIMIT
        ),
        name="share_panel",
    )(tiles)


STEP = 16


def both(value):
    return jnp.concatenate([value, value], axis=1)


def eliminate(work):
    at = lax.broadcasted_iota(jnp.int32, (8, WIN), 0)
    for top in range(0, TB, STEP):
        rows = [jnp.broadcast_to(work[top + i : top + i + 1, :], (8, WIN)) for i in range(STEP)]
        entry = {
            (i, j): jnp.broadcast_to(rows[i][:, top + j : top + j + 1], (8, TB))
            for i in range(STEP)
            for j in range(i + 1)
        }
        for j in range(STEP):
            scale = lax.rsqrt(entry[j, j])
            for i in range(j + 1, STEP):
                entry[i, j] = entry[i, j] * scale
            for i in range(j + 1, STEP):
                for k in range(j + 1, i + 1):
                    entry[i, k] = entry[i, k] - entry[i, j] * entry[k, j]
            rows[j] = rows[j] * both(scale)
            for i in range(j + 1, STEP):
                rows[i] = rows[i] - both(entry[i, j]) * rows[j]
        groups = []
        for g in range(0, STEP, 8):
            group = rows[g]
            for i in range(1, 8):
                group = jnp.where(at == i, rows[g + i], group)
            groups.append(group)
        panel = jnp.concatenate(groups, axis=0)
        work[top : top + STEP, :] = panel
        after = top + STEP
        if after < TB:
            high, low = split(panel)
            left = jnp.concatenate([high, high, low], axis=0)
            right = jnp.concatenate([high, low, high], axis=0)
            for lo, up in ((after, after + STEP), (after + STEP, TB)):
                if lo < up:
                    work[lo:up, :] -= lax.dot_general(
                        left[:, lo:up],
                        right,
                        (((0,), (0,)), ((), ())),
                        preferred_element_type=jnp.float32,
                    )


def nt3(a, b):
    (a_hi, a_lo), (b_hi, b_lo) = split(a), split(b)
    return nt(a_hi, b_hi) + (nt(a_lo, b_hi) + nt(a_hi, b_lo))


def factor_kernel(panel_ref, tile_ref, out_ref, work):
    mb, mg = here()
    head = panel_ref[0]
    row = lax.broadcasted_iota(jnp.int32, (TB, TB), 0)
    col = lax.broadcasted_iota(jnp.int32, (TB, TB), 1)
    work[:, 0:TB] = 0.5 * (head + head.T)
    work[:, TB:WIN] = jnp.where(row == col, 1.0, 0.0)
    eliminate(work)
    lower = jnp.where(row >= col, work[:, 0:TB].T, 0.0)
    inverse = jnp.where(row >= col, work[:, TB:WIN], 0.0)
    solved = nt3(panel_ref[1:4].reshape(3 * TB, TB), inverse)
    left = jnp.where(mg == 0, lower, solved[0:TB])
    update = nt3(left, solved[TB : 3 * TB])
    for t in range(2):
        tile_col = mb + BLK * t
        value = jnp.where(tile_col == 0, left, tile_ref[t] - update[:, TB * t : TB * (t + 1)])
        keep = mg * TB + row >= tile_col * TB + col
        out_ref[0, :, t, :] = jnp.where(keep, value, 0.0)


def factor(panel, tiles):
    vmem = pl.BlockSpec(memory_space=pltpu.VMEM)
    return pl.pallas_call(
        factor_kernel,
        out_shape=jax.ShapeDtypeStruct((1, TB, 2, TB), jnp.float32),
        in_specs=[vmem] * 2,
        out_specs=vmem,
        scratch_shapes=[pltpu.VMEM((TB, WIN), jnp.float32)],
        compiler_params=pltpu.CompilerParams(vmem_limit_bytes=VMEM_LIMIT),
        name="factor_tiles",
    )(panel, tiles)


def shards(conn, extract, points):
    records, x, total = gather_pair(conn, extract, points)
    parts = totals_exchange(total)
    pieces = make_pieces(records, x, parts)
    tiles = reduce_pieces(pieces)
    panel = share_panel(tiles)
    return factor(panel, tiles)


def solution(mesh):
    in_specs = (
        P(("blk", "grid"), None),
        P(None, None, ("blk", "grid")),
        P(None, None, ("blk", "grid")),
    )
    out_specs = P(None, "grid", None, "blk")
    return jax.shard_map(shards, mesh=mesh, in_specs=in_specs, out_specs=out_specs, check_vma=False)
```

```python
import functools
import math

import jax
import jax.numpy as jnp
import numpy as np
from jax import lax
from jax.experimental import pallas as pl
from jax.experimental.pallas import tpu as pltpu
from jax.sharding import PartitionSpec as P

M = 2048
EX = 64
EY = 32
QP = 9
TB = 128
BLK = 8
GRID = 16
PTS = QP * TB
WIN = 256
AUG = 192

KERNEL_GAIN = 0.02
MASS_SHIFT = 0.05

FX, FY, FW, FV, FC = 0, 9, 18, 27, 108

MESH = pl.DeviceIdType.MESH
VMEM_LIMIT = 48 * 1024 * 1024
EXACT = lax.Precision.HIGHEST


def bernstein_table():
    spread_root = 0.5 * math.sqrt(0.6)
    nodes = [0.5 - spread_root, 0.5, 0.5 + spread_root]
    poly = [[(1.0 - t) ** 2, 2.0 * t * (1.0 - t), t * t] for t in nodes]
    return np.array(
        [
            [poly[i][a] * poly[j][b] for a in range(3) for b in range(3)]
            for i in range(3)
            for j in range(3)
        ],
        np.float32,
    )


def bernstein_lanes():
    table = np.zeros((16, TB), np.float32)
    table[:QP, :QP] = bernstein_table()
    return table


def column_device(column, place):
    return column // 2, 8 * (column % 2) + place


def differs(b, g, mb, mg):
    return jnp.logical_or(b != mb, g != mg)


def remote(src, dst, send_sem, recv_sem, b, g):
    return pltpu.make_async_remote_copy(
        src_ref=src,
        dst_ref=dst,
        send_sem=send_sem,
        recv_sem=recv_sem,
        device_id=(b, g),
        device_id_type=MESH,
    )


def others(b, g):
    return [(b, (g + n) % GRID) for n in range(1, GRID)] + [((b + n) % BLK, g) for n in range(1, BLK)]


def when(condition):
    return pl.when(condition)


def split(value):
    high = value.astype(jnp.bfloat16)
    return high, (value - high.astype(jnp.float32)).astype(jnp.bfloat16)


def build_phi(fields, start, weigh, spread, high_ref, low_ref):
    lane = lax.broadcasted_iota(jnp.int32, (QP, TB), 1)
    cell_y = lane % EY
    cell_x = lane // EY
    target = fields[FC : FC + QP, :].astype(jnp.int32) - start
    target = jnp.where(target < 0, target + M, target)
    place = 3 * (target // EY - cell_x) + (target % EY - cell_y + EY) % EY
    weight = fields[FW : FW + QP, :]
    slots = [jnp.zeros((QP, TB), jnp.float32) for _ in range(QP)]
    for a in range(QP):
        value = fields[FV + QP * a : FV + QP * (a + 1), :]
        if weigh:
            value = value * weight
        here_a = jnp.broadcast_to(place[a : a + 1, :], (QP, TB))
        for n in range(QP):
            slots[n] = jnp.where(here_a == n, value, slots[n])
    for jx in range(6):
        for t in range(3):
            row = jnp.zeros((QP, TB), jnp.float32)
            for step in range(3):
                if 0 <= jx - step <= 3:
                    row = jnp.where(cell_x == jx - step, slots[3 * step + t], row)
            spread[3 * jx + t, 0:QP, :] = row
    rows = EY
    wide_y = lax.broadcasted_iota(jnp.int32, (rows, TB), 1) % EY
    down_y = lax.broadcasted_iota(jnp.int32, (rows, TB), 0)
    hits = [(wide_y + t) % EY == down_y for t in range(3)]
    for jx in range(6):
        for k in range(QP):
            value = jnp.zeros((rows, TB), jnp.float32)
            for t in range(3):
                line = jnp.broadcast_to(spread[3 * jx + t, k : k + 1, :], (rows, TB))
                value = jnp.where(hits[t], line, value)
            high, low = split(value)
            high_ref[rows * jx : rows * (jx + 1), TB * k : TB * (k + 1)] = high
            low_ref[rows * jx : rows * (jx + 1), TB * k : TB * (k + 1)] = low


def nt(a, b):
    return lax.dot_general(a, b, (((1,), (1,)), ((), ())), preferred_element_type=jnp.float32)


def nn(a, b):
    return lax.dot_general(a, b, (((1,), (0,)), ((), ())), preferred_element_type=jnp.float32)


STEP = 16


def both(value):
    return jnp.concatenate([value, value], axis=1)


def eliminate(work):
    at = lax.broadcasted_iota(jnp.int32, (8, WIN), 0)
    for top in range(0, TB, STEP):
        rows = [jnp.broadcast_to(work[top + i : top + i + 1, :], (8, WIN)) for i in range(STEP)]
        entry = {
            (i, j): jnp.broadcast_to(rows[i][:, top + j : top + j + 1], (8, TB))
            for i in range(STEP)
            for j in range(i + 1)
        }
        for j in range(STEP):
            scale = lax.rsqrt(entry[j, j])
            for i in range(j + 1, STEP):
                entry[i, j] = entry[i, j] * scale
            for i in range(j + 1, STEP):
                for k in range(j + 1, i + 1):
                    entry[i, k] = entry[i, k] - entry[i, j] * entry[k, j]
            rows[j] = rows[j] * both(scale)
            for i in range(j + 1, STEP):
                rows[i] = rows[i] - both(entry[i, j]) * rows[j]
        groups = []
        for g in range(0, STEP, 8):
            group = rows[g]
            for i in range(1, 8):
                group = jnp.where(at == i, rows[g + i], group)
            groups.append(group)
        panel = jnp.concatenate(groups, axis=0)
        work[top : top + STEP, :] = panel
        after = top + STEP
        if after < TB:
            high, low = split(panel)
            left = jnp.concatenate([high, high, low], axis=0)
            right = jnp.concatenate([high, low, high], axis=0)
            for lo, up in ((after, after + STEP), (after + STEP, TB)):
                if lo < up:
                    work[lo:up, :] -= lax.dot_general(
                        left[:, lo:up],
                        right,
                        (((0,), (0,)), ((), ())),
                        preferred_element_type=jnp.float32,
                    )


def nt3(a, b):
    (a_hi, a_lo), (b_hi, b_lo) = split(a), split(b)
    return nt(a_hi, b_hi) + (nt(a_lo, b_hi) + nt(a_hi, b_lo))


HALF_X = float(EX) / 4.0
HALF_Y = float(EY) / 4.0


def make_record(bern, conn, extract, points, raw):
    raw[...] = jnp.zeros_like(raw)
    for c in range(3):
        raw[QP * c : QP * (c + 1), 0:16] = points[:, c, :]
    for a in range(QP):
        value = jnp.zeros((QP, 16), jnp.float32)
        for n in range(QP):
            value = value + bern[0:QP, n : n + 1] * extract[a, n : n + 1, :]
        raw[FV + QP * a : FV + QP * (a + 1), 0:16] = value
    raw[FC : FC + QP, 0:16] = conn[...].astype(jnp.float32).T
    return raw[...].T[0:16, :]


def set_up_block(slot, block, shift, rec, fields, spread, phi_hi, phi_lo, trial_x, trial_y):
    cell_y = lax.broadcasted_iota(jnp.int32, (QP, TB), 1) % EY
    first = lax.broadcasted_iota(jnp.int32, (16, TB), 0) == 0
    view = fields.at[slot]
    view[...] = rec[slot].T
    build_phi(view, block * TB, True, spread, phi_hi.at[slot], phi_lo.at[slot])
    for ref in (phi_hi, phi_lo):
        ref[slot, AUG:WIN, :] = jnp.zeros((WIN - AUG, PTS), jnp.bfloat16)
    for k in range(QP):
        weight = jnp.broadcast_to(view[FW + k : FW + k + 1, :], (16, TB))
        high, low = split(jnp.where(first, weight, 0.0))
        phi_hi[slot, AUG : AUG + 16, TB * k : TB * (k + 1)] = high
        phi_lo[slot, AUG : AUG + 16, TB * k : TB * (k + 1)] = low
    trial_x[slot, 0:QP, :] = view[FX : FX + QP, :] * (EX / 2.0) + shift
    for quarter in range(4):
        turn = jnp.where(cell_y > 8 * quarter + 8, -HALF_Y, HALF_Y)
        trial_y[slot, quarter, 0:QP, :] = view[FY : FY + QP, :] * (EX / 2.0) + turn


def kernel_chunk(i, j, q_slot, trial_x, trial_y, splat, kern):
    qx = jnp.broadcast_to(trial_x[q_slot, pl.ds(j, 1), :], (8, TB))
    qy = [jnp.broadcast_to(trial_y[q_slot, quarter, pl.ds(j, 1), :], (8, TB)) for quarter in range(4)]
    sums = jnp.zeros((8, TB), jnp.float32)
    for h in range(8):
        values = []
        for n in (2 * h, 2 * h + 1):
            rows = slice(8 * n, 8 * n + 8)
            gap_x = HALF_X - jnp.abs(qx - splat[0, rows, :])
            gap_y = HALF_Y - jnp.abs(splat[1, rows, :] - qy[n % 4])
            root = lax.rsqrt(1.0 + (gap_x * gap_x + gap_y * gap_y))
            square = root * root
            value = square * square * lax.rsqrt(root)
            sums = sums + value * splat[2, rows, :]
            values.append(value)
        kern[TB * i + 16 * h : TB * i + 16 * h + 16, pl.ds(pl.multiple_of(j * TB, TB), TB)] = (
            jnp.concatenate(values, axis=0).astype(jnp.bfloat16)
        )
    return jnp.sum(sums, axis=0, keepdims=True)


def below(value):
    return jnp.concatenate([value, jnp.zeros((TB - 64, TB), jnp.float32)], axis=0)


def stiffness_kernel(
    bern_in, conn_in, extract_in, points_in, out_ref,
    bern, conn, extract, points, raw, rec, fields, spread, phi_hi, phi_lo, trial_x, trial_y, splat, kern, pot,
    col_sum, totals, parts, xs, stage_big, stage_small, land_big, land_small, tiles, head, row_tile, col_tile, work,
    in_sem, rec_send, rec_recv, total_send, total_recv, piece_send, big_recv, small_recv,
    head_send, head_recv, row_send, row_recv, col_send, col_recv, ready,
):
    mb, mg = lax.axis_index("blk"), lax.axis_index("grid")
    own = 2 * mb + mg // 8
    place = mg % 8
    core = mg % 2
    chip = mg // 2
    last = place == 7
    partner = mg + 1 - 2 * core
    barrier = pltpu.get_barrier_semaphore()

    fetch = [
        pltpu.make_async_copy(src, dst, in_sem.at[n])
        for n, (src, dst) in enumerate(
            ((bern_in, bern), (extract_in, extract), (points_in, points), (conn_in, conn))
        )
    ]
    for copy in fetch:
        copy.start()
    row_tile[...] = jnp.zeros_like(row_tile)
    col_tile[...] = jnp.zeros_like(col_tile)
    for b, g in others(mb, mg):
        pl.semaphore_signal(barrier, inc=1, device_id=(b, g), device_id_type=MESH)
    for copy in fetch:
        copy.wait()
    mine = pl.ds(pl.multiple_of(16 * place, 16), 16)
    rec[0, mine, :] = make_record(bern, conn, extract, points, raw)
    pl.semaphore_wait(barrier, GRID - 1 + BLK - 1)
    for n in range(1, BLK):
        pl.semaphore_signal(ready, inc=1, device_id=((mb + n) % BLK, mg), device_id_type=MESH)

    base = 8 * (mg // 8)
    z = place // 2

    def record_copy(from_z, from_core, n, g):
        at = 2 * from_z + from_core
        view = rec.at[0, pl.ds(16 * at, 16), :]
        return remote(view, view, rec_send.at[n], rec_recv.at[at], mb, g)

    record_copy(z, core, 0, partner).start()
    for n in range(1, 4):
        record_copy(z, core, n, base + 2 * ((z + n) % 4) + core).start()
    for n in range(1, 4):
        from_z = (z + 4 - n) % 4
        record_copy(from_z, core, 0, mg).wait_recv()
        record_copy(from_z, core, 3 + n, partner).start()
    for n in range(4):
        record_copy((z + 4 - n) % 4, 1 - core, 0, mg).wait_recv()
    pl.semaphore_wait(ready, BLK - 1)
    to_b, to_g = column_device((own + 15 - place) % 16, place)
    block_copy = remote(rec.at[0], rec.at[1], rec_send.at[7], rec_recv.at[8], to_b, to_g)
    block_copy.start()

    other = (own + 1 + place) % 16
    set_up_block(0, own, -HALF_X, rec, fields, spread, phi_hi, phi_lo, trial_x, trial_y)
    block_copy.wait_recv()
    wrapped = jnp.where(other < own, HALF_X, -HALF_X)
    set_up_block(1, other, wrapped, rec, fields, spread, phi_hi, phi_lo, trial_x, trial_y)

    lower = own < 8

    def evaluate(i, low, high, q_slot):
        def part(j, carry):
            col_sum[pl.ds(j, 1), :] += kernel_chunk(i, j, q_slot, trial_x, trial_y, splat, kern)
            return carry

        steps = high - low
        lax.fori_loop(low, high, part, 0, unroll=3 if steps % 3 == 0 else 2 if steps % 2 == 0 else 1)

    def run(r):
        q_slot = 1 - r
        col_sum[...] = jnp.zeros_like(col_sum)
        if r == 0:
            @when(jnp.logical_and(last, lower))
            def _():
                kern[5 * TB : PTS, :] = jnp.zeros((4 * TB, PTS), jnp.bfloat16)

            @when(jnp.logical_and(last, jnp.logical_not(lower)))
            def _():
                kern[:, 0 : 5 * TB] = jnp.zeros((PTS, 5 * TB), jnp.bfloat16)

        for i in range(QP):
            for n, field in ((0, FX), (1, FY), (2, FW)):
                picked = rec[0, :, field + i : field + i + 1] * (EX / 2.0 if n < 2 else KERNEL_GAIN)
                splat[n] = jnp.broadcast_to(picked, (TB, TB))
            if r == 1:
                at = slice(TB * i, TB * (i + 1))
                if i > 0:
                    kern[at, 0 : TB * i] = jnp.zeros((TB, TB * i), jnp.bfloat16)
                col_sum[i : i + 1, :] += 0.5 * kernel_chunk(i, i, q_slot, trial_x, trial_y, splat, kern)
                kern[at, at] = kern[at, at] * 0.5
                if i + 1 < QP:
                    evaluate(i, i + 1, QP, q_slot)
                continue
            whole = jnp.logical_not(last)
            if i < 5:
                whole = jnp.logical_or(whole, lower)

            @when(whole)
            def _(i=i):
                evaluate(i, 0, QP, q_slot)

            @when(jnp.logical_and(last, jnp.logical_not(lower)))
            def _(i=i):
                evaluate(i, 5, QP, q_slot)

        pot[...] = nt(kern[...], phi_hi[q_slot]) + nt(kern[...], phi_lo[q_slot])

        columns = [
            pot[TB * i : TB * (i + 1), TB:WIN].T[AUG - TB : AUG - TB + 1, :] * KERNEL_GAIN for i in range(QP)
        ]
        if r == 0:
            totals[1, 0:QP, :] = col_sum[0:QP, :]
            for i in range(QP):
                totals[0, i : i + 1, :] = columns[i]
            total_copy(1).start()

            @when(jnp.logical_not(last))
            def _():
                total_copy(0).start()
        else:
            for i in range(QP):
                parts[7, i : i + 1, :] = totals[0, i : i + 1, :] + col_sum[i : i + 1, :] + columns[i]

        high, low = split(pot[...])
        inside = jnp.logical_and(
            lax.broadcasted_iota(jnp.int32, (WIN, WIN), 0) < AUG,
            lax.broadcasted_iota(jnp.int32, (WIN, WIN), 1) < AUG,
        )
        value = nn(phi_hi[0], high) + nn(phi_lo[0], high) + nn(phi_hi[0], low)
        xs[...] = jnp.where(inside, -KERNEL_GAIN * value, 0.0)
        if r == 0:
            pair_pieces()

    def total_copy(n):
        b, g = column_device(other if n == 1 else own, 7)
        slot = 8 + place if n == 1 else place
        return remote(totals.at[n], parts.at[slot], total_send.at[n], total_recv.at[slot], b, g)

    def target(n):
        if n < 4:
            u, v = (0, 1, 0, 1)[n], (0, 0, 1, 1)[n]
            row, col = (own + u) % 16, (other + v) % 16
            slot = {0: 0, 1: jnp.where(row < col, 1, 2), 2: jnp.where(row < col, 2, 1), 3: 3}[n]
            half = jnp.where(jnp.logical_and(last, own >= 8), 1, 0)
        else:
            after = (own + 1) % 16
            row, col = (own, after, after)[n - 4], (own, own, after)[n - 4]
            slot = {4: 0, 5: jnp.where(own == 15, 1, 2), 6: 3}[n]
            half = 0
        big, small = jnp.maximum(row, col), jnp.minimum(row, col)
        return small % BLK, big, small // BLK, slot, half, row < col

    STAGE = {0: 0, 4: 1, 1: 0, 2: 1, 3: 2, 5: 3, 6: 4}

    def piece_copy(n):
        b, g, t, slot, half, flip = target(n)
        if n in (0, 4):
            return stage_big.at[STAGE[n]], land_big.at[t, half], big_recv.at[t, half], b, g
        return stage_small.at[STAGE[n]], land_small.at[t, slot - 1, half], small_recv.at[t, slot - 1, half], b, g

    def send_piece(n):
        src, dst, sem, b, g = piece_copy(n)

        @when(differs(b, g, mb, mg))
        def _():
            remote(src, dst, piece_send.at[n], sem, b, g).start()

        @when(jnp.logical_not(differs(b, g, mb, mg)))
        def _():
            pltpu.make_async_copy(src, dst, piece_send.at[n]).start()

    def drain_piece(n):
        src, dst, sem, b, g = piece_copy(n)

        @when(differs(b, g, mb, mg))
        def _():
            remote(src, dst, piece_send.at[n], sem, b, g).wait_send()

    def settle_piece(n):
        src, dst, sem, b, g = piece_copy(n)

        @when(jnp.logical_not(differs(b, g, mb, mg)))
        def _():
            pltpu.make_async_copy(src, dst, piece_send.at[n]).wait()

    def pair_pieces():
        corner, side = slice(0, TB), slice(TB, TB + 64)
        flip0 = target(0)[5]
        flip3 = target(3)[5]

        @when(flip0)
        def _():
            stage_big[0] = xs[corner, corner].T

        @when(jnp.logical_not(flip0))
        def _():
            stage_big[0] = xs[corner, corner]

        send_piece(0)
        stage_small[0] = xs[side, corner]
        send_piece(1)
        stage_small[1] = xs[corner, TB:WIN].T[0:64, :]
        send_piece(2)

        @when(flip3)
        def _():
            stage_small[2] = xs[TB:WIN, TB:WIN].T[0:64, :]

        @when(jnp.logical_not(flip3))
        def _():
            stage_small[2] = xs[side, TB:WIN]

        send_piece(3)

    run(0)

    @when(last)
    def _():
        run(1)
        build_phi(fields.at[0], own * TB, False, spread, phi_hi.at[1], phi_lo.at[1])
        for ref in (phi_hi, phi_lo):
            ref[1, AUG:WIN, :] = jnp.zeros((WIN - AUG, PTS), jnp.bfloat16)
        for n in range(16):
            if n != 7:
                remote(totals.at[0], parts.at[n], total_send.at[0], total_recv.at[n], mb, mg).wait_recv()
        gain = parts[0]
        for n in range(1, 16):
            gain = gain + parts[n]
        mass = xs[...] + xs[...].T
        for k in range(QP):
            lanes = slice(TB * k, TB * (k + 1))
            left = phi_hi[1, :, lanes].astype(jnp.float32) + phi_lo[1, :, lanes].astype(jnp.float32)
            factor = fields[0, FW + k : FW + k + 1, :] * (MASS_SHIFT + gain[k : k + 1, :])
            high, low = split(left * factor)
            mass += nt(high, phi_hi[1, :, lanes]) + nt(low, phi_hi[1, :, lanes]) + nt(high, phi_lo[1, :, lanes])
        stage_big[1] = mass[0:TB, 0:TB]
        send_piece(4)
        stage_small[3] = mass[TB : TB + 64, 0:TB]
        send_piece(5)
        stage_small[4] = mass[TB : TB + 64, TB:WIN]
        send_piece(6)

    for n in range(4):
        settle_piece(n)

    @when(last)
    def _():
        for n in range(4, 7):
            settle_piece(n)

    for t in range(2):
        tile_col = mb + BLK * t
        owned = mg >= tile_col
        square = mg == tile_col
        tiles[t] = jnp.zeros((TB, TB), jnp.float32)
        for slot in range(4):
            first, second = (mg - slot // 2 + 16) % 16, (tile_col - slot % 2 + 16) % 16
            ahead = (first - second + 16) % 16
            skip = jnp.logical_and(square, slot == 1)
            for half in range(2):
                host = jnp.where(ahead < 8, second, first)
                step = jnp.where(ahead == 0, 7, jnp.where(ahead < 8, ahead - 1, 15 - ahead))
                if half == 0:
                    host = jnp.where(ahead == 8, jnp.minimum(first, second), host)
                    there = jnp.logical_and(owned, jnp.logical_not(skip))
                else:
                    host = jnp.maximum(first, second)
                    there = jnp.logical_and(owned, ahead == 8)
                from_b, from_g = column_device(host, step)
                if slot == 0:
                    src, dst, sem = stage_big.at[0], land_big.at[t, half], big_recv.at[t, half]
                else:
                    src = stage_small.at[0]
                    dst, sem = land_small.at[t, slot - 1, half], small_recv.at[t, slot - 1, half]

                @when(there)
                def _(src=src, dst=dst, sem=sem, t=t, slot=slot, square=square, from_b=from_b, from_g=from_g):
                    @when(differs(from_b, from_g, mb, mg))
                    def _():
                        remote(src, dst, piece_send.at[0], sem, mb, mg).wait_recv()

                    if slot == 0:
                        tiles[t] += dst[...]
                    elif slot == 1:
                        tiles[t] += below(dst[...]).T
                    elif slot == 3:
                        tiles[t, 0:64, :] += dst[...]
                    else:
                        tiles[t, 0:64, :] += dst[...]

                        @when(square)
                        def _():
                            tiles[t] += below(dst[...]).T

    first = mb == 0
    upper_half = core == 0
    half_rows = pl.ds(pl.multiple_of(64 * core, 64), 64)
    other_rows = pl.ds(pl.multiple_of(64 * (1 - core), 64), 64)
    active = mb <= 2 * chip + 1
    relay = jnp.logical_and(mg >= 1, mb == mg % BLK)
    special = jnp.logical_and(first, mg % BLK != 0)

    def row_copy(n, b):
        return remote(tiles.at[0], row_tile, row_send.at[n], row_recv, b, mg)

    @when(special)
    def _():
        row_copy(0, mg % BLK).start()

    def head_half(n, b, g, rows):
        return remote(head.at[rows, :], head.at[rows, :], head_send.at[n], head_recv.at[0], b, g)

    def head_swap(rows, g):
        return remote(head.at[rows, :], head.at[rows, :], head_send.at[15], head_recv.at[1], mb, g)

    root = jnp.logical_and(first, mg == 0)
    root_pair = jnp.logical_and(first, chip == 0)
    whole_head = remote(head, head, head_send.at[16], head_recv.at[2], mb, partner)

    @when(root)
    def _():
        head[...] = tiles[0]
        whole_head.start()

    @when(jnp.logical_and(root_pair, mg == 1))
    def _():
        whole_head.wait_recv()

    @when(root_pair)
    def _():
        for n in range(1, 8):
            head_half(n, 0, 2 * n + core, half_rows).start()

    @when(jnp.logical_and(first, mg == 8))
    def _():
        row_tile[...] = tiles[0]

    def relay_copy(n):
        return remote(row_tile, col_tile.at[mg // BLK], col_send.at[n], col_recv.at[mg // BLK], mb, 2 * n + core)

    relay_partner = remote(
        row_tile, col_tile.at[mg // BLK], col_send.at[8], col_recv.at[mg // BLK], mb, partner
    )
    with_partner = jnp.logical_and(relay, core == 0)

    @when(jnp.logical_and(relay, jnp.logical_not(first)))
    def _():
        row_copy(0, mb).wait_recv()

    for n in range(1, 8):
        @when(jnp.logical_and(relay, chip < n))
        def _(n=n):
            relay_copy(n).start()

    @when(with_partner)
    def _():
        relay_partner.start()

    @when(jnp.logical_and(active, jnp.logical_not(root_pair)))
    def _():
        head_half(0, mb, mg, half_rows).wait_recv()

    for n in range(1, 8):
        @when(jnp.logical_and(first, n <= 2 * chip + 1))
        def _(n=n):
            head_half(7 + n, n, mg, half_rows).start()

    swaps = jnp.logical_and(active, jnp.logical_not(root_pair))

    @when(swaps)
    def _():
        head_swap(half_rows, partner).start()

    for n in range(1, 8):
        @when(jnp.logical_and(first, jnp.logical_and(n <= mg, n != mg % BLK)))
        def _(n=n):
            row_copy(n, n).start()

    @when(swaps)
    def _():
        head_swap(other_rows, partner).wait_recv()

    def forward(t):
        return remote(col_tile.at[t], col_tile.at[t], col_send.at[9 + t], col_recv.at[t], mb, partner)

    for t in range(2):
        tile_col = mb + BLK * t
        wants = jnp.logical_and(tile_col >= 1, mg > tile_col)

        @when(wants)
        def _(t=t, tile_col=tile_col):
            forward(t).wait_recv()

            @when(core == tile_col % 2)
            def _():
                forward(t).start()

    needs_row = jnp.logical_and(jnp.logical_not(first), jnp.logical_and(mb <= mg, jnp.logical_not(relay)))

    row = lax.broadcasted_iota(jnp.int32, (TB, TB), 0)
    col = lax.broadcasted_iota(jnp.int32, (TB, TB), 1)
    busy = mg >= mb

    @when(busy)
    def _():
        work[:, 0:TB] = 0.5 * (head[...] + head[...].T)
        work[:, TB:WIN] = jnp.where(row == col, 1.0, 0.0)
        eliminate(work)

        @when(needs_row)
        def _():
            row_copy(0, mb).wait_recv()

        lower = jnp.where(row >= col, work[:, 0:TB].T, 0.0)
        inverse = jnp.where(row >= col, work[:, TB:WIN], 0.0)
        row_value = jnp.where(first, tiles[0], row_tile[...])
        columns = [jnp.where(mg == mb + BLK * t, row_value, col_tile[t]) for t in range(2)]
        solved = nt3(jnp.concatenate([row_value] + columns, axis=0), inverse)
        left = jnp.where(mg == 0, lower, solved[0:TB])
        update = nt3(left, solved[TB : 3 * TB])
        for t in range(2):
            tile_col = mb + BLK * t
            value = jnp.where(tile_col == 0, left, tiles[t] - update[:, TB * t : TB * (t + 1)])
            keep = mg * TB + row >= tile_col * TB + col
            out_ref[0, :, t, :] = jnp.where(keep, value, 0.0)

    @when(jnp.logical_not(busy))
    def _():
        out_ref[...] = jnp.zeros_like(out_ref)

    record_copy(z, core, 0, partner).wait_send()
    for n in range(1, 4):
        record_copy(z, core, n, partner).wait_send()
        record_copy(z, core, 3 + n, partner).wait_send()
    block_copy.wait_send()
    total_copy(1).wait_send()

    @when(jnp.logical_not(last))
    def _():
        total_copy(0).wait_send()

    for n in range(4):
        drain_piece(n)

    @when(last)
    def _():
        for n in range(4, 7):
            drain_piece(n)

    @when(special)
    def _():
        row_copy(0, mg % BLK).wait_send()

    @when(root)
    def _():
        whole_head.wait_send()

    @when(root_pair)
    def _():
        for n in range(1, 8):
            head_half(n, 0, mg, half_rows).wait_send()

    @when(swaps)
    def _():
        head_swap(half_rows, partner).wait_send()

    for n in range(1, 8):
        @when(jnp.logical_and(relay, chip < n))
        def _(n=n):
            relay_copy(n).wait_send()

        @when(jnp.logical_and(first, n <= 2 * chip + 1))
        def _(n=n):
            head_half(7 + n, n, mg, half_rows).wait_send()

        @when(jnp.logical_and(first, jnp.logical_and(n <= mg, n != mg % BLK)))
        def _(n=n):
            row_copy(n, n).wait_send()

    @when(with_partner)
    def _():
        relay_partner.wait_send()

    for t in range(2):
        tile_col = mb + BLK * t
        wants = jnp.logical_and(tile_col >= 1, mg > tile_col)

        @when(jnp.logical_and(wants, core == tile_col % 2))
        def _(t=t):
            forward(t).wait_send()


def shards(conn, extract, points):
    f32, bf16 = jnp.float32, jnp.bfloat16
    vmem = lambda dtype, *shape: pltpu.VMEM(shape, dtype)
    dma = pltpu.SemaphoreType.DMA
    anywhere = pl.BlockSpec(memory_space=pl.ANY)
    return pl.pallas_call(
        stiffness_kernel,
        out_shape=jax.ShapeDtypeStruct((1, TB, 2, TB), f32),
        in_specs=[anywhere] * 4,
        out_specs=pl.BlockSpec(memory_space=pltpu.VMEM),
        scratch_shapes=[
            vmem(f32, 16, TB),
            vmem(jnp.int32, 16, QP),
            vmem(f32, QP, QP, 16),
            vmem(f32, QP, 3, 16),
            vmem(f32, TB, TB),
            vmem(f32, 2, TB, TB),
            vmem(f32, 2, TB, TB),
            vmem(f32, 18, 16, TB),
            vmem(bf16, 2, WIN, PTS),
            vmem(bf16, 2, WIN, PTS),
            vmem(f32, 2, 16, TB),
            vmem(f32, 2, 4, 16, TB),
            vmem(f32, 3, TB, TB),
            vmem(bf16, PTS, PTS),
            vmem(f32, PTS, WIN),
            vmem(f32, 16, TB),
            vmem(f32, 2, 16, TB),
            vmem(f32, 16, 16, TB),
            vmem(f32, WIN, WIN),
            vmem(f32, 2, TB, TB),
            vmem(f32, 5, 64, TB),
            vmem(f32, 2, 2, TB, TB),
            vmem(f32, 2, 3, 2, 64, TB),
            vmem(f32, 2, TB, TB),
            vmem(f32, TB, TB),
            vmem(f32, TB, TB),
            vmem(f32, 2, TB, TB),
            vmem(f32, TB, WIN),
            dma((4,)),
            dma((8,)),
            dma((9,)),
            dma((2,)),
            dma((16,)),
            dma((7,)),
            dma((2, 2)),
            dma((2, 3, 2)),
            dma((17,)),
            dma((3,)),
            dma((8,)),
            dma,
            dma((11,)),
            dma((2,)),
            pltpu.SemaphoreType.REGULAR,
        ],
        compiler_params=pltpu.CompilerParams(
            collective_id=0, has_side_effects=True, vmem_limit_bytes=VMEM_LIMIT
        ),
        name="stiffness",
    )(jnp.asarray(bernstein_lanes()), conn, extract, points.transpose(1, 0, 2))


def solution(mesh):
    in_specs = (
        P(("blk", "grid"), None),
        P(None, None, ("blk", "grid")),
        P(None, None, ("blk", "grid")),
    )
    out_specs = P(None, "grid", None, "blk")
    return jax.shard_map(shards, mesh=mesh, in_specs=in_specs, out_specs=out_specs, check_vma=False)
```

```python
import functools
import math

import jax
import jax.numpy as jnp
import numpy as np
from jax import lax
from jax.experimental import pallas as pl
from jax.experimental.pallas import tpu as pltpu
from jax.sharding import PartitionSpec as P

M = 2048
EX = 64
EY = 32
QP = 9
TB = 128
BLK = 8
GRID = 16
PTS = QP * TB
WIN = 256
AUG = 192

KERNEL_GAIN = 0.02
MASS_SHIFT = 0.05

FX, FY, FW, FV, FC = 0, 9, 18, 27, 108

MESH = pl.DeviceIdType.MESH
VMEM_LIMIT = 60 * 1024 * 1024
EXACT = lax.Precision.HIGHEST


def bernstein_table():
    spread_root = 0.5 * math.sqrt(0.6)
    nodes = [0.5 - spread_root, 0.5, 0.5 + spread_root]
    poly = [[(1.0 - t) ** 2, 2.0 * t * (1.0 - t), t * t] for t in nodes]
    return np.array(
        [
            [poly[i][a] * poly[j][b] for a in range(3) for b in range(3)]
            for i in range(3)
            for j in range(3)
        ],
        np.float32,
    )


def bernstein_lanes():
    table = np.zeros((16, TB), np.float32)
    table[:QP, :QP] = bernstein_table()
    return table


def column_device(column, place):
    return column // 2, 8 * (column % 2) + place


def differs(b, g, mb, mg):
    return jnp.logical_or(b != mb, g != mg)


def remote(src, dst, send_sem, recv_sem, b, g):
    return pltpu.make_async_remote_copy(
        src_ref=src,
        dst_ref=dst,
        send_sem=send_sem,
        recv_sem=recv_sem,
        device_id=(b, g),
        device_id_type=MESH,
    )


def others(b, g):
    return [(b, (g + n) % GRID) for n in range(1, GRID)] + [((b + n) % BLK, g) for n in range(1, BLK)]


def when(condition):
    return pl.when(condition)


def split(value):
    high = value.astype(jnp.bfloat16)
    return high, (value - high.astype(jnp.float32)).astype(jnp.bfloat16)


def build_phi(fields, start, weigh, spread, high_ref, low_ref):
    lane = lax.broadcasted_iota(jnp.int32, (QP, TB), 1)
    cell_y = lane % EY
    cell_x = lane // EY
    target = fields[FC : FC + QP, :].astype(jnp.int32) - start
    target = jnp.where(target < 0, target + M, target)
    place = 3 * (target // EY - cell_x) + (target % EY - cell_y + EY) % EY
    weight = fields[FW : FW + QP, :]
    slots = [jnp.zeros((QP, TB), jnp.float32) for _ in range(QP)]
    for a in range(QP):
        value = fields[FV + QP * a : FV + QP * (a + 1), :]
        if weigh:
            value = value * weight
        here_a = jnp.broadcast_to(place[a : a + 1, :], (QP, TB))
        for n in range(QP):
            slots[n] = jnp.where(here_a == n, value, slots[n])
    for jx in range(6):
        for t in range(3):
            row = jnp.zeros((QP, TB), jnp.float32)
            for step in range(3):
                if 0 <= jx - step <= 3:
                    row = jnp.where(cell_x == jx - step, slots[3 * step + t], row)
            spread[3 * jx + t, 0:QP, :] = row
    rows = EY
    wide_y = lax.broadcasted_iota(jnp.int32, (rows, TB), 1) % EY
    down_y = lax.broadcasted_iota(jnp.int32, (rows, TB), 0)
    hits = [(wide_y + t) % EY == down_y for t in range(3)]
    for jx in range(6):
        for k in range(QP):
            value = jnp.zeros((rows, TB), jnp.float32)
            for t in range(3):
                line = jnp.broadcast_to(spread[3 * jx + t, k : k + 1, :], (rows, TB))
                value = jnp.where(hits[t], line, value)
            high, low = split(value)
            high_ref[rows * jx : rows * (jx + 1), TB * k : TB * (k + 1)] = high
            low_ref[rows * jx : rows * (jx + 1), TB * k : TB * (k + 1)] = low


def nt(a, b):
    return lax.dot_general(a, b, (((1,), (1,)), ((), ())), preferred_element_type=jnp.float32)


def nn(a, b):
    return lax.dot_general(a, b, (((1,), (0,)), ((), ())), preferred_element_type=jnp.float32)


STEP = 16


def both(value):
    return jnp.concatenate([value, value], axis=1)


def eliminate(work, midway):
    at = lax.broadcasted_iota(jnp.int32, (8, WIN), 0)
    for top in range(0, TB, STEP):
        if top == TB // 2:
            midway()
        rows = [jnp.broadcast_to(work[top + i : top + i + 1, :], (8, WIN)) for i in range(STEP)]
        entry = {
            (i, j): jnp.broadcast_to(rows[i][:, top + j : top + j + 1], (8, TB))
            for i in range(STEP)
            for j in range(i + 1)
        }
        for j in range(STEP):
            scale = lax.rsqrt(entry[j, j])
            for i in range(j + 1, STEP):
                entry[i, j] = entry[i, j] * scale
            for i in range(j + 1, STEP):
                for k in range(j + 1, i + 1):
                    entry[i, k] = entry[i, k] - entry[i, j] * entry[k, j]
            rows[j] = rows[j] * both(scale)
            for i in range(j + 1, STEP):
                rows[i] = rows[i] - both(entry[i, j]) * rows[j]
        groups = []
        for g in range(0, STEP, 8):
            group = rows[g]
            for i in range(1, 8):
                group = jnp.where(at == i, rows[g + i], group)
            groups.append(group)
        panel = jnp.concatenate(groups, axis=0)
        work[top : top + STEP, :] = panel
        after = top + STEP
        if after < TB:
            high, low = split(panel)
            left = jnp.concatenate([high, high, low], axis=0)
            right = jnp.concatenate([high, low, high], axis=0)
            for lo, up in ((after, after + STEP), (after + STEP, TB)):
                if lo < up:
                    work[lo:up, :] -= lax.dot_general(
                        left[:, lo:up],
                        right,
                        (((0,), (0,)), ((), ())),
                        preferred_element_type=jnp.float32,
                    )


def nt3(a, b):
    (a_hi, a_lo), (b_hi, b_lo) = split(a), split(b)
    return nt(a_hi, b_hi) + (nt(a_lo, b_hi) + nt(a_hi, b_lo))


HALF_X = float(EX) / 4.0
HALF_Y = float(EY) / 4.0


def make_record(bern, conn, extract, points, raw):
    raw[...] = jnp.zeros_like(raw)
    for c in range(3):
        raw[QP * c : QP * (c + 1), 0:16] = points[:, c, :]
    for a in range(QP):
        value = jnp.zeros((QP, 16), jnp.float32)
        for n in range(QP):
            value = value + bern[0:QP, n : n + 1] * extract[a, n : n + 1, :]
        raw[FV + QP * a : FV + QP * (a + 1), 0:16] = value
    raw[FC : FC + QP, 0:16] = conn[...].astype(jnp.float32).T
    return raw[...].T[0:16, :]


def set_up_block(slot, block, shift, rec, fields, spread, phi_hi, phi_lo, trial_x, trial_y):
    cell_y = lax.broadcasted_iota(jnp.int32, (QP, TB), 1) % EY
    first = lax.broadcasted_iota(jnp.int32, (16, TB), 0) == 0
    view = fields.at[slot]
    view[...] = rec[slot].T
    build_phi(view, block * TB, True, spread, phi_hi.at[slot], phi_lo.at[slot])
    for ref in (phi_hi, phi_lo):
        ref[slot, AUG:WIN, :] = jnp.zeros((WIN - AUG, PTS), jnp.bfloat16)
    for k in range(QP):
        weight = jnp.broadcast_to(view[FW + k : FW + k + 1, :], (16, TB))
        high, low = split(jnp.where(first, weight, 0.0))
        phi_hi[slot, AUG : AUG + 16, TB * k : TB * (k + 1)] = high
        phi_lo[slot, AUG : AUG + 16, TB * k : TB * (k + 1)] = low
    trial_x[slot, 0:QP, :] = view[FX : FX + QP, :] * (EX / 2.0) + shift
    for quarter in range(4):
        turn = jnp.where(cell_y > 8 * quarter + 8, -HALF_Y, HALF_Y)
        trial_y[slot, quarter, 0:QP, :] = view[FY : FY + QP, :] * (EX / 2.0) + turn


def kernel_chunk(i, j, q_slot, trial_x, trial_y, splat, kern):
    qx = jnp.broadcast_to(trial_x[q_slot, j : j + 1, :], (8, TB))
    qy = [jnp.broadcast_to(trial_y[q_slot, quarter, j : j + 1, :], (8, TB)) for quarter in range(4)]
    sums = jnp.zeros((8, TB), jnp.float32)
    for h in range(8):
        values = []
        for n in (2 * h, 2 * h + 1):
            rows = slice(8 * n, 8 * n + 8)
            gap_x = HALF_X - jnp.abs(qx - splat[0, rows, :])
            gap_y = HALF_Y - jnp.abs(splat[1, rows, :] - qy[n % 4])
            root = lax.rsqrt(1.0 + (gap_x * gap_x + gap_y * gap_y))
            square = root * root
            value = square * square * lax.rsqrt(root)
            sums = sums + value * splat[2, rows, :]
            values.append(value)
        kern[TB * i + 16 * h : TB * i + 16 * h + 16, TB * j : TB * (j + 1)] = jnp.concatenate(
            values, axis=0
        ).astype(jnp.bfloat16)
    return jnp.sum(sums, axis=0, keepdims=True)


def below(value):
    return jnp.concatenate([value, jnp.zeros((TB - 64, TB), jnp.float32)], axis=0)


def stiffness_kernel(
    bern_in, conn_in, extract_in, points_in, out_ref,
    bern, conn, extract, points, raw, rec, fields, spread, phi_hi, phi_lo, trial_x, trial_y, splat, kern, pot,
    col_sum, totals, parts, xs, own_x, stage_big, stage_small, land_big, land_small, tiles, head, row_tile, col_tile, work,
    in_sem, rec_send, rec_recv, total_send, total_recv, piece_send, big_recv, small_recv,
    head_send, head_recv, row_send, row_recv, col_send, col_recv, ready,
):
    mb, mg = lax.axis_index("blk"), lax.axis_index("grid")
    own = 2 * mb + mg // 8
    place = mg % 8
    core = mg % 2
    chip = mg // 2
    last = place == 7
    partner = mg + 1 - 2 * core
    barrier = pltpu.get_barrier_semaphore()

    fetch = [
        pltpu.make_async_copy(src, dst, in_sem.at[n])
        for n, (src, dst) in enumerate(
            ((bern_in, bern), (extract_in, extract), (points_in, points), (conn_in, conn))
        )
    ]
    for copy in fetch:
        copy.start()
    row_tile[...] = jnp.zeros_like(row_tile)
    col_tile[...] = jnp.zeros_like(col_tile)
    for b, g in others(mb, mg):
        pl.semaphore_signal(barrier, inc=1, device_id=(b, g), device_id_type=MESH)
    for copy in fetch:
        copy.wait()
    mine = pl.ds(pl.multiple_of(16 * place, 16), 16)
    rec[0, mine, :] = make_record(bern, conn, extract, points, raw)
    pl.semaphore_wait(barrier, GRID - 1 + BLK - 1)
    for n in range(1, BLK):
        pl.semaphore_signal(ready, inc=1, device_id=((mb + n) % BLK, mg), device_id_type=MESH)

    base = 8 * (mg // 8)
    z = place // 2

    def record_copy(from_z, from_core, n, g):
        at = 2 * from_z + from_core
        view = rec.at[0, pl.ds(16 * at, 16), :]
        return remote(view, view, rec_send.at[n], rec_recv.at[at], mb, g)

    record_copy(z, core, 0, partner).start()
    for n in range(1, 4):
        record_copy(z, core, n, base + 2 * ((z + n) % 4) + core).start()
    for n in range(1, 4):
        from_z = (z + 4 - n) % 4
        record_copy(from_z, core, 0, mg).wait_recv()
        record_copy(from_z, core, 3 + n, partner).start()
    for n in range(4):
        record_copy((z + 4 - n) % 4, 1 - core, 0, mg).wait_recv()
    pl.semaphore_wait(ready, BLK - 1)
    to_b, to_g = column_device((own + 15 - place) % 16, place)
    block_copy = remote(rec.at[0], rec.at[1], rec_send.at[7], rec_recv.at[8], to_b, to_g)
    block_copy.start()

    other = (own + 1 + place) % 16
    lower = own < 8

    def test_points(i):
        for n, field in ((0, FX), (1, FY), (2, FW)):
            picked = rec[0, :, field + i : field + i + 1] * (EX / 2.0 if n < 2 else KERNEL_GAIN)
            splat[n] = jnp.broadcast_to(picked, (TB, TB))

    def evaluate(i, columns, q_slot):
        for j in columns:
            col_sum[j : j + 1, :] += kernel_chunk(i, j, q_slot, trial_x, trial_y, splat, kern)

    def multiply(rows, points, q_slot):
        pot[rows, :] = nt(kern[rows, points], phi_hi[q_slot, :, points]) + nt(
            kern[rows, points], phi_lo[q_slot, :, points]
        )

    def row_sums():
        return [pot[TB * i : TB * (i + 1), TB:WIN].T[AUG - TB : AUG - TB + 1, :] * KERNEL_GAIN for i in range(QP)]

    def window():
        high, low = split(pot[...])
        inside = jnp.logical_and(
            lax.broadcasted_iota(jnp.int32, (WIN, WIN), 0) < AUG,
            lax.broadcasted_iota(jnp.int32, (WIN, WIN), 1) < AUG,
        )
        value = nn(phi_hi[0], high) + nn(phi_lo[0], high) + nn(phi_hi[0], low)
        return jnp.where(inside, -KERNEL_GAIN * value, 0.0)

    every = slice(0, PTS)
    split_at = 5 * TB

    def run_diagonal():
        middle = 4 * TB
        col_sum[...] = jnp.zeros_like(col_sum)
        for i in range(QP):
            test_points(i)
            at = slice(TB * i, TB * (i + 1))
            start = 0 if i < 4 else middle
            if TB * i > start:
                kern[at, start : TB * i] = jnp.zeros((TB, TB * i - start), jnp.bfloat16)
            col_sum[i : i + 1, :] += 0.5 * kernel_chunk(i, i, 0, trial_x, trial_y, splat, kern)
            kern[at, at] = kern[at, at] * 0.5
            evaluate(i, range(i + 1, QP), 0)
        multiply(slice(0, middle), every, 0)
        multiply(slice(middle, PTS), slice(middle, PTS), 0)
        for i, value in enumerate(row_sums()):
            parts[7, i : i + 1, :] = col_sum[i : i + 1, :] + value
        own_x[...] = window()

    def run_pair():
        low_last = jnp.logical_and(last, lower)
        high_last = jnp.logical_and(last, jnp.logical_not(lower))
        col_sum[...] = jnp.zeros_like(col_sum)
        for i in range(QP):
            test_points(i)
            whole = jnp.logical_not(last)
            if TB * i < split_at:
                whole = jnp.logical_or(whole, lower)

            @when(whole)
            def _(i=i):
                evaluate(i, range(QP), 1)

            @when(high_last)
            def _(i=i):
                evaluate(i, range(5, QP), 1)

        @when(jnp.logical_not(last))
        def _():
            multiply(every, every, 1)

        @when(low_last)
        def _():
            multiply(slice(0, split_at), every, 1)
            pot[split_at:PTS, :] = jnp.zeros((PTS - split_at, WIN), jnp.float32)

        @when(high_last)
        def _():
            multiply(every, slice(split_at, PTS), 1)

        totals[1, 0:QP, :] = col_sum[0:QP, :]
        total_copy(1).start()
        for i, value in enumerate(row_sums()):
            totals[0, i : i + 1, :] = value

        @when(jnp.logical_not(last))
        def _():
            total_copy(0).start()

        @when(last)
        def _():
            parts[7, 0:QP, :] += totals[0, 0:QP, :]

        xs[...] = window()
        pair_pieces()

    def total_copy(n):
        b, g = column_device(other if n == 1 else own, 7)
        slot = 8 + place if n == 1 else place
        return remote(totals.at[n], parts.at[slot], total_send.at[n], total_recv.at[slot], b, g)

    def target(n):
        if n < 4:
            u, v = (0, 1, 0, 1)[n], (0, 0, 1, 1)[n]
            row, col = (own + u) % 16, (other + v) % 16
            slot = {0: 0, 1: jnp.where(row < col, 1, 2), 2: jnp.where(row < col, 2, 1), 3: 3}[n]
            half = jnp.where(jnp.logical_and(last, own >= 8), 1, 0)
        else:
            after = (own + 1) % 16
            row, col = (own, after, after)[n - 4], (own, own, after)[n - 4]
            slot = {4: 0, 5: jnp.where(own == 15, 1, 2), 6: 3}[n]
            half = 0
        big, small = jnp.maximum(row, col), jnp.minimum(row, col)
        return small % BLK, big, small // BLK, slot, half, row < col

    STAGE = {0: 0, 4: 1, 1: 0, 2: 1, 3: 2, 5: 3, 6: 4}

    def piece_copy(n):
        b, g, t, slot, half, flip = target(n)
        if n in (0, 4):
            return stage_big.at[STAGE[n]], land_big.at[t, half], big_recv.at[t, half], b, g
        return stage_small.at[STAGE[n]], land_small.at[t, slot - 1, half], small_recv.at[t, slot - 1, half], b, g

    def send_piece(n):
        src, dst, sem, b, g = piece_copy(n)

        @when(differs(b, g, mb, mg))
        def _():
            remote(src, dst, piece_send.at[n], sem, b, g).start()

        @when(jnp.logical_not(differs(b, g, mb, mg)))
        def _():
            pltpu.make_async_copy(src, dst, piece_send.at[n]).start()

    def drain_piece(n):
        src, dst, sem, b, g = piece_copy(n)

        @when(differs(b, g, mb, mg))
        def _():
            remote(src, dst, piece_send.at[n], sem, b, g).wait_send()

    def settle_piece(n):
        src, dst, sem, b, g = piece_copy(n)

        @when(jnp.logical_not(differs(b, g, mb, mg)))
        def _():
            pltpu.make_async_copy(src, dst, piece_send.at[n]).wait()

    def pair_pieces():
        corner, side = slice(0, TB), slice(TB, TB + 64)
        flip0 = target(0)[5]
        flip3 = target(3)[5]

        @when(flip0)
        def _():
            stage_big[0] = xs[corner, corner].T

        @when(jnp.logical_not(flip0))
        def _():
            stage_big[0] = xs[corner, corner]

        send_piece(0)
        stage_small[0] = xs[side, corner]
        send_piece(1)
        stage_small[1] = xs[corner, TB:WIN].T[0:64, :]
        send_piece(2)

        @when(flip3)
        def _():
            stage_small[2] = xs[TB:WIN, TB:WIN].T[0:64, :]

        @when(jnp.logical_not(flip3))
        def _():
            stage_small[2] = xs[side, TB:WIN]

        send_piece(3)

    set_up_block(0, own, -HALF_X, rec, fields, spread, phi_hi, phi_lo, trial_x, trial_y)
    @when(last)
    def _():
        run_diagonal()

    block_copy.wait_recv()
    wrapped = jnp.where(other < own, HALF_X, -HALF_X)
    set_up_block(1, other, wrapped, rec, fields, spread, phi_hi, phi_lo, trial_x, trial_y)

    run_pair()

    @when(last)
    def _():
        build_phi(fields.at[0], own * TB, False, spread, phi_hi.at[1], phi_lo.at[1])
        for ref in (phi_hi, phi_lo):
            ref[1, AUG:WIN, :] = jnp.zeros((WIN - AUG, PTS), jnp.bfloat16)
        for n in range(16):
            if n != 7:
                remote(totals.at[0], parts.at[n], total_send.at[0], total_recv.at[n], mb, mg).wait_recv()
        gain = parts[0]
        for n in range(1, 16):
            gain = gain + parts[n]
        mass = own_x[...] + own_x[...].T
        for k in range(QP):
            lanes = slice(TB * k, TB * (k + 1))
            left = phi_hi[1, :, lanes].astype(jnp.float32) + phi_lo[1, :, lanes].astype(jnp.float32)
            factor = fields[0, FW + k : FW + k + 1, :] * (MASS_SHIFT + gain[k : k + 1, :])
            high, low = split(left * factor)
            mass += nt(high, phi_hi[1, :, lanes]) + nt(low, phi_hi[1, :, lanes]) + nt(high, phi_lo[1, :, lanes])
        stage_big[1] = mass[0:TB, 0:TB]
        send_piece(4)
        stage_small[3] = mass[TB : TB + 64, 0:TB]
        send_piece(5)
        stage_small[4] = mass[TB : TB + 64, TB:WIN]
        send_piece(6)

    for n in range(4):
        settle_piece(n)

    @when(last)
    def _():
        for n in range(4, 7):
            settle_piece(n)

    for t in range(2):
        tile_col = mb + BLK * t
        owned = mg >= tile_col
        square = mg == tile_col
        tiles[t] = jnp.zeros((TB, TB), jnp.float32)
        for slot in range(4):
            first, second = (mg - slot // 2 + 16) % 16, (tile_col - slot % 2 + 16) % 16
            ahead = (first - second + 16) % 16
            skip = jnp.logical_and(square, slot == 1)
            for half in range(2):
                host = jnp.where(ahead < 8, second, first)
                step = jnp.where(ahead == 0, 7, jnp.where(ahead < 8, ahead - 1, 15 - ahead))
                if half == 0:
                    host = jnp.where(ahead == 8, jnp.minimum(first, second), host)
                    there = jnp.logical_and(owned, jnp.logical_not(skip))
                else:
                    host = jnp.maximum(first, second)
                    there = jnp.logical_and(owned, ahead == 8)
                from_b, from_g = column_device(host, step)
                if slot == 0:
                    src, dst, sem = stage_big.at[0], land_big.at[t, half], big_recv.at[t, half]
                else:
                    src = stage_small.at[0]
                    dst, sem = land_small.at[t, slot - 1, half], small_recv.at[t, slot - 1, half]

                @when(there)
                def _(src=src, dst=dst, sem=sem, t=t, slot=slot, square=square, from_b=from_b, from_g=from_g):
                    @when(differs(from_b, from_g, mb, mg))
                    def _():
                        remote(src, dst, piece_send.at[0], sem, mb, mg).wait_recv()

                    if slot == 0:
                        tiles[t] += dst[...]
                    elif slot == 1:
                        tiles[t] += below(dst[...]).T
                    elif slot == 3:
                        tiles[t, 0:64, :] += dst[...]
                    else:
                        tiles[t, 0:64, :] += dst[...]

                        @when(square)
                        def _():
                            tiles[t] += below(dst[...]).T

    first = mb == 0
    upper_half = core == 0
    half_rows = pl.ds(pl.multiple_of(64 * core, 64), 64)
    other_rows = pl.ds(pl.multiple_of(64 * (1 - core), 64), 64)
    active = mb <= 2 * chip + 1
    relay = jnp.logical_and(mg >= 1, mb == mg % BLK)
    special = jnp.logical_and(first, mg % BLK != 0)

    def row_copy(n, b, src=None):
        return remote(tiles.at[0] if src is None else src, row_tile, row_send.at[n], row_recv, b, mg)

    edges = [(0, 4, 1, None), (0, 1, 2, None), (0, 3, 3, None), (4, 5, 1, None), (4, 7, 2, None)]
    edges += [(1, 2, 1, 0), (3, 2, 1, 1), (5, 6, 1, 0), (7, 6, 1, 1)]

    def edge_on(parent, child, which):
        on = jnp.logical_and(mb == parent, jnp.logical_and(mg >= child, mg % BLK != child))
        return on if which is None else jnp.logical_and(on, core == which)

    def edge_copy(parent, child, n):
        return row_copy(n, child, None if parent == 0 else row_tile)

    @when(special)
    def _():
        row_copy(0, mg % BLK).start()

    def head_half(n, b, g, rows):
        return remote(head.at[rows, :], head.at[rows, :], head_send.at[n], head_recv.at[0], b, g)

    def head_swap(rows, g):
        return remote(head.at[rows, :], head.at[rows, :], head_send.at[15], head_recv.at[1], mb, g)

    root = jnp.logical_and(first, mg == 0)
    root_pair = jnp.logical_and(first, chip == 0)
    whole_head = remote(head, head, head_send.at[16], head_recv.at[2], mb, partner)

    @when(root)
    def _():
        head[...] = tiles[0]
        whole_head.start()

    @when(jnp.logical_and(root_pair, mg == 1))
    def _():
        whole_head.wait_recv()

    @when(root_pair)
    def _():
        for n in range(1, 8):
            head_half(n, 0, 2 * n + core, half_rows).start()

    for parent, child, n, which in edges[:3]:
        @when(edge_on(parent, child, which))
        def _(parent=parent, child=child, n=n):
            edge_copy(parent, child, n).start()

    @when(jnp.logical_and(first, mg == 8))
    def _():
        row_tile[...] = tiles[0]

    def relay_copy(n):
        return remote(row_tile, col_tile.at[mg // BLK], col_send.at[n], col_recv.at[mg // BLK], mb, 2 * n + core)

    relay_partner = remote(
        row_tile, col_tile.at[mg // BLK], col_send.at[8], col_recv.at[mg // BLK], mb, partner
    )
    with_partner = jnp.logical_and(relay, core == 0)

    early = relay
    for parent, child, n, which in edges[3:]:
        early = jnp.logical_or(early, edge_on(parent, child, which))
    early = jnp.logical_and(early, jnp.logical_not(first))

    @when(early)
    def _():
        row_copy(0, mb).wait_recv()

    for parent, child, n, which in edges[3:]:
        @when(edge_on(parent, child, which))
        def _(parent=parent, child=child, n=n):
            edge_copy(parent, child, n).start()

    for n in range(1, 8):
        @when(jnp.logical_and(relay, chip < n))
        def _(n=n):
            relay_copy(n).start()

    @when(with_partner)
    def _():
        relay_partner.start()

    @when(jnp.logical_and(active, jnp.logical_not(root_pair)))
    def _():
        head_half(0, mb, mg, half_rows).wait_recv()

    for n in range(1, 8):
        @when(jnp.logical_and(first, n <= 2 * chip + 1))
        def _(n=n):
            head_half(7 + n, n, mg, half_rows).start()

    swaps = jnp.logical_and(active, jnp.logical_not(root_pair))

    @when(swaps)
    def _():
        head_swap(half_rows, partner).start()

    @when(swaps)
    def _():
        head_swap(other_rows, partner).wait_recv()

    def forward(t):
        return remote(col_tile.at[t], col_tile.at[t], col_send.at[9 + t], col_recv.at[t], mb, partner)

    def columns_in():
        for t in range(2):
            tile_col = mb + BLK * t
            wants = jnp.logical_and(tile_col >= 1, mg > tile_col)

            @when(wants)
            def _(t=t, tile_col=tile_col):
                forward(t).wait_recv()

                @when(core == tile_col % 2)
                def _():
                    forward(t).start()

    needs_row = jnp.logical_and(jnp.logical_not(first), jnp.logical_and(mb <= mg, jnp.logical_not(early)))

    row = lax.broadcasted_iota(jnp.int32, (TB, TB), 0)
    col = lax.broadcasted_iota(jnp.int32, (TB, TB), 1)
    busy = mg >= mb

    @when(busy)
    def _():
        work[:, 0:TB] = 0.5 * (head[...] + head[...].T)
        work[:, TB:WIN] = jnp.where(row == col, 1.0, 0.0)
        eliminate(work, columns_in)

        @when(needs_row)
        def _():
            row_copy(0, mb).wait_recv()

        lower = jnp.where(row >= col, work[:, 0:TB].T, 0.0)
        inverse = jnp.where(row >= col, work[:, TB:WIN], 0.0)
        row_value = jnp.where(first, tiles[0], row_tile[...])
        columns = [jnp.where(mg == mb + BLK * t, row_value, col_tile[t]) for t in range(2)]
        solved = nt3(jnp.concatenate([row_value] + columns, axis=0), inverse)
        left = jnp.where(mg == 0, lower, solved[0:TB])
        update = nt3(left, solved[TB : 3 * TB])
        for t in range(2):
            tile_col = mb + BLK * t
            value = jnp.where(tile_col == 0, left, tiles[t] - update[:, TB * t : TB * (t + 1)])
            keep = mg * TB + row >= tile_col * TB + col
            out_ref[0, :, t, :] = jnp.where(keep, value, 0.0)

    @when(jnp.logical_not(busy))
    def _():
        out_ref[...] = jnp.zeros_like(out_ref)

    record_copy(z, core, 0, partner).wait_send()
    for n in range(1, 4):
        record_copy(z, core, n, partner).wait_send()
        record_copy(z, core, 3 + n, partner).wait_send()
    block_copy.wait_send()
    total_copy(1).wait_send()

    @when(jnp.logical_not(last))
    def _():
        total_copy(0).wait_send()

    for n in range(4):
        drain_piece(n)

    @when(last)
    def _():
        for n in range(4, 7):
            drain_piece(n)

    @when(special)
    def _():
        row_copy(0, mg % BLK).wait_send()

    @when(root)
    def _():
        whole_head.wait_send()

    @when(root_pair)
    def _():
        for n in range(1, 8):
            head_half(n, 0, mg, half_rows).wait_send()

    @when(swaps)
    def _():
        head_swap(half_rows, partner).wait_send()

    for n in range(1, 8):
        @when(jnp.logical_and(relay, chip < n))
        def _(n=n):
            relay_copy(n).wait_send()

        @when(jnp.logical_and(first, n <= 2 * chip + 1))
        def _(n=n):
            head_half(7 + n, n, mg, half_rows).wait_send()


    for parent, child, n, which in edges:
        @when(edge_on(parent, child, which))
        def _(parent=parent, child=child, n=n):
            edge_copy(parent, child, n).wait_send()

    @when(with_partner)
    def _():
        relay_partner.wait_send()

    for t in range(2):
        tile_col = mb + BLK * t
        wants = jnp.logical_and(tile_col >= 1, mg > tile_col)

        @when(jnp.logical_and(wants, core == tile_col % 2))
        def _(t=t):
            forward(t).wait_send()


def shards(conn, extract, points):
    f32, bf16 = jnp.float32, jnp.bfloat16
    vmem = lambda dtype, *shape: pltpu.VMEM(shape, dtype)
    dma = pltpu.SemaphoreType.DMA
    anywhere = pl.BlockSpec(memory_space=pltpu.HBM)
    return pl.pallas_call(
        stiffness_kernel,
        out_shape=jax.ShapeDtypeStruct((1, TB, 2, TB), f32),
        in_specs=[anywhere] * 4,
        out_specs=pl.BlockSpec(memory_space=pltpu.VMEM),
        scratch_shapes=[
            vmem(f32, 16, TB),
            vmem(jnp.int32, 16, QP),
            vmem(f32, QP, QP, 16),
            vmem(f32, QP, 3, 16),
            vmem(f32, TB, TB),
            vmem(f32, 2, TB, TB),
            vmem(f32, 2, TB, TB),
            vmem(f32, 18, 16, TB),
            vmem(bf16, 2, WIN, PTS),
            vmem(bf16, 2, WIN, PTS),
            vmem(f32, 2, 16, TB),
            vmem(f32, 2, 4, 16, TB),
            vmem(f32, 3, TB, TB),
            vmem(bf16, PTS, PTS),
            vmem(f32, PTS, WIN),
            vmem(f32, 16, TB),
            vmem(f32, 2, 16, TB),
            vmem(f32, 16, 16, TB),
            vmem(f32, WIN, WIN),
            vmem(f32, WIN, WIN),
            vmem(f32, 2, TB, TB),
            vmem(f32, 5, 64, TB),
            vmem(f32, 2, 2, TB, TB),
            vmem(f32, 2, 3, 2, 64, TB),
            vmem(f32, 2, TB, TB),
            vmem(f32, TB, TB),
            vmem(f32, TB, TB),
            vmem(f32, 2, TB, TB),
            vmem(f32, TB, WIN),
            dma((4,)),
            dma((8,)),
            dma((9,)),
            dma((2,)),
            dma((16,)),
            dma((7,)),
            dma((2, 2)),
            dma((2, 3, 2)),
            dma((17,)),
            dma((3,)),
            dma((8,)),
            dma,
            dma((11,)),
            dma((2,)),
            pltpu.SemaphoreType.REGULAR,
        ],
        compiler_params=pltpu.CompilerParams(
            collective_id=0, has_side_effects=True, vmem_limit_bytes=VMEM_LIMIT
        ),
        name="stiffness",
    )(jnp.asarray(bernstein_lanes()), conn, extract, points.transpose(1, 0, 2))


def solution(mesh):
    in_specs = (
        P(("blk", "grid"), None),
        P(None, None, ("blk", "grid")),
        P(None, None, ("blk", "grid")),
    )
    out_specs = P(None, "grid", None, "blk")
    return jax.shard_map(shards, mesh=mesh, in_specs=in_specs, out_specs=out_specs, check_vma=False)
```

```python
import functools
import math

import jax
import jax.numpy as jnp
import numpy as np
from jax import lax
from jax.experimental import pallas as pl
from jax.experimental.pallas import tpu as pltpu
from jax.sharding import PartitionSpec as P

M = 2048
EX = 64
EY = 32
QP = 9
TB = 128
BLK = 8
GRID = 16
PTS = QP * TB
WIN = 256
AUG = 192

KERNEL_GAIN = 0.02
MASS_SHIFT = 0.05

FX, FY, FW, FV, FC = 0, 9, 18, 27, 108

MESH = pl.DeviceIdType.MESH
VMEM_LIMIT = 60 * 1024 * 1024
EXACT = lax.Precision.HIGHEST


def bernstein_table():
    spread_root = 0.5 * math.sqrt(0.6)
    nodes = [0.5 - spread_root, 0.5, 0.5 + spread_root]
    poly = [[(1.0 - t) ** 2, 2.0 * t * (1.0 - t), t * t] for t in nodes]
    return np.array(
        [
            [poly[i][a] * poly[j][b] for a in range(3) for b in range(3)]
            for i in range(3)
            for j in range(3)
        ],
        np.float32,
    )


def bernstein_lanes():
    table = np.zeros((16, TB), np.float32)
    table[:QP, :QP] = bernstein_table()
    return table


def column_device(column, place):
    return column // 2, 8 * (column % 2) + place


def differs(b, g, mb, mg):
    return jnp.logical_or(b != mb, g != mg)


def remote(src, dst, send_sem, recv_sem, b, g):
    return pltpu.make_async_remote_copy(
        src_ref=src,
        dst_ref=dst,
        send_sem=send_sem,
        recv_sem=recv_sem,
        device_id=(b, g),
        device_id_type=MESH,
    )


def others(b, g):
    return [(b, (g + n) % GRID) for n in range(1, GRID)] + [((b + n) % BLK, g) for n in range(1, BLK)]


def when(condition):
    return pl.when(condition)


def split(value):
    high = value.astype(jnp.bfloat16)
    return high, (value - high.astype(jnp.float32)).astype(jnp.bfloat16)


def build_phi(fields, start, weigh, spread, high_ref, low_ref):
    lane = lax.broadcasted_iota(jnp.int32, (QP, TB), 1)
    cell_y = lane % EY
    cell_x = lane // EY
    target = fields[FC : FC + QP, :].astype(jnp.int32) - start
    target = jnp.where(target < 0, target + M, target)
    place = 3 * (target // EY - cell_x) + (target % EY - cell_y + EY) % EY
    weight = fields[FW : FW + QP, :]
    slots = [jnp.zeros((QP, TB), jnp.float32) for _ in range(QP)]
    for a in range(QP):
        value = fields[FV + QP * a : FV + QP * (a + 1), :]
        if weigh:
            value = value * weight
        here_a = jnp.broadcast_to(place[a : a + 1, :], (QP, TB))
        for n in range(QP):
            slots[n] = jnp.where(here_a == n, value, slots[n])
    for jx in range(6):
        for t in range(3):
            row = jnp.zeros((QP, TB), jnp.float32)
            for step in range(3):
                if 0 <= jx - step <= 3:
                    row = jnp.where(cell_x == jx - step, slots[3 * step + t], row)
            spread[3 * jx + t, 0:QP, :] = row
    rows = EY
    wide_y = lax.broadcasted_iota(jnp.int32, (rows, TB), 1) % EY
    down_y = lax.broadcasted_iota(jnp.int32, (rows, TB), 0)
    hits = [(wide_y + t) % EY == down_y for t in range(3)]
    for jx in range(6):
        for k in range(QP):
            value = jnp.zeros((rows, TB), jnp.float32)
            for t in range(3):
                line = jnp.broadcast_to(spread[3 * jx + t, k : k + 1, :], (rows, TB))
                value = jnp.where(hits[t], line, value)
            high, low = split(value)
            high_ref[rows * jx : rows * (jx + 1), TB * k : TB * (k + 1)] = high
            low_ref[rows * jx : rows * (jx + 1), TB * k : TB * (k + 1)] = low


def nt(a, b):
    return lax.dot_general(a, b, (((1,), (1,)), ((), ())), preferred_element_type=jnp.float32)


def nn(a, b):
    return lax.dot_general(a, b, (((1,), (0,)), ((), ())), preferred_element_type=jnp.float32)


STEP = 16


def both(value):
    return jnp.concatenate([value, value], axis=1)


def eliminate(work, midway):
    at = lax.broadcasted_iota(jnp.int32, (8, WIN), 0)
    for top in range(0, TB, STEP):
        if top == TB // 2:
            midway()
        rows = [jnp.broadcast_to(work[top + i : top + i + 1, :], (8, WIN)) for i in range(STEP)]
        entry = {
            (i, j): jnp.broadcast_to(rows[i][:, top + j : top + j + 1], (8, TB))
            for i in range(STEP)
            for j in range(i + 1)
        }
        for j in range(STEP):
            scale = lax.rsqrt(entry[j, j])
            for i in range(j + 1, STEP):
                entry[i, j] = entry[i, j] * scale
            for i in range(j + 1, STEP):
                for k in range(j + 1, i + 1):
                    entry[i, k] = entry[i, k] - entry[i, j] * entry[k, j]
            rows[j] = rows[j] * both(scale)
            for i in range(j + 1, STEP):
                rows[i] = rows[i] - both(entry[i, j]) * rows[j]
        groups = []
        for g in range(0, STEP, 8):
            group = rows[g]
            for i in range(1, 8):
                group = jnp.where(at == i, rows[g + i], group)
            groups.append(group)
        panel = jnp.concatenate(groups, axis=0)
        work[top : top + STEP, :] = panel
        after = top + STEP
        if after < TB:
            high, low = split(panel)
            left = jnp.concatenate([high, high, low], axis=0)
            right = jnp.concatenate([high, low, high], axis=0)
            for lo, up in ((after, after + STEP), (after + STEP, TB)):
                if lo < up:
                    work[lo:up, :] -= lax.dot_general(
                        left[:, lo:up],
                        right,
                        (((0,), (0,)), ((), ())),
                        preferred_element_type=jnp.float32,
                    )


def nt3(a, b):
    (a_hi, a_lo), (b_hi, b_lo) = split(a), split(b)
    return nt(a_hi, b_hi) + (nt(a_lo, b_hi) + nt(a_hi, b_lo))


HALF_X = float(EX) / 4.0
HALF_Y = float(EY) / 4.0


def make_record(bern, conn, extract, points, raw):
    raw[...] = jnp.zeros_like(raw)
    for c in range(3):
        raw[QP * c : QP * (c + 1), 0:16] = points[:, c, :]
    for a in range(QP):
        value = jnp.zeros((QP, 16), jnp.float32)
        for n in range(QP):
            value = value + bern[0:QP, n : n + 1] * extract[a, n : n + 1, :]
        raw[FV + QP * a : FV + QP * (a + 1), 0:16] = value
    raw[FC : FC + QP, 0:16] = conn[...].astype(jnp.float32).T
    return raw[...].T[0:16, :]


def set_up_block(slot, block, shift, rec, fields, spread, phi_hi, phi_lo, trial_x, trial_y):
    cell_y = lax.broadcasted_iota(jnp.int32, (QP, TB), 1) % EY
    first = lax.broadcasted_iota(jnp.int32, (16, TB), 0) == 0
    view = fields.at[slot]
    view[...] = rec[slot].T
    build_phi(view, block * TB, True, spread, phi_hi.at[slot], phi_lo.at[slot])
    for ref in (phi_hi, phi_lo):
        ref[slot, AUG:WIN, :] = jnp.zeros((WIN - AUG, PTS), jnp.bfloat16)
    for k in range(QP):
        weight = jnp.broadcast_to(view[FW + k : FW + k + 1, :], (16, TB))
        high, low = split(jnp.where(first, weight, 0.0))
        phi_hi[slot, AUG : AUG + 16, TB * k : TB * (k + 1)] = high
        phi_lo[slot, AUG : AUG + 16, TB * k : TB * (k + 1)] = low
    trial_x[slot, 0:QP, :] = view[FX : FX + QP, :] * (EX / 2.0) + shift
    for quarter in range(4):
        turn = jnp.where(cell_y > 8 * quarter + 8, -HALF_Y, HALF_Y)
        trial_y[slot, quarter, 0:QP, :] = view[FY : FY + QP, :] * (EX / 2.0) + turn


def kernel_chunk(i, j, q_slot, trial_x, trial_y, splat, kern):
    qx = jnp.broadcast_to(trial_x[q_slot, j : j + 1, :], (8, TB))
    qy = [jnp.broadcast_to(trial_y[q_slot, quarter, j : j + 1, :], (8, TB)) for quarter in range(4)]
    sums = jnp.zeros((8, TB), jnp.float32)
    for h in range(8):
        values = []
        for n in (2 * h, 2 * h + 1):
            rows = slice(8 * n, 8 * n + 8)
            gap_x = HALF_X - jnp.abs(qx - splat[0, rows, :])
            gap_y = HALF_Y - jnp.abs(splat[1, rows, :] - qy[n % 4])
            root = lax.rsqrt(1.0 + (gap_x * gap_x + gap_y * gap_y))
            square = root * root
            value = square * square * lax.rsqrt(root)
            sums = sums + value * splat[2, rows, :]
            values.append(value)
        kern[TB * i + 16 * h : TB * i + 16 * h + 16, TB * j : TB * (j + 1)] = jnp.concatenate(
            values, axis=0
        ).astype(jnp.bfloat16)
    return jnp.sum(sums, axis=0, keepdims=True)


def below(value):
    return jnp.concatenate([value, jnp.zeros((TB - 64, TB), jnp.float32)], axis=0)


def stiffness_kernel(
    bern_in, conn_in, extract_in, points_in, out_ref,
    bern, conn, extract, points, raw, rec, fields, spread, phi_hi, phi_lo, trial_x, trial_y, splat, kern, pot,
    col_sum, totals, parts, xs, own_x, stage_big, stage_small, land_big, land_small, tiles, head, row_tile, col_tile, work,
    in_sem, rec_send, rec_recv, total_send, total_recv, piece_send, big_recv, small_recv,
    head_send, head_recv, row_send, row_recv, col_send, col_recv, ready,
):
    mb, mg = lax.axis_index("blk"), lax.axis_index("grid")
    own = 2 * mb + mg // 8
    place = mg % 8
    core = mg % 2
    chip = mg // 2
    last = place == 7
    partner = mg + 1 - 2 * core
    barrier = pltpu.get_barrier_semaphore()

    fetch = [
        pltpu.make_async_copy(src, dst, in_sem.at[n])
        for n, (src, dst) in enumerate(
            ((bern_in, bern), (extract_in, extract), (points_in, points), (conn_in, conn))
        )
    ]
    for copy in fetch:
        copy.start()
    row_tile[...] = jnp.zeros_like(row_tile)
    col_tile[...] = jnp.zeros_like(col_tile)
    for b, g in others(mb, mg):
        pl.semaphore_signal(barrier, inc=1, device_id=(b, g), device_id_type=MESH)
    for copy in fetch:
        copy.wait()
    mine = pl.ds(pl.multiple_of(16 * place, 16), 16)
    rec[0, mine, :] = make_record(bern, conn, extract, points, raw)
    pl.semaphore_wait(barrier, GRID - 1 + BLK - 1)
    for n in range(1, BLK):
        pl.semaphore_signal(ready, inc=1, device_id=((mb + n) % BLK, mg), device_id_type=MESH)

    base = 8 * (mg // 8)
    z = place // 2

    def record_copy(from_z, from_core, n, g):
        at = 2 * from_z + from_core
        view = rec.at[0, pl.ds(16 * at, 16), :]
        return remote(view, view, rec_send.at[n], rec_recv.at[at], mb, g)

    record_copy(z, core, 0, partner).start()
    for n in range(1, 4):
        record_copy(z, core, n, base + 2 * ((z + n) % 4) + core).start()
    for n in range(1, 4):
        from_z = (z + 4 - n) % 4
        record_copy(from_z, core, 0, mg).wait_recv()
        record_copy(from_z, core, 3 + n, partner).start()
    for n in range(4):
        record_copy((z + 4 - n) % 4, 1 - core, 0, mg).wait_recv()
    pl.semaphore_wait(ready, BLK - 1)
    to_b, to_g = column_device((own + 15 - place) % 16, place)
    block_copy = remote(rec.at[0], rec.at[1], rec_send.at[7], rec_recv.at[8], to_b, to_g)
    block_copy.start()

    other = (own + 1 + place) % 16
    lower = own < 8

    def test_points(i):
        for n, field in ((0, FX), (1, FY), (2, FW)):
            picked = rec[0, :, field + i : field + i + 1] * (EX / 2.0 if n < 2 else KERNEL_GAIN)
            splat[n] = jnp.broadcast_to(picked, (TB, TB))

    def evaluate(i, columns, q_slot):
        for j in columns:
            col_sum[j : j + 1, :] += kernel_chunk(i, j, q_slot, trial_x, trial_y, splat, kern)

    def multiply(rows, points, q_slot):
        pot[rows, :] = nt(kern[rows, points], phi_hi[q_slot, :, points]) + nt(
            kern[rows, points], phi_lo[q_slot, :, points]
        )

    def row_sums():
        pick = (lax.broadcasted_iota(jnp.int32, (16, TB), 1) == AUG - TB).astype(jnp.bfloat16)
        high, low = split(pot[:, TB:WIN])
        sums = (nt(pick, high) + nt(pick, low)) * KERNEL_GAIN
        return [sums[0:1, TB * i : TB * (i + 1)] for i in range(QP)]

    def window():
        high, low = split(pot[...])
        inside = jnp.logical_and(
            lax.broadcasted_iota(jnp.int32, (WIN, WIN), 0) < AUG,
            lax.broadcasted_iota(jnp.int32, (WIN, WIN), 1) < AUG,
        )
        value = nn(phi_hi[0], high) + nn(phi_lo[0], high) + nn(phi_hi[0], low)
        return jnp.where(inside, -KERNEL_GAIN * value, 0.0)

    every = slice(0, PTS)
    split_at = 5 * TB

    def run_diagonal():
        middle = 4 * TB
        col_sum[...] = jnp.zeros_like(col_sum)
        for i in range(QP):
            test_points(i)
            at = slice(TB * i, TB * (i + 1))
            start = 0 if i < 4 else middle
            if TB * i > start:
                kern[at, start : TB * i] = jnp.zeros((TB, TB * i - start), jnp.bfloat16)
            col_sum[i : i + 1, :] += 0.5 * kernel_chunk(i, i, 0, trial_x, trial_y, splat, kern)
            kern[at, at] = kern[at, at] * 0.5
            evaluate(i, range(i + 1, QP), 0)
        multiply(slice(0, middle), every, 0)
        multiply(slice(middle, PTS), slice(middle, PTS), 0)
        for i, value in enumerate(row_sums()):
            parts[7, i : i + 1, :] = col_sum[i : i + 1, :] + value
        own_x[...] = window()

    def run_pair():
        low_last = jnp.logical_and(last, lower)
        high_last = jnp.logical_and(last, jnp.logical_not(lower))
        col_sum[...] = jnp.zeros_like(col_sum)
        for i in range(QP):
            test_points(i)
            whole = jnp.logical_not(last)
            if TB * i < split_at:
                whole = jnp.logical_or(whole, lower)

            @when(whole)
            def _(i=i):
                evaluate(i, range(QP), 1)

            @when(high_last)
            def _(i=i):
                evaluate(i, range(5, QP), 1)

        @when(jnp.logical_not(last))
        def _():
            multiply(every, every, 1)

        @when(low_last)
        def _():
            multiply(slice(0, split_at), every, 1)
            pot[split_at:PTS, :] = jnp.zeros((PTS - split_at, WIN), jnp.float32)

        @when(high_last)
        def _():
            multiply(every, slice(split_at, PTS), 1)

        totals[1, 0:QP, :] = col_sum[0:QP, :]
        total_copy(1).start()
        for i, value in enumerate(row_sums()):
            totals[0, i : i + 1, :] = value

        @when(jnp.logical_not(last))
        def _():
            total_copy(0).start()

        @when(last)
        def _():
            parts[7, 0:QP, :] += totals[0, 0:QP, :]

        xs[...] = window()
        pair_pieces()

    def total_copy(n):
        b, g = column_device(other if n == 1 else own, 7)
        slot = 8 + place if n == 1 else place
        return remote(totals.at[n], parts.at[slot], total_send.at[n], total_recv.at[slot], b, g)

    def target(n):
        if n < 4:
            u, v = (0, 1, 0, 1)[n], (0, 0, 1, 1)[n]
            row, col = (own + u) % 16, (other + v) % 16
            slot = {0: 0, 1: jnp.where(row < col, 1, 2), 2: jnp.where(row < col, 2, 1), 3: 3}[n]
            half = jnp.where(jnp.logical_and(last, own >= 8), 1, 0)
        else:
            after = (own + 1) % 16
            row, col = (own, after, after)[n - 4], (own, own, after)[n - 4]
            slot = {4: 0, 5: jnp.where(own == 15, 1, 2), 6: 3}[n]
            half = 0
        big, small = jnp.maximum(row, col), jnp.minimum(row, col)
        return small % BLK, big, small // BLK, slot, half, row < col

    STAGE = {0: 0, 4: 1, 1: 0, 2: 1, 3: 2, 5: 3, 6: 4}

    def piece_copy(n):
        b, g, t, slot, half, flip = target(n)
        if n in (0, 4):
            return stage_big.at[STAGE[n]], land_big.at[t, half], big_recv.at[t, half], b, g
        return stage_small.at[STAGE[n]], land_small.at[t, slot - 1, half], small_recv.at[t, slot - 1, half], b, g

    def send_piece(n):
        src, dst, sem, b, g = piece_copy(n)

        @when(differs(b, g, mb, mg))
        def _():
            remote(src, dst, piece_send.at[n], sem, b, g).start()

        @when(jnp.logical_not(differs(b, g, mb, mg)))
        def _():
            pltpu.make_async_copy(src, dst, piece_send.at[n]).start()

    def drain_piece(n):
        src, dst, sem, b, g = piece_copy(n)

        @when(differs(b, g, mb, mg))
        def _():
            remote(src, dst, piece_send.at[n], sem, b, g).wait_send()

    def settle_piece(n):
        src, dst, sem, b, g = piece_copy(n)

        @when(jnp.logical_not(differs(b, g, mb, mg)))
        def _():
            pltpu.make_async_copy(src, dst, piece_send.at[n]).wait()

    def pair_pieces():
        corner, side = slice(0, TB), slice(TB, TB + 64)
        flip0 = target(0)[5]
        flip3 = target(3)[5]

        @when(flip0)
        def _():
            stage_big[0] = xs[corner, corner].T

        @when(jnp.logical_not(flip0))
        def _():
            stage_big[0] = xs[corner, corner]

        send_piece(0)
        stage_small[0] = xs[side, corner]
        send_piece(1)
        stage_small[1] = xs[corner, TB:WIN].T[0:64, :]
        send_piece(2)

        @when(flip3)
        def _():
            stage_small[2] = xs[TB:WIN, TB:WIN].T[0:64, :]

        @when(jnp.logical_not(flip3))
        def _():
            stage_small[2] = xs[side, TB:WIN]

        send_piece(3)

    set_up_block(0, own, -HALF_X, rec, fields, spread, phi_hi, phi_lo, trial_x, trial_y)
    @when(last)
    def _():
        run_diagonal()

    block_copy.wait_recv()
    wrapped = jnp.where(other < own, HALF_X, -HALF_X)
    set_up_block(1, other, wrapped, rec, fields, spread, phi_hi, phi_lo, trial_x, trial_y)

    run_pair()

    @when(last)
    def _():
        build_phi(fields.at[0], own * TB, False, spread, phi_hi.at[1], phi_lo.at[1])
        for ref in (phi_hi, phi_lo):
            ref[1, AUG:WIN, :] = jnp.zeros((WIN - AUG, PTS), jnp.bfloat16)
        for n in range(16):
            if n != 7:
                remote(totals.at[0], parts.at[n], total_send.at[0], total_recv.at[n], mb, mg).wait_recv()
        gain = parts[0]
        for n in range(1, 16):
            gain = gain + parts[n]
        mass = own_x[...] + own_x[...].T
        for k in range(QP):
            lanes = slice(TB * k, TB * (k + 1))
            left = phi_hi[1, :, lanes].astype(jnp.float32) + phi_lo[1, :, lanes].astype(jnp.float32)
            factor = fields[0, FW + k : FW + k + 1, :] * (MASS_SHIFT + gain[k : k + 1, :])
            high, low = split(left * factor)
            mass += nt(high, phi_hi[1, :, lanes]) + nt(low, phi_hi[1, :, lanes]) + nt(high, phi_lo[1, :, lanes])
        stage_big[1] = mass[0:TB, 0:TB]
        send_piece(4)
        stage_small[3] = mass[TB : TB + 64, 0:TB]
        send_piece(5)
        stage_small[4] = mass[TB : TB + 64, TB:WIN]
        send_piece(6)

    for n in range(4):
        settle_piece(n)

    @when(last)
    def _():
        for n in range(4, 7):
            settle_piece(n)

    def sum_tile(t):
        tile_col = mb + BLK * t
        owned = mg >= tile_col
        square = mg == tile_col
        tiles[t] = jnp.zeros((TB, TB), jnp.float32)
        for slot in range(4):
            first, second = (mg - slot // 2 + 16) % 16, (tile_col - slot % 2 + 16) % 16
            ahead = (first - second + 16) % 16
            skip = jnp.logical_and(square, slot == 1)
            for half in range(2):
                host = jnp.where(ahead < 8, second, first)
                step = jnp.where(ahead == 0, 7, jnp.where(ahead < 8, ahead - 1, 15 - ahead))
                if half == 0:
                    host = jnp.where(ahead == 8, jnp.minimum(first, second), host)
                    there = jnp.logical_and(owned, jnp.logical_not(skip))
                else:
                    host = jnp.maximum(first, second)
                    there = jnp.logical_and(owned, ahead == 8)
                from_b, from_g = column_device(host, step)
                if slot == 0:
                    src, dst, sem = stage_big.at[0], land_big.at[t, half], big_recv.at[t, half]
                else:
                    src = stage_small.at[0]
                    dst, sem = land_small.at[t, slot - 1, half], small_recv.at[t, slot - 1, half]

                @when(there)
                def _(src=src, dst=dst, sem=sem, t=t, slot=slot, square=square, from_b=from_b, from_g=from_g):
                    @when(differs(from_b, from_g, mb, mg))
                    def _():
                        remote(src, dst, piece_send.at[0], sem, mb, mg).wait_recv()

                    if slot == 0:
                        tiles[t] += dst[...]
                    elif slot == 1:
                        tiles[t] += below(dst[...]).T
                    elif slot == 3:
                        tiles[t, 0:64, :] += dst[...]
                    else:
                        tiles[t, 0:64, :] += dst[...]

                        @when(square)
                        def _():
                            tiles[t] += below(dst[...]).T

    first = mb == 0

    @when(first)
    def _():
        sum_tile(0)

    half_rows = pl.ds(pl.multiple_of(64 * core, 64), 64)
    other_rows = pl.ds(pl.multiple_of(64 * (1 - core), 64), 64)
    active = mb <= 2 * chip + 1
    relay = jnp.logical_and(mg >= 1, mb == mg % BLK)
    special = jnp.logical_and(first, mg % BLK != 0)

    def row_copy(n, b, src=None):
        return remote(tiles.at[0] if src is None else src, row_tile, row_send.at[n], row_recv, b, mg)

    edges = [(0, 4, 1, None), (0, 1, 2, None), (0, 3, 3, None), (4, 5, 1, None), (4, 7, 2, None)]
    edges += [(1, 2, 1, 0), (3, 2, 1, 1), (5, 6, 1, 0), (7, 6, 1, 1)]

    def edge_on(parent, child, which):
        on = jnp.logical_and(mb == parent, jnp.logical_and(mg >= child, mg % BLK != child))
        return on if which is None else jnp.logical_and(on, core == which)

    def edge_copy(parent, child, n):
        return row_copy(n, child, None if parent == 0 else row_tile)

    @when(special)
    def _():
        row_copy(0, mg % BLK).start()

    def head_half(n, b, g, rows):
        return remote(head.at[rows, :], head.at[rows, :], head_send.at[n], head_recv.at[0], b, g)

    def head_swap(rows, g):
        return remote(head.at[rows, :], head.at[rows, :], head_send.at[15], head_recv.at[1], mb, g)

    root = jnp.logical_and(first, mg == 0)
    root_pair = jnp.logical_and(first, chip == 0)
    whole_head = remote(head, head, head_send.at[16], head_recv.at[2], mb, partner)

    @when(root)
    def _():
        head[...] = tiles[0]
        whole_head.start()

    @when(jnp.logical_and(root_pair, mg == 1))
    def _():
        whole_head.wait_recv()

    @when(root_pair)
    def _():
        for n in range(1, 8):
            head_half(n, 0, 2 * n + core, half_rows).start()

    for parent, child, n, which in edges[:3]:
        @when(edge_on(parent, child, which))
        def _(parent=parent, child=child, n=n):
            edge_copy(parent, child, n).start()

    @when(jnp.logical_and(first, mg == 8))
    def _():
        row_tile[...] = tiles[0]

    def relay_copy(n):
        return remote(row_tile, col_tile.at[mg // BLK], col_send.at[n], col_recv.at[mg // BLK], mb, 2 * n + core)

    relay_partner = remote(
        row_tile, col_tile.at[mg // BLK], col_send.at[8], col_recv.at[mg // BLK], mb, partner
    )
    helper = jnp.logical_and(partner >= 1, mb == partner % BLK)

    def helper_copy(n):
        view = col_tile.at[mg // BLK]
        return remote(view, view, col_send.at[n], col_recv.at[mg // BLK], mb, 2 * n + core)


    early = relay
    for parent, child, n, which in edges[3:]:
        early = jnp.logical_or(early, edge_on(parent, child, which))
    early = jnp.logical_and(early, jnp.logical_not(first))

    @when(early)
    def _():
        row_copy(0, mb).wait_recv()

    for parent, child, n, which in edges[3:]:
        @when(edge_on(parent, child, which))
        def _(parent=parent, child=child, n=n):
            edge_copy(parent, child, n).start()

    @when(relay)
    def _():
        relay_partner.start()

    for n in (2, 4, 6):
        @when(jnp.logical_and(relay, chip < n))
        def _(n=n):
            relay_copy(n).start()

    @when(helper)
    def _():
        helper_copy(0).wait_recv()

    for n in (1, 3, 5, 7):
        @when(jnp.logical_and(helper, chip < n))
        def _(n=n):
            helper_copy(n).start()

    @when(jnp.logical_and(active, jnp.logical_not(root_pair)))
    def _():
        head_half(0, mb, mg, half_rows).wait_recv()

    for n in range(1, 8):
        @when(jnp.logical_and(first, n <= 2 * chip + 1))
        def _(n=n):
            head_half(7 + n, n, mg, half_rows).start()

    swaps = jnp.logical_and(active, jnp.logical_not(root_pair))

    @when(swaps)
    def _():
        head_swap(half_rows, partner).start()

    @when(swaps)
    def _():
        head_swap(other_rows, partner).wait_recv()

    def forward(t):
        return remote(col_tile.at[t], col_tile.at[t], col_send.at[9 + t], col_recv.at[t], mb, partner)

    def columns_in():
        for t in range(2):
            tile_col = mb + BLK * t
            wants = jnp.logical_and(tile_col >= 1, chip > tile_col // 2)

            @when(wants)
            def _(t=t, tile_col=tile_col):
                forward(t).wait_recv()

                @when(core == (tile_col + chip) % 2)
                def _():
                    forward(t).start()

    needs_row = jnp.logical_and(jnp.logical_not(first), jnp.logical_and(mb <= mg, jnp.logical_not(early)))

    row = lax.broadcasted_iota(jnp.int32, (TB, TB), 0)
    col = lax.broadcasted_iota(jnp.int32, (TB, TB), 1)
    busy = mg >= mb

    @when(busy)
    def _():
        work[:, 0:TB] = 0.5 * (head[...] + head[...].T)
        work[:, TB:WIN] = jnp.where(row == col, 1.0, 0.0)
        eliminate(work, columns_in)

        @when(jnp.logical_not(first))
        def _():
            sum_tile(0)

        sum_tile(1)


        @when(needs_row)
        def _():
            row_copy(0, mb).wait_recv()

        lower = jnp.where(row >= col, work[:, 0:TB].T, 0.0)
        inverse = jnp.where(row >= col, work[:, TB:WIN], 0.0)
        row_value = jnp.where(first, tiles[0], row_tile[...])
        columns = [jnp.where(mg == mb + BLK * t, row_value, col_tile[t]) for t in range(2)]
        solved = nt3(jnp.concatenate([row_value] + columns, axis=0), inverse)
        left = jnp.where(mg == 0, lower, solved[0:TB])
        update = nt3(left, solved[TB : 3 * TB])
        for t in range(2):
            tile_col = mb + BLK * t
            value = jnp.where(tile_col == 0, left, tiles[t] - update[:, TB * t : TB * (t + 1)])
            keep = mg * TB + row >= tile_col * TB + col
            out_ref[0, :, t, :] = jnp.where(keep, value, 0.0)

    @when(jnp.logical_not(busy))
    def _():
        out_ref[...] = jnp.zeros_like(out_ref)

    record_copy(z, core, 0, partner).wait_send()
    for n in range(1, 4):
        record_copy(z, core, n, partner).wait_send()
        record_copy(z, core, 3 + n, partner).wait_send()
    block_copy.wait_send()
    total_copy(1).wait_send()

    @when(jnp.logical_not(last))
    def _():
        total_copy(0).wait_send()

    for n in range(4):
        drain_piece(n)

    @when(last)
    def _():
        for n in range(4, 7):
            drain_piece(n)

    @when(special)
    def _():
        row_copy(0, mg % BLK).wait_send()

    @when(root)
    def _():
        whole_head.wait_send()

    @when(root_pair)
    def _():
        for n in range(1, 8):
            head_half(n, 0, mg, half_rows).wait_send()

    @when(swaps)
    def _():
        head_swap(half_rows, partner).wait_send()

    for n in range(1, 8):
        @when(jnp.logical_and(relay if n % 2 == 0 else helper, chip < n))
        def _(n=n):
            (relay_copy(n) if n % 2 == 0 else helper_copy(n)).wait_send()

        @when(jnp.logical_and(first, n <= 2 * chip + 1))
        def _(n=n):
            head_half(7 + n, n, mg, half_rows).wait_send()


    for parent, child, n, which in edges:
        @when(edge_on(parent, child, which))
        def _(parent=parent, child=child, n=n):
            edge_copy(parent, child, n).wait_send()

    @when(relay)
    def _():
        relay_partner.wait_send()

    for t in range(2):
        tile_col = mb + BLK * t
        wants = jnp.logical_and(tile_col >= 1, chip > tile_col // 2)

        @when(jnp.logical_and(wants, core == (tile_col + chip) % 2))
        def _(t=t):
            forward(t).wait_send()


def shards(conn, extract, points):
    f32, bf16 = jnp.float32, jnp.bfloat16
    vmem = lambda dtype, *shape: pltpu.VMEM(shape, dtype)
    dma = pltpu.SemaphoreType.DMA
    anywhere = pl.BlockSpec(memory_space=pltpu.HBM)
    return pl.pallas_call(
        stiffness_kernel,
        out_shape=jax.ShapeDtypeStruct((1, TB, 2, TB), f32),
        in_specs=[anywhere] * 4,
        out_specs=pl.BlockSpec(memory_space=pltpu.VMEM),
        scratch_shapes=[
            vmem(f32, 16, TB),
            vmem(jnp.int32, 16, QP),
            vmem(f32, QP, QP, 16),
            vmem(f32, QP, 3, 16),
            vmem(f32, TB, TB),
            vmem(f32, 2, TB, TB),
            vmem(f32, 2, TB, TB),
            vmem(f32, 18, 16, TB),
            vmem(bf16, 2, WIN, PTS),
            vmem(bf16, 2, WIN, PTS),
            vmem(f32, 2, 16, TB),
            vmem(f32, 2, 4, 16, TB),
            vmem(f32, 3, TB, TB),
            vmem(bf16, PTS, PTS),
            vmem(f32, PTS, WIN),
            vmem(f32, 16, TB),
            vmem(f32, 2, 16, TB),
            vmem(f32, 16, 16, TB),
            vmem(f32, WIN, WIN),
            vmem(f32, WIN, WIN),
            vmem(f32, 2, TB, TB),
            vmem(f32, 5, 64, TB),
            vmem(f32, 2, 2, TB, TB),
            vmem(f32, 2, 3, 2, 64, TB),
            vmem(f32, 2, TB, TB),
            vmem(f32, TB, TB),
            vmem(f32, TB, TB),
            vmem(f32, 2, TB, TB),
            vmem(f32, TB, WIN),
            dma((4,)),
            dma((8,)),
            dma((9,)),
            dma((2,)),
            dma((16,)),
            dma((7,)),
            dma((2, 2)),
            dma((2, 3, 2)),
            dma((17,)),
            dma((3,)),
            dma((8,)),
            dma,
            dma((11,)),
            dma((2,)),
            pltpu.SemaphoreType.REGULAR,
        ],
        compiler_params=pltpu.CompilerParams(
            collective_id=0, has_side_effects=True, vmem_limit_bytes=VMEM_LIMIT
        ),
        name="stiffness",
    )(jnp.asarray(bernstein_lanes()), conn, extract, points.transpose(1, 0, 2))


def solution(mesh):
    in_specs = (
        P(("blk", "grid"), None),
        P(None, None, ("blk", "grid")),
        P(None, None, ("blk", "grid")),
    )
    out_specs = P(None, "grid", None, "blk")
    return jax.shard_map(shards, mesh=mesh, in_specs=in_specs, out_specs=out_specs, check_vma=False)
```
